512 devices in a mesh: gx: 16 (over x_lo, z), gy: 32 (over x_hi, y, core).
Axes of the slice: x: 4 (x_hi: 2, x_lo: 2; x = x_hi * 2 + x_lo), y: 8, z: 8, core: 2. Of those that a mesh axis runs over, the one named last changes fastest.
Arguments:
- state: float32 [8, 2, 64, 16256], P(None, None, 'gx', 'gy'), may hold values from -1 to 5, as said below
- shear_offset: int32 [1], replicated, may hold values from 0 to 16255
- remap_shift: int32 [64], P('gx'), may hold values from 0 to 16255
- frac_index: int32 [64], P('gx'), may hold values from 0 to 15
Outputs:
- new_state: float32 [8, 2, 64, 16256], P(None, None, 'gx', 'gy')
The draws below stay inside these ranges and needn't reach their ends.
Inputs may be any that keep to these rules, and one draw needn't show every extreme that they name: `state`: field 0 lies in 0.5 to 2, fields 1 to 3 and 5 to 7 within 1 in magnitude, field 4 in 1 to 5.
All inputs are finite; a program needn't handle non-finite values.
Results may differ from the reference program's by a relative error of at most 0.00002.
Values sent between devices are 32-bit elements; how exact they have to be, the bound alone decides.
A program may use at most 64 MiB of HBM per device.

```python
import jax
import jax.numpy as jnp
from jax import lax

FRAC = 16
NZ = 2
NX = 64
NY = 16256


def signed_values(key, shape, low, high):
    keys = jax.random.split(key, 2)
    magnitude = jax.random.uniform(keys[0], shape, jnp.float32, low, high)
    sign_bit = jax.random.bernoulli(keys[1], 0.5, shape)
    return jnp.where(sign_bit, magnitude, -magnitude)


def draw_state(key, part):
    keys = jax.random.split(jax.random.fold_in(key, 11), 4)
    shape = (NZ, NX, NY)
    density = jax.random.uniform(keys[0], shape, jnp.float32, 0.5, 0.6)
    momenta = signed_values(keys[1], (3,) + shape, 0.7, 1.0)
    fields = signed_values(keys[3], (3,) + shape, 0.7, 1.0)
    thermal = jax.random.uniform(keys[2], shape, jnp.float32, 0.2, 0.4)
    kinetic = 0.5 * jnp.sum(momenta * momenta, axis=0) / density
    energy = thermal + kinetic + 1.5
    return jnp.concatenate([density[None], momenta, energy[None], fields], axis=0)


def set_ends(result, stream_key, low, top_value):
    spot = [jax.random.randint(jax.random.fold_in(stream_key, axis), (), 0, length) for axis, length in enumerate(result.shape)]
    longest = result.shape.index(max(result.shape))
    next_to = spot[:longest] + [(spot[longest] + 1) % result.shape[longest]] + spot[longest + 1:]
    return result.at[tuple(spot)].set(low).at[tuple(next_to)].set(top_value)


def setup_inputs(seed: int = 0) -> dict:
    seeds = jax.random.split(jax.random.key(seed), 5)
    return {
        "state": draw_state(jax.random.fold_in(seeds[4], 71), 0),
        "shear_offset": jax.random.randint(seeds[1], (1,), 0, NY).astype(jnp.int32),
        "remap_shift": set_ends(jax.random.randint(seeds[2], (NX,), 0, NY), jax.random.fold_in(seeds[2], 1), 0, NY - 1).astype(jnp.int32),
        "frac_index": set_ends(jax.random.randint(seeds[3], (NX,), 0, FRAC), jax.random.fold_in(seeds[3], 1), 0, FRAC - 1).astype(jnp.int32),
    }


ADIABATIC = 5.0 / 3.0
ROTATION = 1.0
SHEAR_RATE = 1.5
MAX_SPEED = 5.0
TIME_STEP = 0.05


def next_cell(value, grid_axis):
    return jnp.roll(value, -1, grid_axis)


def prev_cell(value, grid_axis):
    return jnp.roll(value, 1, grid_axis)


def tendency(state):
    density, mom_x, mom_y, mom_z, energy, face_x, face_y, face_z = state
    cen_x = 0.5 * (face_x + next_cell(face_x, 1))
    cen_y = 0.5 * (face_y + next_cell(face_y, 2))
    cen_z = 0.5 * (face_z + next_cell(face_z, 0))
    vel_x = mom_x / density
    vel_y = mom_y / density
    vel_z = mom_z / density
    magnetic = 0.5 * (cen_x * cen_x + cen_y * cen_y + cen_z * cen_z)
    pressure = (ADIABATIC - 1.0) * (energy - 0.5 * (mom_x * vel_x + mom_y * vel_y + mom_z * vel_z) - magnetic) + magnetic
    vel_dot = vel_x * cen_x + vel_y * cen_y + vel_z * cen_z
    conserved = (density, mom_x, mom_y, mom_z, energy)
    momenta = (mom_x, mom_y, mom_z)
    centred = (cen_x, cen_y, cen_z)
    velocity = (vel_x, vel_y, vel_z)
    change = [jnp.zeros_like(density) for member in range(5)]
    for normal, grid_axis in ((0, 1), (1, 2), (2, 0)):
        normal_speed = velocity[normal]
        across = centred[normal]
        fluxes = [momenta[normal]]
        for second in range(3):
            flux_term = momenta[second] * normal_speed - across * centred[second]
            if second == normal:
                flux_term = flux_term + pressure
            fluxes.append(flux_term)
        fluxes.append((energy + pressure) * normal_speed - across * vel_dot)
        for member in range(5):
            upwind = 0.5 * (prev_cell(fluxes[member], grid_axis) + fluxes[member]) - 0.5 * MAX_SPEED * (conserved[member] - prev_cell(conserved[member], grid_axis))
            change[member] = change[member] - (next_cell(upwind, grid_axis) - upwind)
    change[1] = change[1] + 2.0 * ROTATION * mom_y
    change[2] = change[2] - (2.0 - SHEAR_RATE) * ROTATION * mom_x
    change[4] = change[4] + SHEAR_RATE * ROTATION * (mom_x * vel_y - cen_x * cen_y)
    elec_x = -(vel_y * cen_z - vel_z * cen_y)
    elec_y = -(vel_z * cen_x - vel_x * cen_z)
    elec_z = -(vel_x * cen_y - vel_y * cen_x)
    edge_x = 0.25 * (elec_x + prev_cell(elec_x, 2) + prev_cell(elec_x, 0) + prev_cell(prev_cell(elec_x, 2), 0))
    edge_y = 0.25 * (elec_y + prev_cell(elec_y, 1) + prev_cell(elec_y, 0) + prev_cell(prev_cell(elec_y, 1), 0))
    edge_z = 0.25 * (elec_z + prev_cell(elec_z, 1) + prev_cell(elec_z, 2) + prev_cell(prev_cell(elec_z, 1), 2))
    delta_x = -((next_cell(edge_z, 2) - edge_z) - (next_cell(edge_y, 0) - edge_y))
    delta_y = -((next_cell(edge_x, 0) - edge_x) - (next_cell(edge_z, 1) - edge_z))
    delta_z = -((next_cell(edge_y, 1) - edge_y) - (next_cell(edge_x, 2) - edge_x))
    return jnp.stack(change + [delta_x, delta_y, delta_z])


def pad_shear(state, offset, width):
    left_strip = jnp.roll(state[:, :, -width:, :], offset, axis=3)
    right_strip = jnp.roll(state[:, :, :width, :], -offset, axis=3)
    radial = jnp.concatenate([left_strip, state, right_strip], axis=2)
    return jnp.concatenate([radial[..., -width:], radial, radial[..., :width]], axis=3)


def reference(state, shear_offset, remap_shift, frac_index):
    offset = shear_offset[0]
    first = state + TIME_STEP * tendency(pad_shear(state, offset, 2))[:, :, 2:-2, 2:-2]
    advanced = 0.5 * (state + (first + TIME_STEP * tendency(pad_shear(first, offset, 2))[:, :, 2:-2, 2:-2]))
    fraction = (frac_index.astype(jnp.float32) + 0.5) / FRAC
    column = jnp.arange(NY, dtype=jnp.int32)
    source = (column[None, :] - remap_shift.astype(jnp.int32)[:, None]) % NY
    before = (source - 1) % NY

    def remap_field(field):
        here = jnp.take_along_axis(field, jnp.broadcast_to(source[None], field.shape), axis=2)
        there = jnp.take_along_axis(field, jnp.broadcast_to(before[None], field.shape), axis=2)
        return (1.0 - fraction)[None, :, None] * here + fraction[None, :, None] * there

    return lax.map(remap_field, advanced)
```

```python
import functools

import jax
import jax.numpy as jnp
from jax import lax
from jax.experimental import pallas as pl
from jax.experimental.pallas import tpu as pltpu
from jax.sharding import PartitionSpec as P

FRAC = 16
GAMMA_LESS = 5.0 / 3.0 - 1.0
ROTATION = 1.0
SHEAR_RATE = 1.5
MAX_SPEED = 5.0
TIME_STEP = 0.05

FACE_X, FACE_Y, FACE_Z, NEXT_Y = 5, 6, 7, 8
ROWS = 4
LINES = 8 * ROWS
STRIPS = 17
MESH = pl.DeviceIdType.MESH


def ahead(value, count):
    lane = lax.broadcasted_iota(jnp.int32, value.shape, 2)
    moved = pltpu.roll(value, 128 - count, 2)
    return jnp.where(lane >= 128 - count, pltpu.roll(moved, 7, 1), moved)


def behind(value, count):
    lane = lax.broadcasted_iota(jnp.int32, value.shape, 2)
    moved = pltpu.roll(value, count, 2)
    return jnp.where(lane < count, pltpu.roll(moved, 1, 1), moved)


def other_plane(value):
    return pltpu.roll(value, 4, 1)


def euler(fields, next_y):
    density, mom_x, mom_y, mom_z, energy, face_x, face_y, face_z = fields
    rows = density.shape[0]
    mid = slice(1, rows - 1)
    cen_x = 0.5 * (face_x[:-1] + face_x[1:])
    cen_y = 0.5 * (face_y + next_y)
    cen_z = 0.5 * (face_z + other_plane(face_z))
    inverse = 1.0 / density
    vel_x = mom_x * inverse
    vel_y = mom_y * inverse
    vel_z = mom_z * inverse
    magnetic = 0.5 * (cen_x * cen_x + cen_y * cen_y + cen_z * cen_z)
    pressure = (
        GAMMA_LESS * (energy - 0.5 * (mom_x * vel_x + mom_y * vel_y + mom_z * vel_z) - magnetic) + magnetic
    )
    vel_dot = vel_x * cen_x + vel_y * cen_y + vel_z * cen_z
    conserved = (density, mom_x, mom_y, mom_z, energy)
    momenta = (mom_x, mom_y, mom_z)
    centred = (cen_x, cen_y, cen_z)
    velocity = (vel_x, vel_y, vel_z)
    change = [None] * 5
    for normal in range(3):
        part = slice(None) if normal == 0 else mid
        speed = velocity[normal][part]
        across = centred[normal][part]
        fluxes = [momenta[normal][part]]
        for second in range(3):
            term = momenta[second][part] * speed - across * centred[second][part]
            if second == normal:
                term = term + pressure[part]
            fluxes.append(term)
        fluxes.append((energy[part] + pressure[part]) * speed - across * vel_dot[part])
        for member in range(5):
            flux = fluxes[member]
            held = conserved[member][part]
            if normal == 0:
                upwind = 0.5 * (flux[:-1] + flux[1:]) - 0.5 * MAX_SPEED * (held[1:] - held[:-1])
                delta = upwind[1:] - upwind[:-1]
            elif normal == 1:
                upwind = 0.5 * (behind(flux, 1) + flux) - 0.5 * MAX_SPEED * (held - behind(held, 1))
                delta = ahead(upwind, 1) - upwind
            else:
                upwind = 0.5 * (other_plane(flux) + flux) - 0.5 * MAX_SPEED * (held - other_plane(held))
                delta = other_plane(upwind) - upwind
            change[member] = -delta if change[member] is None else change[member] - delta
    change[1] = change[1] + 2.0 * ROTATION * mom_y[mid]
    change[2] = change[2] - (2.0 - SHEAR_RATE) * ROTATION * mom_x[mid]
    change[4] = change[4] + SHEAR_RATE * ROTATION * (mom_x[mid] * vel_y[mid] - cen_x[mid] * cen_y[mid])
    elec_x = -(vel_y * cen_z - vel_z * cen_y)
    elec_y = -(vel_z * cen_x - vel_x * cen_z)
    elec_z = -(vel_x * cen_y - vel_y * cen_x)
    pair_x = elec_x[mid] + behind(elec_x[mid], 1)
    edge_x = 0.25 * (pair_x + other_plane(pair_x))
    pair_y = elec_y[1:] + elec_y[:-1]
    edge_y = 0.25 * (pair_y + other_plane(pair_y))
    pair_z = elec_z[1:] + elec_z[:-1]
    edge_z = 0.25 * (pair_z + behind(pair_z, 1))
    delta_x = -(ahead(edge_z, 1) - edge_z - (other_plane(edge_y) - edge_y))
    delta_y = -(other_plane(edge_x) - edge_x - (edge_z[1:] - edge_z[:-1]))
    delta_z = -(edge_y[1:] - edge_y[:-1] - (ahead(edge_x, 1) - edge_x))
    done = [conserved[member][mid] + TIME_STEP * change[member] for member in range(5)]
    done.append(face_x[1:rows] + TIME_STEP * delta_x)
    done.append(face_y[mid] + TIME_STEP * delta_y)
    done.append(face_z[mid] + TIME_STEP * delta_z)
    return done


def window(ref, slot, blocks, cells, amount, kinds):
    hops = lax.div(amount, cells)
    rest = lax.rem(amount, cells)
    if kinds == 3:
        low = rest < 2
        hops = jnp.where(low, hops - 1, hops)
        rest = jnp.where(low, rest + cells, rest)
    total = blocks * 8
    lane = lax.broadcasted_iota(jnp.int32, (blocks, 8, 128), 2)
    chunk = lax.broadcasted_iota(jnp.int32, (blocks, 8, 128), 1) % 4
    place = chunk * 128 + lane - 2 - rest
    result = None
    for kind in reversed(range(kinds)):
        distance = rest - kind * cells + 1024
        lanes = lax.rem(distance, 128)
        sublanes = lax.div(distance, 128) - 8
        back = lax.rem(8 * (hops + kind) + sublanes + total, total)
        near = ref[slot, pl.ds(total - back, total), :].reshape(blocks, 8, 128)
        far = ref[slot, pl.ds(total - back - 1, total), :].reshape(blocks, 8, 128)
        near = pltpu.roll(near, lanes, 2)
        far = pltpu.roll(far, lanes, 2)
        moved = jnp.where(lane >= lanes, near, far)
        if result is None:
            result = moved
        else:
            result = jnp.where(place >= -kind * cells, moved, result)
    return result


def kernel(
    n_gx,
    n_gy,
    cells,
    shear_ref,
    remap_ref,
    frac_ref,
    state_ref,
    out_ref,
    raw,
    held,
    ext,
    last_face,
    to_left,
    to_right,
    from_left,
    from_right,
    edges,
    next_edges,
    strip_in,
    strip_out,
    moved,
    line_in,
    line_out,
    lines,
    send_sems,
    recv_sems,
):
    gx = lax.axis_index("gx")
    gy = lax.axis_index("gy")
    half = n_gy // 2
    slots = -(-STRIPS // n_gy)
    per = LINES // n_gy
    left_y = lax.rem(gy + n_gy - 1, n_gy)
    right_y = lax.rem(gy + 1, n_gy)
    first_x = gx == 0
    last_x = gx == n_gx - 1
    edge_x = jnp.logical_or(first_x, last_x)
    facing = jnp.where(first_x, n_gx - 1, 0)
    barrier = pltpu.get_barrier_semaphore()

    def greet(x, y):
        pl.semaphore_signal(barrier, inc=1, device_id=(x, y), device_id_type=MESH)

    def send(source, target, sem, x, y):
        return pltpu.make_async_remote_copy(
            src_ref=source,
            dst_ref=target,
            send_sem=send_sems.at[sem],
            recv_sem=recv_sems.at[sem],
            device_id=(x, y),
            device_id_type=MESH,
        )

    def wait_bytes(ref, sem):
        pltpu.make_async_copy(ref, ref, sem).wait()

    def peers(body):
        def step(k, carry):
            body(lax.rem(gy + k, n_gy))
            return carry

        lax.fori_loop(1, n_gy, step, 0)

    peers(lambda y: greet(gx, y))

    @pl.when(jnp.logical_not(first_x))
    def _():
        greet(gx - 1, gy)

    @pl.when(jnp.logical_not(last_x))
    def _():
        greet(gx + 1, gy)

    @pl.when(edge_x)
    def _():
        def step(y, carry):
            greet(facing, y)
            return carry

        lax.fori_loop(0, n_gy, step, 0)

    whole = cells // 128
    for field in range(8):
        for plane in range(2):
            for chunk in range(4):
                if chunk < whole:
                    part = state_ref[field, plane, :, pl.ds(128 * chunk, 128)]
                else:
                    part = state_ref[field, plane, :, pl.ds(128 * whole, cells - 128 * whole)]
                    part = jnp.concatenate([part, jnp.zeros((ROWS, 128 * (whole + 1) - cells), jnp.float32)], axis=1)
                raw[pl.ds(field * 32 + plane * 4 + chunk, ROWS, stride=8), :] = part
    to_left[...] = raw[pl.ds(0, 64, stride=4), :]
    to_right[...] = raw[pl.ds(3, 64, stride=4), :]
    held[...] = behind(raw[...].reshape(LINES, 8, 128), 2)
    pl.semaphore_wait(barrier, n_gy - 1 + jnp.where(edge_x, n_gy + 1, 2))

    strip_left = send(to_left, from_right, 0, gx, left_y)
    strip_right = send(to_right, from_left, 1, gx, right_y)
    strip_left.start()
    strip_right.start()
    base = jnp.where(first_x, 0, 2)

    def boundary_tile(t):
        plain = lax.div(t, 2) * ROWS + base + lax.rem(t, 2)
        return jnp.where(t == STRIPS - 1, FACE_X * ROWS + 2, plain)

    mine = jnp.where(lax.rem(gy, 2) == 0, lax.div(gy, 2), half + lax.div(gy, 2))

    @pl.when(edge_x)
    def _():
        def step(t, carry):
            rank = lax.rem(t, n_gy)
            slot = lax.div(t, n_gy)
            owner = jnp.where(rank < half, 2 * rank, 2 * (rank - half) + 1)
            source = held.at[boundary_tile(t)]
            target = strip_in.at[slot, pl.ds(pl.multiple_of(8 * gy, 8), 8), :]

            @pl.when(owner != gy)
            def _():
                send(source, target, 2, gx, owner).start()

            @pl.when(owner == gy)
            def _():
                pltpu.make_async_copy(source, target, recv_sems.at[2]).start()

            return carry

        lax.fori_loop(0, STRIPS, step, 0)

    strip_left.wait_recv()
    strip_right.wait_recv()
    lane = lax.broadcasted_iota(jnp.int32, (LINES, 8, 128), 2)
    chunk = lax.broadcasted_iota(jnp.int32, (LINES, 8, 128), 1) % 4
    beyond = cells % 128
    after = from_right[...]
    edges[pl.ds(0, 64, stride=4), :] = pltpu.roll(from_left[...], 130 - beyond, 1)
    edges[pl.ds(3, 64, stride=4), :] = pltpu.roll(after, beyond + 2, 1)
    outside = jnp.logical_or(
        jnp.logical_and(chunk == 0, lane < 2), jnp.logical_and(chunk == 3, lane >= beyond + 2)
    )
    full = jnp.where(outside, edges[...].reshape(LINES, 8, 128), held[...])
    for field in range(8):
        ext[field, 2:6] = full[ROWS * field : ROWS * field + ROWS]
    next_edges[pl.ds(3, 2 * ROWS, stride=4), :] = pltpu.roll(after[2 * ROWS * FACE_Y : 2 * ROWS * (FACE_Y + 1)], beyond + 1, 1)
    final = jnp.logical_and(chunk == 3, lane == 127)[:ROWS]
    ext[NEXT_Y, 2:6] = jnp.where(
        final, next_edges[...].reshape(ROWS, 8, 128), ahead(full[ROWS * FACE_Y : ROWS * (FACE_Y + 1)], 1)
    )

    to_up = send(ext.at[:, pl.ds(4, 2)], ext.at[:, pl.ds(0, 2)], 3, gx + 1, gy)
    to_down = send(ext.at[:, pl.ds(2, 2)], ext.at[:, pl.ds(6, 2)], 4, gx - 1, gy)
    to_down_face = send(ext.at[FACE_X, 4], last_face, 5, gx - 1, gy)

    @pl.when(jnp.logical_not(last_x))
    def _():
        to_up.start()

    @pl.when(jnp.logical_not(first_x))
    def _():
        to_down.start()
        to_down_face.start()

    @pl.when(edge_x)
    def _():
        total_cells = cells * n_gy
        offset = shear_ref[0]
        amount = jnp.where(first_x, lax.rem(total_cells - offset, total_cells), offset)
        amount_next = lax.rem(amount + total_cells - 1, total_cells)
        landing = jnp.where(first_x, 6, 0)

        def ship(tiles, field, row, sem):
            def step(y, carry):
                send(tiles.at[y], ext.at[field, row], sem, facing, y).start()
                return carry

            lax.fori_loop(0, n_gy, step, 0)

        def ship_face(tiles):
            def step(y, carry):
                send(tiles.at[y], last_face, 5, facing, y).start()
                return carry

            lax.fori_loop(0, n_gy, step, 0)

        for slot in range(slots):
            t = slot * n_gy + mine
            field = lax.div(t, 2)

            @pl.when(t < STRIPS)
            def _(slot=slot, t=t, field=field):
                block = strip_in.at[slot, pl.ds(0, 8 * n_gy), :]
                wait_bytes(block, recv_sems.at[2])
                strip_in[slot, pl.ds(8 * n_gy, 8 * n_gy), :] = strip_in[slot, pl.ds(0, 8 * n_gy), :]
                strip_out[slot] = window(strip_in, slot, n_gy, cells, amount, 3)

                @pl.when(t < STRIPS - 1)
                def _():
                    ship(strip_out.at[slot], field, landing + lax.rem(t, 2), jnp.where(first_x, 4, 3))

                @pl.when(jnp.logical_and(t == STRIPS - 1, first_x))
                def _():
                    ship_face(strip_out.at[slot])

                @pl.when(field == FACE_Y)
                def _():
                    moved[slot] = window(strip_in, slot, n_gy, cells, amount_next, 3)
                    ship(moved.at[slot], NEXT_Y, landing + lax.rem(t, 2), jnp.where(first_x, 4, 3))

    wait_bytes(ext.at[:, pl.ds(0, 2)], recv_sems.at[3])
    wait_bytes(ext.at[:, pl.ds(6, 2)], recv_sems.at[4])
    wait_bytes(last_face, recv_sems.at[5])

    fields = [ext[field] for field in range(8)]
    fields[FACE_X] = jnp.concatenate([fields[FACE_X], last_face[...][None]], axis=0)
    once = euler(fields, ext[NEXT_Y])
    twice = euler(once, ahead(once[FACE_Y], 1))
    for field in range(8):
        lines[ROWS * field : ROWS * field + ROWS] = 0.5 * (ext[field, 2:6] + twice[field][:ROWS])

    def spread(source, target, sem):
        def step(t, carry):
            owner = lax.div(t, per)

            @pl.when(owner != gy)
            def _():
                send(source(t, owner), target(t), sem, gx, owner).start()

            @pl.when(owner == gy)
            def _():
                pltpu.make_async_copy(source(t, owner), target(t), recv_sems.at[sem]).start()

            return carry

        lax.fori_loop(0, LINES, step, 0)

    spread(
        lambda t, owner: lines.at[t],
        lambda t: line_in.at[lax.rem(t, per), pl.ds(pl.multiple_of(8 * gy, 8), 8), :],
        6,
    )
    wait_bytes(line_in.at[:, pl.ds(0, 8 * n_gy), :], recv_sems.at[6])

    for slot in range(per):
        row = lax.rem(gy * per + slot, ROWS)
        line_in[slot, pl.ds(8 * n_gy, 8 * n_gy), :] = line_in[slot, pl.ds(0, 8 * n_gy), :]
        tiles = window(line_in, slot, n_gy, cells, remap_ref[row], 2)
        weight = (frac_ref[row].astype(jnp.float32) + 0.5) / FRAC
        line_out[slot] = (1.0 - weight) * ahead(tiles, 2) + weight * ahead(tiles, 1)

    def back(k, carry):
        y = lax.div(k, per)
        slot = lax.rem(k, per)
        source = line_out.at[slot, y]
        target = raw.at[pl.ds(pl.multiple_of(8 * (gy * per + slot), 8), 8), :]

        @pl.when(y != gy)
        def _():
            send(source, target, 7, gx, y).start()

        @pl.when(y == gy)
        def _():
            pltpu.make_async_copy(source, target, recv_sems.at[7]).start()

        return carry

    lax.fori_loop(0, LINES, back, 0)
    wait_bytes(raw, recv_sems.at[7])
    for field in range(8):
        for plane in range(2):
            for chunk in range(4):
                part = raw[pl.ds(field * 32 + plane * 4 + chunk, ROWS, stride=8), :]
                width = min(128, cells - 128 * chunk)
                out_ref[field, plane, :, pl.ds(128 * chunk, width)] = part[:, :width]

    strip_left.wait_send()
    strip_right.wait_send()

    @pl.when(jnp.logical_not(last_x))
    def _():
        to_up.wait_send()

    @pl.when(jnp.logical_not(first_x))
    def _():
        to_down.wait_send()
        to_down_face.wait_send()

    @pl.when(edge_x)
    def _():
        for count in range(STRIPS - slots, STRIPS + 1):
            own = sum((slot * n_gy + mine < STRIPS).astype(jnp.int32) for slot in range(slots))

            @pl.when(STRIPS - own == count)
            def _(count=count):
                wait_bytes(held.at[pl.ds(0, count)], send_sems.at[2])

        for slot in range(slots):
            t = slot * n_gy + mine
            field = lax.div(t, 2)

            @pl.when(t < STRIPS - 1)
            def _(slot=slot):
                wait_bytes(strip_out.at[slot], send_sems.at[jnp.where(first_x, 4, 3)])

            @pl.when(jnp.logical_and(t == STRIPS - 1, first_x))
            def _(slot=slot):
                wait_bytes(strip_out.at[slot], send_sems.at[5])

            @pl.when(jnp.logical_and(t < STRIPS, field == FACE_Y))
            def _(slot=slot):
                wait_bytes(moved.at[slot], send_sems.at[jnp.where(first_x, 4, 3)])

    wait_bytes(lines.at[pl.ds(0, LINES - per)], send_sems.at[6])
    wait_bytes(lines.at[pl.ds(0, LINES - per)], send_sems.at[7])


def solution(mesh):
    n_gx = mesh.shape["gx"]
    n_gy = mesh.shape["gy"]

    def shards(state, shear_offset, remap_shift, frac_index):
        cells = state.shape[3]
        per = LINES // n_gy
        slots = -(-STRIPS // n_gy)
        vmem = lambda *shape: pltpu.VMEM(shape, jnp.float32)
        small = pl.BlockSpec(memory_space=pltpu.SMEM)
        large = pl.BlockSpec(memory_space=pltpu.VMEM)
        return pl.pallas_call(
            functools.partial(kernel, n_gx, n_gy, cells),
            out_shape=jax.ShapeDtypeStruct(state.shape, jnp.float32),
            in_specs=[small, small, small, large],
            out_specs=large,
            scratch_shapes=[
                vmem(8 * LINES, 128),
                vmem(LINES, 8, 128),
                vmem(9, 8, 8, 128),
                vmem(8, 128),
                vmem(64, 128),
                vmem(64, 128),
                vmem(64, 128),
                vmem(64, 128),
                vmem(8 * LINES, 128),
                vmem(8 * ROWS, 128),
                vmem(slots, 16 * n_gy, 128),
                vmem(slots, n_gy, 8, 128),
                vmem(slots, n_gy, 8, 128),
                vmem(per, 16 * n_gy, 128),
                vmem(per, n_gy, 8, 128),
                vmem(LINES, 8, 128),
                pltpu.SemaphoreType.DMA((8,)),
                pltpu.SemaphoreType.DMA((8,)),
            ],
            compiler_params=pltpu.CompilerParams(collective_id=0, has_side_effects=True),
        )(shear_offset, remap_shift, frac_index, state)

    placed = (P(None, None, "gx", "gy"), P(), P("gx"), P("gx"))
    return jax.shard_map(shards, mesh=mesh, in_specs=placed, out_specs=P(None, None, "gx", "gy"), check_vma=False)
```

```python
import functools

import jax
import jax.numpy as jnp
from jax import lax
from jax.experimental import pallas as pl
from jax.experimental.pallas import tpu as pltpu
from jax.sharding import PartitionSpec as P

FRAC = 16
GAMMA_LESS = 5.0 / 3.0 - 1.0
ROTATION = 1.0
SHEAR_RATE = 1.5
MAX_SPEED = 5.0
TIME_STEP = 0.05

FACE_X, FACE_Y, FACE_Z, NEXT_Y = 5, 6, 7, 8
ROWS = 4
LINES = 8 * ROWS
STRIPS = 17
MESH = pl.DeviceIdType.MESH


def ahead(value, count):
    lane = lax.broadcasted_iota(jnp.int32, value.shape, 2)
    moved = pltpu.roll(value, 128 - count, 2)
    return jnp.where(lane >= 128 - count, pltpu.roll(moved, 7, 1), moved)


def behind(value, count):
    lane = lax.broadcasted_iota(jnp.int32, value.shape, 2)
    moved = pltpu.roll(value, count, 2)
    return jnp.where(lane < count, pltpu.roll(moved, 1, 1), moved)


def other_plane(value):
    return pltpu.roll(value, 4, 1)


def euler(fields, next_y):
    density, mom_x, mom_y, mom_z, energy, face_x, face_y, face_z = fields
    rows = density.shape[0]
    mid = slice(1, rows - 1)
    cen_x = 0.5 * (face_x[:-1] + face_x[1:])
    cen_y = 0.5 * (face_y + next_y)
    cen_z = 0.5 * (face_z + other_plane(face_z))
    inverse = 1.0 / density
    vel_x = mom_x * inverse
    vel_y = mom_y * inverse
    vel_z = mom_z * inverse
    magnetic = 0.5 * (cen_x * cen_x + cen_y * cen_y + cen_z * cen_z)
    pressure = (
        GAMMA_LESS * (energy - 0.5 * (mom_x * vel_x + mom_y * vel_y + mom_z * vel_z) - magnetic) + magnetic
    )
    vel_dot = vel_x * cen_x + vel_y * cen_y + vel_z * cen_z
    conserved = (density, mom_x, mom_y, mom_z, energy)
    momenta = (mom_x, mom_y, mom_z)
    centred = (cen_x, cen_y, cen_z)
    velocity = (vel_x, vel_y, vel_z)
    change = [None] * 5
    for normal in range(3):
        part = slice(None) if normal == 0 else mid
        speed = velocity[normal][part]
        across = centred[normal][part]
        fluxes = [momenta[normal][part]]
        for second in range(3):
            term = momenta[second][part] * speed - across * centred[second][part]
            if second == normal:
                term = term + pressure[part]
            fluxes.append(term)
        fluxes.append((energy[part] + pressure[part]) * speed - across * vel_dot[part])
        for member in range(5):
            flux = fluxes[member]
            held = conserved[member][part]
            if normal == 0:
                upwind = 0.5 * (flux[:-1] + flux[1:]) - 0.5 * MAX_SPEED * (held[1:] - held[:-1])
                delta = upwind[1:] - upwind[:-1]
            elif normal == 1:
                upwind = 0.5 * (behind(flux, 1) + flux) - 0.5 * MAX_SPEED * (held - behind(held, 1))
                delta = ahead(upwind, 1) - upwind
            else:
                upwind = 0.5 * (other_plane(flux) + flux) - 0.5 * MAX_SPEED * (held - other_plane(held))
                delta = other_plane(upwind) - upwind
            change[member] = -delta if change[member] is None else change[member] - delta
    change[1] = change[1] + 2.0 * ROTATION * mom_y[mid]
    change[2] = change[2] - (2.0 - SHEAR_RATE) * ROTATION * mom_x[mid]
    change[4] = change[4] + SHEAR_RATE * ROTATION * (mom_x[mid] * vel_y[mid] - cen_x[mid] * cen_y[mid])
    elec_x = -(vel_y * cen_z - vel_z * cen_y)
    elec_y = -(vel_z * cen_x - vel_x * cen_z)
    elec_z = -(vel_x * cen_y - vel_y * cen_x)
    pair_x = elec_x[mid] + behind(elec_x[mid], 1)
    edge_x = 0.25 * (pair_x + other_plane(pair_x))
    pair_y = elec_y[1:] + elec_y[:-1]
    edge_y = 0.25 * (pair_y + other_plane(pair_y))
    pair_z = elec_z[1:] + elec_z[:-1]
    edge_z = 0.25 * (pair_z + behind(pair_z, 1))
    delta_x = -(ahead(edge_z, 1) - edge_z - (other_plane(edge_y) - edge_y))
    delta_y = -(other_plane(edge_x) - edge_x - (edge_z[1:] - edge_z[:-1]))
    delta_z = -(edge_y[1:] - edge_y[:-1] - (ahead(edge_x, 1) - edge_x))
    done = [conserved[member][mid] + TIME_STEP * change[member] for member in range(5)]
    done.append(face_x[1:rows] + TIME_STEP * delta_x)
    done.append(face_y[mid] + TIME_STEP * delta_y)
    done.append(face_z[mid] + TIME_STEP * delta_z)
    return done


def window(ref, slot, blocks, cells, amount, kinds):
    hops = lax.div(amount, cells)
    rest = lax.rem(amount, cells)
    if kinds == 3:
        low = rest < 2
        hops = jnp.where(low, hops - 1, hops)
        rest = jnp.where(low, rest + cells, rest)
    total = blocks * 8
    lane = lax.broadcasted_iota(jnp.int32, (blocks, 8, 128), 2)
    chunk = lax.broadcasted_iota(jnp.int32, (blocks, 8, 128), 1) % 4
    place = chunk * 128 + lane - 2 - rest
    result = None
    for kind in reversed(range(kinds)):
        distance = rest - kind * cells + 1024
        lanes = lax.rem(distance, 128)
        sublanes = lax.div(distance, 128) - 8
        back = lax.rem(8 * (hops + kind) + sublanes + total, total)
        near = ref[slot, pl.ds(total - back, total), :].reshape(blocks, 8, 128)
        far = ref[slot, pl.ds(total - back - 1, total), :].reshape(blocks, 8, 128)
        near = pltpu.roll(near, lanes, 2)
        far = pltpu.roll(far, lanes, 2)
        moved = jnp.where(lane >= lanes, near, far)
        if result is None:
            result = moved
        else:
            result = jnp.where(place >= -kind * cells, moved, result)
    return result


def kernel(
    n_gx,
    n_gy,
    cells,
    shear_hbm,
    remap_hbm,
    frac_hbm,
    state_hbm,
    out_ref,
    shear_ref,
    remap_ref,
    frac_ref,
    state_ref,
    raw,
    held,
    ext,
    last_face,
    to_left,
    to_right,
    from_left,
    from_right,
    edges,
    next_edges,
    strip_in_0,
    strip_in_1,
    strip_out,
    moved,
    line_in,
    line_out,
    lines,
    send_sems,
    recv_sems,
    load_sems,
    known,
):
    gx = lax.axis_index("gx")
    gy = lax.axis_index("gy")
    half = n_gy // 2
    slots = -(-STRIPS // n_gy)
    per = LINES // n_gy
    left_y = lax.rem(gy + n_gy - 1, n_gy)
    right_y = lax.rem(gy + 1, n_gy)
    inside = lax.rem(gy, half)
    side = gy - inside
    core = gy + 1 - 2 * lax.rem(gy, 2)
    up, down, up_2, down_2 = (side + lax.rem(inside + half + step, half) for step in (2, -2, 4, -4))
    partner = lax.rem(gx + n_gx // 2, n_gx)
    last = n_gx - 1
    first_x = gx == 0
    last_x = gx == last
    strip_in = (strip_in_0, strip_in_1)
    barrier = pltpu.get_barrier_semaphore()
    load = pltpu.make_async_copy(state_hbm, state_ref, load_sems.at[0])
    load.start()
    load_shear = pltpu.make_async_copy(shear_hbm, shear_ref, load_sems.at[1])
    load_shear.start()

    def tell(sem, x, y):
        pl.semaphore_signal(sem, inc=1, device_id=(x, y), device_id_type=MESH)

    def everyone(body):
        def step(k, carry):
            body(lax.rem(k + gy, n_gy))
            return carry

        lax.fori_loop(0, n_gy, step, 0)

    def send(source, target, sent, arrived, x, y):
        return pltpu.make_async_remote_copy(
            src_ref=source,
            dst_ref=target,
            send_sem=send_sems.at[sent],
            recv_sem=recv_sems.at[arrived],
            device_id=(x, y),
            device_id_type=MESH,
        )

    def wait_bytes(ref, sem):
        pltpu.make_async_copy(ref, ref, sem).wait()

    for y in (left_y, right_y, up, down):
        tell(barrier, gx, y)
    for y in (gy, lax.rem(gy + half, n_gy)):
        tell(barrier, partner, y)

    @pl.when(jnp.logical_not(first_x))
    def _():
        tell(barrier, gx - 1, gy)

    @pl.when(jnp.logical_not(last_x))
    def _():
        tell(barrier, gx + 1, gy)

    @pl.when(first_x)
    def _():
        tell(barrier, 0, lax.rem(gy + half, n_gy))
        everyone(lambda y: tell(barrier, last, y))

    load.wait()
    whole = cells // 128
    for field in range(8):
        for plane in range(2):
            for chunk in range(4):
                if chunk < whole:
                    part = state_ref[field, plane, :, pl.ds(128 * chunk, 128)]
                else:
                    part = state_ref[field, plane, :, pl.ds(128 * whole, cells - 128 * whole)]
                    part = jnp.concatenate([part, jnp.zeros((ROWS, 128 * (whole + 1) - cells), jnp.float32)], axis=1)
                raw[pl.ds(field * 32 + plane * 4 + chunk, ROWS, stride=8), :] = part
    to_left[...] = raw[pl.ds(0, 64, stride=4), :]
    to_right[...] = raw[pl.ds(3, 64, stride=4), :]
    held[...] = behind(raw[...].reshape(LINES, 8, 128), 2)
    pl.semaphore_wait(barrier, jnp.where(last_x, 7 + n_gy, 8))
    for y in (core, up, down):
        tell(known.at[0], gx, y)

    def strips_to_first(count, base, way):
        def step(k, carry):
            t = lax.rem(k + lax.div(gy, 2), count)
            rank = lax.rem(t, n_gy)
            slot = lax.div(t, n_gy)
            owner = jnp.where(rank < half, 2 * rank, 2 * (rank - half) + 1)
            tile = lax.div(t, 2) * ROWS + base + lax.rem(t, 2)
            tile = jnp.where(t == STRIPS - 1, FACE_X * ROWS + 2, tile)
            target = strip_in[way].at[slot, pl.ds(pl.multiple_of(8 * gy, 8), 8), :]
            arrived = 8 + slots * way + slot

            @pl.when(jnp.logical_or(last_x, owner != gy))
            def _():
                send(held.at[tile], target, 2, arrived, 0, owner).start()

            @pl.when(jnp.logical_and(first_x, owner == gy))
            def _():
                pltpu.make_async_copy(held.at[tile], target, recv_sems.at[arrived]).start()

            return carry

        lax.fori_loop(0, count, step, 0)

    @pl.when(last_x)
    def _():
        strips_to_first(STRIPS - 1, 2, 1)
        everyone(lambda y: tell(known.at[3], 0, y))

    strip_left = send(to_left, from_right, 0, 0, gx, left_y)
    strip_right = send(to_right, from_left, 1, 1, gx, right_y)
    strip_left.start()
    strip_right.start()
    amounts = send(remap_hbm, remap_ref, 10, 8 + 2 * slots, partner, gy)
    levels = send(frac_hbm, frac_ref, 11, 9 + 2 * slots, partner, gy)
    amounts.start()
    levels.start()
    pl.semaphore_wait(known.at[0], 3)
    if half > 4:
        for y in (up_2, down_2):
            tell(known.at[1], gx, y)
        pl.semaphore_wait(known.at[1], 2)
    for y in (gy, core):
        tell(known.at[2], partner, y)
        tell(known.at[2], partner, lax.rem(y + half, n_gy))

    @pl.when(first_x)
    def _():
        tell(known.at[4], 0, core)
        for y in (gy, core):
            tell(known.at[4], 0, lax.rem(y + half, n_gy))
        pl.semaphore_wait(known.at[4], 3)
        strips_to_first(STRIPS, 0, 0)

    strip_left.wait_recv()
    strip_right.wait_recv()
    lane = lax.broadcasted_iota(jnp.int32, (LINES, 8, 128), 2)
    chunk = lax.broadcasted_iota(jnp.int32, (LINES, 8, 128), 1) % 4
    beyond = cells % 128
    after = from_right[...]
    edges[pl.ds(0, 64, stride=4), :] = pltpu.roll(from_left[...], 130 - beyond, 1)
    edges[pl.ds(3, 64, stride=4), :] = pltpu.roll(after, beyond + 2, 1)
    outside = jnp.logical_or(
        jnp.logical_and(chunk == 0, lane < 2), jnp.logical_and(chunk == 3, lane >= beyond + 2)
    )
    full = jnp.where(outside, edges[...].reshape(LINES, 8, 128), held[...])
    for field in range(8):
        ext[field, 2:6] = full[ROWS * field : ROWS * field + ROWS]
    next_edges[pl.ds(3, 2 * ROWS, stride=4), :] = pltpu.roll(after[2 * ROWS * FACE_Y : 2 * ROWS * (FACE_Y + 1)], beyond + 1, 1)
    final = jnp.logical_and(chunk == 3, lane == 127)[:ROWS]
    ext[NEXT_Y, 2:6] = jnp.where(
        final, next_edges[...].reshape(ROWS, 8, 128), ahead(full[ROWS * FACE_Y : ROWS * (FACE_Y + 1)], 1)
    )

    to_up = send(ext.at[:, pl.ds(4, 2)], ext.at[:, pl.ds(0, 2)], 3, 3, gx + 1, gy)
    to_down = send(ext.at[:, pl.ds(2, 2)], ext.at[:, pl.ds(6, 2)], 4, 4, gx - 1, gy)
    to_down_face = send(ext.at[FACE_X, 4], last_face, 5, 5, gx - 1, gy)

    @pl.when(jnp.logical_not(last_x))
    def _():
        to_up.start()

    @pl.when(jnp.logical_not(first_x))
    def _():
        to_down.start()
        to_down_face.start()

    load_shear.wait()

    mine = jnp.where(lax.rem(gy, 2) == 0, lax.div(gy, 2), half + lax.div(gy, 2))

    @pl.when(first_x)
    def _():
        total_cells = cells * n_gy
        offset = shear_ref[0]
        shifts = (lax.rem(total_cells - offset, total_cells), offset)

        def hand(way, tiles, target, arrived):
            def one(y):
                @pl.when(jnp.logical_or(way == 0, y != gy))
                def _():
                    send(tiles.at[y], target, 8 + way, arrived, last * (1 - way), y).start()

                if way == 1:

                    @pl.when(y == gy)
                    def _():
                        pltpu.make_async_copy(tiles.at[y], target, recv_sems.at[arrived]).start()

            everyone(one)

        for way in range(2):
            for slot in range(slots):
                t = slot * n_gy + mine
                field = lax.div(t, 2)

                @pl.when(t < STRIPS - way)
                def _(way=way, slot=slot, field=field):
                    wait_bytes(strip_in[way].at[slot, pl.ds(0, 8 * n_gy), :], recv_sems.at[8 + slots * way + slot])
                    strip_in[way][slot, pl.ds(8 * n_gy, 8 * n_gy), :] = strip_in[way][slot, pl.ds(0, 8 * n_gy), :]
                    strip_out[way, slot] = window(strip_in[way], slot, n_gy, cells, shifts[way], 3)

                    @pl.when(field == FACE_Y)
                    def _():
                        shift = lax.rem(shifts[way] + total_cells - 1, total_cells)
                        moved[way, slot] = window(strip_in[way], slot, n_gy, cells, shift, 3)

            if way == 0:
                pl.semaphore_wait(known.at[3], n_gy)
            for slot in range(slots):
                t = slot * n_gy + mine
                field = lax.div(t, 2)
                landing = 6 * (1 - way) + lax.rem(t, 2)

                @pl.when(t < STRIPS - 1)
                def _(way=way, slot=slot, field=field, landing=landing):
                    hand(way, strip_out.at[way, slot], ext.at[field, landing], 4 - way)

                @pl.when(field == FACE_Y)
                def _(way=way, slot=slot, landing=landing):
                    hand(way, moved.at[way, slot], ext.at[NEXT_Y, landing], 4 - way)

                if way == 0:

                    @pl.when(t == STRIPS - 1)
                    def _(way=way, slot=slot):
                        hand(way, strip_out.at[way, slot], last_face, 5)

    wait_bytes(ext.at[:, pl.ds(0, 2)], recv_sems.at[3])
    wait_bytes(ext.at[:, pl.ds(6, 2)], recv_sems.at[4])
    wait_bytes(last_face, recv_sems.at[5])

    fields = [ext[field] for field in range(8)]
    fields[FACE_X] = jnp.concatenate([fields[FACE_X], last_face[...][None]], axis=0)
    once = euler(fields, ext[NEXT_Y])
    twice = euler(once, ahead(once[FACE_Y], 1))
    for field in range(8):
        lines[ROWS * field : ROWS * field + ROWS] = 0.5 * (ext[field, 2:6] + twice[field][:ROWS])

    def spread(k, carry):
        t = lax.rem(k + (gy + half) * per, LINES)
        slot = lax.rem(t, per)
        target = line_in.at[slot, pl.ds(pl.multiple_of(8 * gy, 8), 8), :]
        send(lines.at[t], target, 6, 6, partner, lax.div(t, per)).start()
        return carry

    pl.semaphore_wait(known.at[2], 4)
    lax.fori_loop(0, LINES, spread, 0)
    amounts.wait_recv()
    levels.wait_recv()
    wait_bytes(line_in.at[:, pl.ds(0, 8 * n_gy), :], recv_sems.at[6])

    for slot in range(per):
        row = lax.rem(gy * per + slot, ROWS)
        line_in[slot, pl.ds(8 * n_gy, 8 * n_gy), :] = line_in[slot, pl.ds(0, 8 * n_gy), :]
        tiles = window(line_in, slot, n_gy, cells, remap_ref[row], 2)
        weight = (frac_ref[row].astype(jnp.float32) + 0.5) / FRAC
        line_out[slot] = (1.0 - weight) * ahead(tiles, 2) + weight * ahead(tiles, 1)

    def back(k, carry):
        y = lax.rem(lax.div(k, per) + gy + half, n_gy)
        slot = lax.rem(k, per)
        target = raw.at[pl.ds(pl.multiple_of(8 * (gy * per + slot), 8), 8), :]
        send(line_out.at[slot, y], target, 7, 7, partner, y).start()
        return carry

    lax.fori_loop(0, LINES, back, 0)
    wait_bytes(raw, recv_sems.at[7])
    for field in range(8):
        for plane in range(2):
            for chunk in range(4):
                part = raw[pl.ds(field * 32 + plane * 4 + chunk, ROWS, stride=8), :]
                width = min(128, cells - 128 * chunk)
                out_ref[field, plane, :, pl.ds(128 * chunk, width)] = part[:, :width]

    for copy in (strip_left, strip_right, amounts, levels):
        copy.wait_send()

    @pl.when(jnp.logical_not(last_x))
    def _():
        to_up.wait_send()

    @pl.when(jnp.logical_not(first_x))
    def _():
        to_down.wait_send()
        to_down_face.wait_send()

    own = sum((slot * n_gy + mine < STRIPS).astype(jnp.int32) for slot in range(slots))
    for count in sorted({STRIPS - 1, STRIPS - slots, STRIPS - slots + 1}):

        @pl.when(jnp.logical_or(last_x & (count == STRIPS - 1), first_x & (STRIPS - own == count)))
        def _(count=count):
            wait_bytes(held.at[pl.ds(0, count)], send_sems.at[2])

    @pl.when(first_x)
    def _():
        for way in range(2):
            for slot in range(slots):
                t = slot * n_gy + mine

                @pl.when(t < STRIPS - way)
                def _(way=way, slot=slot):
                    wait_bytes(strip_out.at[way, slot, pl.ds(0, n_gy - way)], send_sems.at[8 + way])

                @pl.when(lax.div(t, 2) == FACE_Y)
                def _(way=way, slot=slot):
                    wait_bytes(moved.at[way, slot, pl.ds(0, n_gy - way)], send_sems.at[8 + way])

    wait_bytes(lines, send_sems.at[6])
    wait_bytes(lines, send_sems.at[7])


def solution(mesh):
    n_gx = mesh.shape["gx"]
    n_gy = mesh.shape["gy"]

    def shards(state, shear_offset, remap_shift, frac_index):
        cells = state.shape[3]
        per = LINES // n_gy
        slots = -(-STRIPS // n_gy)
        vmem = lambda *shape: pltpu.VMEM(shape, jnp.float32)
        large = pl.BlockSpec(memory_space=pltpu.VMEM)
        whole = pl.BlockSpec(memory_space=pl.ANY)
        return pl.pallas_call(
            functools.partial(kernel, n_gx, n_gy, cells),
            out_shape=jax.ShapeDtypeStruct(state.shape, jnp.float32),
            in_specs=[whole] * 4,
            out_specs=large,
            scratch_shapes=[
                pltpu.SMEM((1,), jnp.int32),
                pltpu.SMEM((ROWS,), jnp.int32),
                pltpu.SMEM((ROWS,), jnp.int32),
                vmem(*state.shape),
                vmem(8 * LINES, 128),
                vmem(LINES, 8, 128),
                vmem(9, 8, 8, 128),
                vmem(8, 128),
                vmem(64, 128),
                vmem(64, 128),
                vmem(64, 128),
                vmem(64, 128),
                vmem(8 * LINES, 128),
                vmem(8 * ROWS, 128),
                vmem(slots, 16 * n_gy, 128),
                vmem(slots, 16 * n_gy, 128),
                vmem(2, slots, n_gy, 8, 128),
                vmem(2, slots, n_gy, 8, 128),
                vmem(per, 16 * n_gy, 128),
                vmem(per, n_gy, 8, 128),
                vmem(LINES, 8, 128),
                pltpu.SemaphoreType.DMA((12,)),
                pltpu.SemaphoreType.DMA((10 + 2 * slots,)),
                pltpu.SemaphoreType.DMA((2,)),
                pltpu.SemaphoreType.REGULAR((5,)),
            ],
            compiler_params=pltpu.CompilerParams(collective_id=0, has_side_effects=True),
        )(shear_offset, remap_shift, frac_index, state)

    placed = (P(None, None, "gx", "gy"), P(), P("gx"), P("gx"))
    return jax.shard_map(shards, mesh=mesh, in_specs=placed, out_specs=P(None, None, "gx", "gy"), check_vma=False)
```

```python
import functools

import jax
import jax.numpy as jnp
from jax import lax
from jax.experimental import pallas as pl
from jax.experimental.pallas import tpu as pltpu
from jax.sharding import PartitionSpec as P

FRAC = 16
GAMMA_LESS = 5.0 / 3.0 - 1.0
ROTATION = 1.0
SHEAR_RATE = 1.5
MAX_SPEED = 5.0
TIME_STEP = 0.05

FACE_X, FACE_Y, FACE_Z, NEXT_Y = 5, 6, 7, 8
ROWS = 4
LINES = 8 * ROWS
STRIPS = 16
PAGES = 6
MESH = pl.DeviceIdType.MESH


def ahead(value, count):
    lane = lax.broadcasted_iota(jnp.int32, value.shape, 2)
    moved = pltpu.roll(value, 128 - count, 2)
    return jnp.where(lane >= 128 - count, pltpu.roll(moved, 7, 1), moved)


def behind(value, count):
    lane = lax.broadcasted_iota(jnp.int32, value.shape, 2)
    moved = pltpu.roll(value, count, 2)
    return jnp.where(lane < count, pltpu.roll(moved, 1, 1), moved)


def other_plane(value):
    return pltpu.roll(value, 4, 1)


def euler(fields, next_y):
    density, mom_x, mom_y, mom_z, energy, face_x, face_y, face_z = fields
    rows = density.shape[0]
    mid = slice(1, rows - 1)
    cen_x = 0.5 * (face_x[:-1] + face_x[1:])
    cen_y = 0.5 * (face_y + next_y)
    cen_z = 0.5 * (face_z + other_plane(face_z))
    inverse = 1.0 / density
    vel_x = mom_x * inverse
    vel_y = mom_y * inverse
    vel_z = mom_z * inverse
    magnetic = 0.5 * (cen_x * cen_x + cen_y * cen_y + cen_z * cen_z)
    pressure = (
        GAMMA_LESS * (energy - 0.5 * (mom_x * vel_x + mom_y * vel_y + mom_z * vel_z) - magnetic) + magnetic
    )
    vel_dot = vel_x * cen_x + vel_y * cen_y + vel_z * cen_z
    conserved = (density, mom_x, mom_y, mom_z, energy)
    momenta = (mom_x, mom_y, mom_z)
    centred = (cen_x, cen_y, cen_z)
    velocity = (vel_x, vel_y, vel_z)
    change = [None] * 5
    for normal in range(3):
        part = slice(None) if normal == 0 else mid
        speed = velocity[normal][part]
        across = centred[normal][part]
        fluxes = [momenta[normal][part]]
        for second in range(3):
            term = momenta[second][part] * speed - across * centred[second][part]
            if second == normal:
                term = term + pressure[part]
            fluxes.append(term)
        fluxes.append((energy[part] + pressure[part]) * speed - across * vel_dot[part])
        for member in range(5):
            flux = fluxes[member]
            held = conserved[member][part]
            if normal == 0:
                upwind = 0.5 * (flux[:-1] + flux[1:]) - 0.5 * MAX_SPEED * (held[1:] - held[:-1])
                delta = upwind[1:] - upwind[:-1]
            elif normal == 1:
                upwind = 0.5 * (behind(flux, 1) + flux) - 0.5 * MAX_SPEED * (held - behind(held, 1))
                delta = ahead(upwind, 1) - upwind
            else:
                upwind = 0.5 * (other_plane(flux) + flux) - 0.5 * MAX_SPEED * (held - other_plane(held))
                delta = other_plane(upwind) - upwind
            change[member] = -delta if change[member] is None else change[member] - delta
    change[1] = change[1] + 2.0 * ROTATION * mom_y[mid]
    change[2] = change[2] - (2.0 - SHEAR_RATE) * ROTATION * mom_x[mid]
    change[4] = change[4] + SHEAR_RATE * ROTATION * (mom_x[mid] * vel_y[mid] - cen_x[mid] * cen_y[mid])
    elec_x = -(vel_y * cen_z - vel_z * cen_y)
    elec_y = -(vel_z * cen_x - vel_x * cen_z)
    elec_z = -(vel_x * cen_y - vel_y * cen_x)
    pair_x = elec_x[mid] + behind(elec_x[mid], 1)
    edge_x = 0.25 * (pair_x + other_plane(pair_x))
    pair_y = elec_y[1:] + elec_y[:-1]
    edge_y = 0.25 * (pair_y + other_plane(pair_y))
    pair_z = elec_z[1:] + elec_z[:-1]
    edge_z = 0.25 * (pair_z + behind(pair_z, 1))
    delta_x = -(ahead(edge_z, 1) - edge_z - (other_plane(edge_y) - edge_y))
    delta_y = -(other_plane(edge_x) - edge_x - (edge_z[1:] - edge_z[:-1]))
    delta_z = -(edge_y[1:] - edge_y[:-1] - (ahead(edge_x, 1) - edge_x))
    done = [conserved[member][mid] + TIME_STEP * change[member] for member in range(5)]
    done.append(face_x[1:rows] + TIME_STEP * delta_x)
    done.append(face_y[mid] + TIME_STEP * delta_y)
    done.append(face_z[mid] + TIME_STEP * delta_z)
    return done


def window(ref, slot, blocks, cells, amount, kinds):
    hops = lax.div(amount, cells)
    rest = lax.rem(amount, cells)
    if kinds == 3:
        low = rest < 2
        hops = jnp.where(low, hops - 1, hops)
        rest = jnp.where(low, rest + cells, rest)
    total = blocks * 8
    lane = lax.broadcasted_iota(jnp.int32, (blocks, 8, 128), 2)
    chunk = lax.broadcasted_iota(jnp.int32, (blocks, 8, 128), 1) % 4
    place = chunk * 128 + lane - 2 - rest
    result = None
    for kind in reversed(range(kinds)):
        distance = rest - kind * cells + 1024
        lanes = lax.rem(distance, 128)
        sublanes = lax.div(distance, 128) - 8
        back = lax.rem(8 * (hops + kind) + sublanes + total, total)
        near = ref[slot, pl.ds(total - back, total), :].reshape(blocks, 8, 128)
        far = ref[slot, pl.ds(total - back - 1, total), :].reshape(blocks, 8, 128)
        near = pltpu.roll(near, lanes, 2)
        far = pltpu.roll(far, lanes, 2)
        moved = jnp.where(lane >= lanes, near, far)
        if result is None:
            result = moved
        else:
            result = jnp.where(place >= -kind * cells, moved, result)
    return result


def kernel(
    n_gx,
    n_gy,
    cells,
    shear_hbm,
    remap_hbm,
    frac_hbm,
    state_hbm,
    out_ref,
    shear_ref,
    remap_ref,
    frac_ref,
    frac_own,
    state_ref,
    raw,
    held,
    ext,
    last_face,
    to_left,
    to_right,
    from_left,
    from_right,
    edges,
    next_edges,
    line_ghost,
    line_own,
    line_far,
    line_face,
    near_face,
    pages,
    framed,
    framed_next,
    ghost_next,
    framed_face,
    fresh,
    fresh_edges,
    to_next,
    from_previous,
    line_in,
    line_out,
    lines,
    send_sems,
    recv_sems,
    load_sems,
    known,
):
    gx = lax.axis_index("gx")
    gy = lax.axis_index("gy")
    half = n_gy // 2
    per = LINES // n_gy
    left_y = lax.rem(gy + n_gy - 1, n_gy)
    right_y = lax.rem(gy + 1, n_gy)
    inside = lax.rem(gy, half)
    side = gy - inside
    core = gy + 1 - 2 * lax.rem(gy, 2)
    up, down, up_2, down_2 = (side + lax.rem(inside + half + step, half) for step in (2, -2, 4, -4))
    core_up, core_down = (y + core - gy for y in (up, down))
    partner = lax.rem(gx + n_gx // 2, n_gx)
    middle = n_gx // 2
    last = n_gx - 1
    first_x = gx == 0
    last_x = gx == last
    barrier = pltpu.get_barrier_semaphore()
    load = pltpu.make_async_copy(state_hbm, state_ref, load_sems.at[0])
    load.start()
    small_loads = [
        pltpu.make_async_copy(source, target, load_sems.at[1 + k])
        for k, (source, target) in enumerate(
            ((shear_hbm, shear_ref), (frac_hbm, frac_own))
        )
    ]
    for copy in small_loads:
        copy.start()

    def tell(sem, x, y):
        pl.semaphore_signal(sem, inc=1, device_id=(x, y), device_id_type=MESH)

    def everyone(body):
        def step(k, carry):
            body(lax.rem(k + gy, n_gy))
            return carry

        lax.fori_loop(0, n_gy, step, 0)

    def send(source, target, sent, arrived, x, y):
        return pltpu.make_async_remote_copy(
            src_ref=source,
            dst_ref=target,
            send_sem=send_sems.at[sent],
            recv_sem=recv_sems.at[arrived],
            device_id=(x, y),
            device_id_type=MESH,
        )

    def wait_bytes(ref, sem):
        pltpu.make_async_copy(ref, ref, sem).wait()

    for y in (left_y, right_y, up, down):
        tell(barrier, gx, y)
    for y in (gy, lax.rem(gy + half, n_gy)):
        tell(barrier, partner, y)

    @pl.when(jnp.logical_not(first_x))
    def _():
        tell(barrier, gx - 1, gy)

    @pl.when(jnp.logical_not(last_x))
    def _():
        tell(barrier, gx + 1, gy)

    @pl.when(first_x)
    def _():
        tell(barrier, 0, lax.rem(gy + half, n_gy))

    @pl.when(jnp.logical_or(first_x, gx == middle))
    def _():
        everyone(lambda y: tell(barrier, last, y))

    load.wait()
    whole = cells // 128
    for field in range(8):
        for plane in range(2):
            for chunk in range(4):
                if chunk < whole:
                    part = state_ref[field, plane, :, pl.ds(128 * chunk, 128)]
                else:
                    part = state_ref[field, plane, :, pl.ds(128 * whole, cells - 128 * whole)]
                    part = jnp.concatenate([part, jnp.zeros((ROWS, 128 * (whole + 1) - cells), jnp.float32)], axis=1)
                raw[pl.ds(field * 32 + plane * 4 + chunk, ROWS, stride=8), :] = part
    to_left[...] = raw[pl.ds(0, 64, stride=4), :]
    to_right[...] = raw[pl.ds(3, 64, stride=4), :]
    held[...] = behind(raw[...].reshape(LINES, 8, 128), 2)
    pl.semaphore_wait(barrier, jnp.where(last_x, 7 + 2 * n_gy, 8))
    for y in (core, up, down):
        tell(known.at[0], gx, y)

    def line_place(buffer, t):
        return buffer.at[lax.rem(t, per), pl.ds(pl.multiple_of(8 * gy, 8), 8), :]

    @pl.when(last_x)
    def _():
        def step(k, carry):
            u = lax.rem(k + lax.div(gy, 2), STRIPS)
            t = lax.div(u, 2) * ROWS + 2 + lax.rem(u, 2)
            send(held.at[t], line_place(line_far, t), 2, 16 + lax.rem(t, per), middle, lax.div(t, per)).start()
            return carry

        lax.fori_loop(0, STRIPS, step, 0)
        everyone(lambda y: tell(known.at[3], 0, y))

    near_copy = send(held.at[FACE_X * ROWS], near_face, 12, 8, 0, gy)
    strip_left = send(to_left, from_right, 0, 0, gx, left_y)
    strip_right = send(to_right, from_left, 1, 1, gx, right_y)
    strip_left.start()
    strip_right.start()

    @pl.when(gx == 1)
    def _():
        near_copy.start()

    amounts = send(remap_hbm, remap_ref, 10, 9, partner, gy)
    levels = send(frac_hbm, frac_ref, 11, 10, partner, gy)
    amounts.start()
    levels.start()
    pl.semaphore_wait(known.at[0], 3)
    if half > 4:
        for y in (up_2, down_2):
            tell(known.at[1], gx, y)
        pl.semaphore_wait(known.at[1], 2)
    for y in (gy, core):
        tell(known.at[2], partner, y)
        tell(known.at[2], partner, lax.rem(y + half, n_gy))

    @pl.when(first_x)
    def _():
        for y in (gy, core):
            tell(known.at[4], 0, lax.rem(y + half, n_gy))
        for y in (core, up, down, core_up, core_down):
            tell(known.at[4], 0, y)
        pl.semaphore_wait(known.at[4], 7)

        def ghosts(k, carry):
            u = lax.rem(k + lax.div(gy, 2), STRIPS + 1)
            rank = lax.rem(u, n_gy)
            slot = lax.div(u, n_gy)
            owner = jnp.where(rank < half, 2 * rank, 2 * (rank - half) + 1)
            tile = jnp.where(u == STRIPS, FACE_X * ROWS + 2, lax.div(u, 2) * ROWS + lax.rem(u, 2))
            target = line_ghost.at[slot, pl.ds(pl.multiple_of(8 * gy, 8), 8), :]
            arrived = 16 + per + slot

            @pl.when(owner != gy)
            def _():
                send(held.at[tile], target, 14, arrived, 0, owner).start()

            @pl.when(owner == gy)
            def _():
                pltpu.make_async_copy(held.at[tile], target, recv_sems.at[arrived]).start()

            return carry

        def whole(k, carry):
            t = lax.rem(k + (gy + half) * per, LINES)
            send(held.at[t], line_place(line_own, t), 2, 2, middle, lax.div(t, per)).start()
            return carry

        lax.fori_loop(0, STRIPS + 1, ghosts, 0)
        lax.fori_loop(0, LINES, whole, 0)
        near_copy.wait_recv()
        send(near_face, line_place(line_face, 0), 13, 16 + 2 * per, middle, n_gy - 1).start()

    strip_left.wait_recv()
    strip_right.wait_recv()
    lane = lax.broadcasted_iota(jnp.int32, (LINES, 8, 128), 2)
    chunk = lax.broadcasted_iota(jnp.int32, (LINES, 8, 128), 1) % 4
    beyond = cells % 128
    after = from_right[...]
    edges[pl.ds(0, 64, stride=4), :] = pltpu.roll(from_left[...], 130 - beyond, 1)
    edges[pl.ds(3, 64, stride=4), :] = pltpu.roll(after, beyond + 2, 1)
    outside = jnp.logical_or(
        jnp.logical_and(chunk == 0, lane < 2), jnp.logical_and(chunk == 3, lane >= beyond + 2)
    )
    full = jnp.where(outside, edges[...].reshape(LINES, 8, 128), held[...])
    for field in range(8):
        ext[field, 2:6] = full[ROWS * field : ROWS * field + ROWS]
    next_edges[pl.ds(3, 2 * ROWS, stride=4), :] = pltpu.roll(after[2 * ROWS * FACE_Y : 2 * ROWS * (FACE_Y + 1)], beyond + 1, 1)
    final = jnp.logical_and(chunk == 3, lane == 127)[:ROWS]
    ext[NEXT_Y, 2:6] = jnp.where(
        final, next_edges[...].reshape(ROWS, 8, 128), ahead(full[ROWS * FACE_Y : ROWS * (FACE_Y + 1)], 1)
    )

    to_up = send(ext.at[:, pl.ds(4, 2)], ext.at[:, pl.ds(0, 2)], 3, 3, gx + 1, gy)
    to_down = send(ext.at[:, pl.ds(2, 2)], ext.at[:, pl.ds(6, 2)], 4, 4, gx - 1, gy)
    to_down_face = send(ext.at[FACE_X, 4], last_face, 5, 5, gx - 1, gy)

    @pl.when(jnp.logical_not(last_x))
    def _():
        to_up.start()

    @pl.when(jnp.logical_not(first_x))
    def _():
        to_down.start()
        to_down_face.start()

    for copy in small_loads:
        copy.wait()

    total_cells = cells * n_gy
    spare = n_gy - 1

    def fill(page, buffer, slot, amount):
        pages[page] = window(buffer, slot, n_gy, cells, amount, 3)

    def hand(page, target, sem, arrived, x):
        everyone(lambda y: send(pages.at[page, y], target, sem, arrived, x, y).start())

    def hand_next(page, target, sem, arrived, x):
        def one(y):
            following = lax.rem(y + 1, n_gy)
            for plane in range(2):
                source = pages.at[page, following, pl.ds(4 * plane, 1)]
                send(source, target(plane), sem, arrived, x, y).start()

        everyone(one)

    def next_faces(faces, rows):
        shape = faces.shape
        lanes = lax.broadcasted_iota(jnp.int32, shape, 2)
        places = lax.broadcasted_iota(jnp.int32, shape, 1)
        follow = pltpu.roll(jnp.broadcast_to(rows[:, 0:1, :], (2 * shape[0], 8, 128)), 123, 2)
        follow = follow.reshape(shape[0], 2, 8, 128)
        chosen = jnp.where(places < 4, follow[:, 0], follow[:, 1])
        return jnp.where((places % 4 == 3) & (lanes == 127), chosen, ahead(faces, 1))

    def wait_left():
        wait_bytes(ext.at[:, pl.ds(0, 2)], recv_sems.at[3])

    def wait_right():
        wait_bytes(ext.at[:, pl.ds(6, 2)], recv_sems.at[4])
        wait_bytes(last_face, recv_sems.at[5])

    places = []
    for slot in range(per):
        t = gy * per + slot
        places.append((slot, lax.div(t, ROWS), lax.rem(t, ROWS)))

    def own_conditions(r, field, row):
        inner = row < 3 + r
        return inner, jnp.logical_and(inner, field == FACE_Y), (row == 3) & (field == FACE_X) & (r == 0)

    def far_conditions(r, field, row):
        inner = row >= 2 + r
        return inner, jnp.logical_and(inner, field == FACE_Y)

    mine = jnp.where(lax.rem(gy, 2) == 0, lax.div(gy, 2), half + lax.div(gy, 2))
    ghost_places = []
    for slot in range(-(-(STRIPS + 1) // n_gy)):
        u = slot * n_gy + mine
        ghost_places.append((slot, u, lax.div(u, 2) == FACE_Y))

    @pl.when(first_x)
    def _():
        wait_right()
        ext[:, 0:2] = ext[:, 2:4]

    @pl.when(jnp.logical_not(first_x))
    def _():
        wait_left()

    @pl.when(jnp.logical_not(jnp.logical_or(first_x, last_x)))
    def _():
        wait_right()

    @pl.when(last_x)
    def _():
        wait_bytes(ext.at[pl.ds(0, 8), pl.ds(6, 2)], recv_sems.at[4])
        wait_bytes(last_face, recv_sems.at[5])
        wait_bytes(ghost_next.at[:, pl.ds(0, 1)], recv_sems.at[17 + 2 * per])
        ext[NEXT_Y, 6:8] = next_faces(ext[FACE_Y, 6:8], ghost_next[...])

    fields = [ext[field] for field in range(8)]
    fields[FACE_X] = jnp.concatenate([fields[FACE_X], last_face[...][None]], axis=0)
    once = euler(fields, ext[NEXT_Y])
    twice = euler(once, ahead(once[FACE_Y], 1))
    for field in range(8):
        lines[ROWS * field : ROWS * field + ROWS] = 0.5 * (ext[field, 2:6] + twice[field][:ROWS])

    def spread(k, carry):
        t = lax.rem(k + (gy + half) * per, LINES)
        slot = lax.rem(t, per)
        target = line_in.at[slot, pl.ds(pl.multiple_of(8 * gy, 8), 8), :]

        @pl.when(jnp.logical_not(first_x) | (lax.rem(t, ROWS) >= 2))
        def _():
            send(lines.at[t], target, 6, 6, partner, lax.div(t, per)).start()

        return carry

    @pl.when(jnp.logical_not(first_x))
    def _():
        pl.semaphore_wait(known.at[2], 4)

    lax.fori_loop(0, LINES, spread, 0)

    @pl.when(first_x)
    def _():
        pl.semaphore_wait(known.at[2], 4)

    @pl.when(first_x)
    def _():
        ghost_amount = lax.rem(total_cells - shear_ref[0], total_cells)
        for slot, u, faces in ghost_places:

            @pl.when(u <= STRIPS)
            def _(slot=slot):
                wait_bytes(line_ghost.at[slot, pl.ds(0, 8 * n_gy), :], recv_sems.at[16 + per + slot])
                line_ghost[slot, pl.ds(8 * n_gy, 8 * n_gy), :] = line_ghost[slot, pl.ds(0, 8 * n_gy), :]
                fill(4 * per + slot, line_ghost, slot, ghost_amount)

        pl.semaphore_wait(known.at[3], n_gy)
        for slot, u, faces in ghost_places:

            @pl.when(u < STRIPS)
            def _(slot=slot, u=u):
                hand(4 * per + slot, ext.at[lax.div(u, 2), 6 + lax.rem(u, 2)], 8, 4, last)

            @pl.when(faces)
            def _(slot=slot, u=u):
                row = lax.rem(u, 2)
                hand_next(4 * per + slot, lambda plane: ghost_next.at[2 * row + plane, pl.ds(0, 1)], 15, 17 + 2 * per, last)

            @pl.when(u == STRIPS)
            def _(slot=slot):
                hand(4 * per + slot, last_face, 8, 5, last)

    amounts.wait_recv()
    levels.wait_recv()

    @pl.when(gx == middle)
    def _():
        wait_bytes(line_own.at[:, pl.ds(0, 8 * n_gy), :], recv_sems.at[2])
        line_own[:, pl.ds(8 * n_gy, 8 * n_gy), :] = line_own[:, pl.ds(0, 8 * n_gy), :]
        for slot, field, row in places:

            def frame(r, carry, slot=slot, field=field, row=row):
                inner, faces, edge = own_conditions(r, field, row)
                page = r * per + slot

                @pl.when(jnp.logical_or(inner, edge))
                def _():
                    fill(page, line_own, slot, remap_ref[r])

                @pl.when(inner)
                def _():
                    hand(page, framed.at[r, field, row + 2 - r], 9, 11 + r, 0)

                @pl.when(edge)
                def _():
                    hand(page, framed_face.at[0], 9, 13, 0)

                @pl.when(faces)
                def _():
                    start = 2 * (row + 2 - r)
                    hand_next(page, lambda plane: framed_next.at[r, start + plane, pl.ds(0, 1)], 15, 18 + 2 * per + r, 0)

                return carry

            lax.fori_loop(0, 2, frame, 0)

        @pl.when(gy == spare)
        def _():
            wait_bytes(line_face.at[0, pl.ds(0, 8 * n_gy), :], recv_sems.at[16 + 2 * per])
            line_face[0, pl.ds(8 * n_gy, 8 * n_gy), :] = line_face[0, pl.ds(0, 8 * n_gy), :]
            fill(5 * per, line_face, 0, remap_ref[1])
            hand(5 * per, framed_face.at[1], 9, 14, 0)

        for slot, field, row in places:

            @pl.when(row >= 2)
            def _(slot=slot, field=field, row=row):
                wait_bytes(line_far.at[slot, pl.ds(0, 8 * n_gy), :], recv_sems.at[16 + slot])
                line_far[slot, pl.ds(8 * n_gy, 8 * n_gy), :] = line_far[slot, pl.ds(0, 8 * n_gy), :]

                def frame(r, carry):
                    inner, faces = far_conditions(r, field, row)
                    page = (2 + r) * per + slot
                    amount = lax.rem(remap_ref[r] + shear_ref[0], total_cells)

                    @pl.when(inner)
                    def _():
                        fill(page, line_far, slot, amount)
                        hand(page, framed.at[r, field, row - 2 - r], 9, 11 + r, 0)

                    @pl.when(faces)
                    def _():
                        start = 2 * (row - 2 - r)
                        hand_next(page, lambda plane: framed_next.at[r, start + plane, pl.ds(0, 1)], 15, 18 + 2 * per + r, 0)

                    return carry

                lax.fori_loop(0, 2, frame, 0)


    expected = [jnp.logical_or(gx != middle, row >= 2) for _, _, row in places]
    for slot in range(per):

        @pl.when(expected[slot])
        def _(slot=slot):
            wait_bytes(line_in.at[slot, pl.ds(0, 8 * n_gy), :], recv_sems.at[6])

    for slot in range(per):

        @pl.when(expected[slot])
        def _(slot=slot):
            row = lax.rem(gy * per + slot, ROWS)
            line_in[slot, pl.ds(8 * n_gy, 8 * n_gy), :] = line_in[slot, pl.ds(0, 8 * n_gy), :]
            tiles = window(line_in, slot, n_gy, cells, remap_ref[row], 2)
            weight = (frac_ref[row].astype(jnp.float32) + 0.5) / FRAC
            line_out[slot] = (1.0 - weight) * ahead(tiles, 2) + weight * ahead(tiles, 1)
            target = raw.at[pl.ds(pl.multiple_of(8 * (gy * per + slot), 8), 8), :]
            everyone(lambda y: send(line_out.at[slot, y], target, 7, 7, partner, y).start())

    next_copy = send(to_next, from_previous, 12, 15, 0, right_y)

    @pl.when(first_x)
    def _():
        for r in range(2):
            wait_bytes(framed.at[r], recv_sems.at[11 + r])
            wait_bytes(framed_face.at[r], recv_sems.at[13 + r])
            fields = [framed[r, field] for field in range(8)]
            fields[FACE_X] = jnp.concatenate([fields[FACE_X], framed_face[r][None]], axis=0)
            wait_bytes(framed_next.at[r, :, pl.ds(0, 1)], recv_sems.at[18 + 2 * per + r])
            once = euler(fields, next_faces(fields[FACE_Y], framed_next[r]))
            twice = euler(once, ahead(once[FACE_Y], 1))
            for field in range(8):
                fresh[pl.ds(64 * r + 8 * field, 8), :] = 0.5 * (framed[r, field, 2] + twice[field][0])
        to_next[...] = fresh[pl.ds(3, 32, stride=4), :]
        next_copy.start()
        next_copy.wait_recv()
        reach = cells % 128 + 1
        fresh_edges[pl.ds(0, 32, stride=4), :] = pltpu.roll(from_previous[...], 129 - reach, 1)

    @pl.when(jnp.logical_not(first_x))
    def _():
        wait_bytes(raw, recv_sems.at[7])

    @pl.when(first_x)
    def _():
        wait_bytes(raw.at[pl.ds(0, 4 * LINES)], recv_sems.at[7])
        tiles = fresh[...].reshape(16, 8, 128)
        lanes = lax.broadcasted_iota(jnp.int32, tiles.shape, 2)
        chunks = lax.broadcasted_iota(jnp.int32, tiles.shape, 1) % 4
        tiles = jnp.where((chunks == 0) & (lanes == 1), fresh_edges[...].reshape(16, 8, 128), tiles)
        here, there = ahead(tiles, 2), ahead(tiles, 1)
        for r in range(2):
            weight = (frac_own[r].astype(jnp.float32) + 0.5) / FRAC
            mixed = (1.0 - weight) * here[8 * r : 8 * r + 8] + weight * there[8 * r : 8 * r + 8]
            for field in range(8):
                raw[pl.ds(32 * field + 8 * r, 8), :] = mixed[field]

    for field in range(8):
        for plane in range(2):
            for chunk in range(4):
                part = raw[pl.ds(field * 32 + plane * 4 + chunk, ROWS, stride=8), :]
                width = min(128, cells - 128 * chunk)
                out_ref[field, plane, :, pl.ds(128 * chunk, width)] = part[:, :width]

    for copy in (strip_left, strip_right, amounts, levels):
        copy.wait_send()

    @pl.when(gx == 1)
    def _():
        near_copy.wait_send()

    @pl.when(jnp.logical_not(last_x))
    def _():
        to_up.wait_send()

    @pl.when(jnp.logical_not(first_x))
    def _():
        to_down.wait_send()
        to_down_face.wait_send()

    @pl.when(last_x)
    def _():
        wait_bytes(held.at[pl.ds(0, STRIPS)], send_sems.at[2])

    def left(condition, page, sem):
        @pl.when(condition)
        def _():
            wait_bytes(pages.at[page], send_sems.at[sem])

    def left_next(condition):
        @pl.when(condition)
        def _():
            wait_bytes(pages.at[0, pl.ds(0, n_gy // 4)], send_sems.at[15])

    @pl.when(first_x)
    def _():
        wait_bytes(held, send_sems.at[2])
        wait_bytes(near_face, send_sems.at[13])
        next_copy.wait_send()
        count_own = sum((u <= STRIPS).astype(jnp.int32) for _, u, _ in ghost_places)
        for count in range(len(ghost_places) + 1):

            @pl.when(count_own == count)
            def _(count=count):
                wait_bytes(held.at[pl.ds(0, STRIPS + 1 - count)], send_sems.at[14])

        for slot, u, faces in ghost_places:
            left(u <= STRIPS, 4 * per + slot, 8)
            left_next(faces)

    @pl.when(gx == middle)
    def _():
        @pl.when(gy == spare)
        def _():
            wait_bytes(pages.at[5 * per], send_sems.at[9])

        for slot, field, row in places:
            for r in range(2):
                inner, faces, edge = own_conditions(r, field, row)
                left(jnp.logical_or(inner, edge), r * per + slot, 9)
                left_next(faces)
                inner, faces = far_conditions(r, field, row)
                left(inner, (2 + r) * per + slot, 9)
                left_next(faces)

    @pl.when(first_x)
    def _():
        wait_bytes(lines.at[pl.ds(0, LINES // 2)], send_sems.at[6])

    @pl.when(jnp.logical_not(first_x))
    def _():
        wait_bytes(lines, send_sems.at[6])

    for slot in range(per):

        @pl.when(expected[slot])
        def _(slot=slot):
            wait_bytes(line_out.at[slot], send_sems.at[7])


def solution(mesh):
    n_gx = mesh.shape["gx"]
    n_gy = mesh.shape["gy"]

    def shards(state, shear_offset, remap_shift, frac_index):
        cells = state.shape[3]
        per = LINES // n_gy
        vmem = lambda *shape: pltpu.VMEM(shape, jnp.float32)
        large = pl.BlockSpec(memory_space=pltpu.VMEM)
        whole = pl.BlockSpec(memory_space=pl.ANY)
        return pl.pallas_call(
            functools.partial(kernel, n_gx, n_gy, cells),
            out_shape=jax.ShapeDtypeStruct(state.shape, jnp.float32),
            in_specs=[whole] * 4,
            out_specs=large,
            scratch_shapes=[
                pltpu.SMEM((1,), jnp.int32),
                pltpu.SMEM((ROWS,), jnp.int32),
                pltpu.SMEM((ROWS,), jnp.int32),
                pltpu.SMEM((ROWS,), jnp.int32),
                vmem(*state.shape),
                vmem(8 * LINES, 128),
                vmem(LINES, 8, 128),
                vmem(9, 8, 8, 128),
                vmem(8, 128),
                vmem(64, 128),
                vmem(64, 128),
                vmem(64, 128),
                vmem(64, 128),
                vmem(8 * LINES, 128),
                vmem(8 * ROWS, 128),
                vmem(per, 16 * n_gy, 128),
                vmem(per, 16 * n_gy, 128),
                vmem(per, 16 * n_gy, 128),
                vmem(1, 16 * n_gy, 128),
                vmem(8, 128),
                vmem(PAGES * per, n_gy, 8, 128),
                vmem(2, 8, 5, 8, 128),
                vmem(2, 10, 8, 128),
                vmem(4, 8, 128),
                vmem(2, 8, 128),
                vmem(128, 128),
                vmem(128, 128),
                vmem(32, 128),
                vmem(32, 128),
                vmem(per, 16 * n_gy, 128),
                vmem(per, n_gy, 8, 128),
                vmem(LINES, 8, 128),
                pltpu.SemaphoreType.DMA((16,)),
                pltpu.SemaphoreType.DMA((20 + 2 * per,)),
                pltpu.SemaphoreType.DMA((3,)),
                pltpu.SemaphoreType.REGULAR((5,)),
            ],
            compiler_params=pltpu.CompilerParams(collective_id=0, has_side_effects=True),
        )(shear_offset, remap_shift, frac_index, state)

    placed = (P(None, None, "gx", "gy"), P(), P("gx"), P("gx"))
    return jax.shard_map(shards, mesh=mesh, in_specs=placed, out_specs=P(None, None, "gx", "gy"), check_vma=False)
```

```python
import functools

import jax
import jax.numpy as jnp
from jax import lax
from jax.experimental import pallas as pl
from jax.experimental.pallas import tpu as pltpu
from jax.sharding import PartitionSpec as P

FRAC = 16
GAMMA_LESS = 5.0 / 3.0 - 1.0
ROTATION = 1.0
SHEAR_RATE = 1.5
MAX_SPEED = 5.0
TIME_STEP = 0.05

FACE_X, FACE_Y, FACE_Z, NEXT_Y = 5, 6, 7, 8
ROWS = 4
LINES = 8 * ROWS
STRIPS = 16
PAGES = 6
MESH = pl.DeviceIdType.MESH


def ahead(value, count):
    lane = lax.broadcasted_iota(jnp.int32, value.shape, 2)
    moved = pltpu.roll(value, 128 - count, 2)
    return jnp.where(lane >= 128 - count, pltpu.roll(moved, 7, 1), moved)


def behind(value, count):
    lane = lax.broadcasted_iota(jnp.int32, value.shape, 2)
    moved = pltpu.roll(value, count, 2)
    return jnp.where(lane < count, pltpu.roll(moved, 1, 1), moved)


def other_plane(value):
    return pltpu.roll(value, 4, 1)


def euler(fields, next_y):
    density, mom_x, mom_y, mom_z, energy, face_x, face_y, face_z = fields
    rows = density.shape[0]
    mid = slice(1, rows - 1)
    cen_x = 0.5 * (face_x[:-1] + face_x[1:])
    cen_y = 0.5 * (face_y + next_y)
    cen_z = 0.5 * (face_z + other_plane(face_z))
    inverse = 1.0 / density
    vel_x = mom_x * inverse
    vel_y = mom_y * inverse
    vel_z = mom_z * inverse
    magnetic = 0.5 * (cen_x * cen_x + cen_y * cen_y + cen_z * cen_z)
    pressure = (
        GAMMA_LESS * (energy - 0.5 * (mom_x * vel_x + mom_y * vel_y + mom_z * vel_z) - magnetic) + magnetic
    )
    vel_dot = vel_x * cen_x + vel_y * cen_y + vel_z * cen_z
    conserved = (density, mom_x, mom_y, mom_z, energy)
    momenta = (mom_x, mom_y, mom_z)
    centred = (cen_x, cen_y, cen_z)
    velocity = (vel_x, vel_y, vel_z)
    change = [None] * 5
    for normal in range(3):
        part = slice(None) if normal == 0 else mid
        speed = velocity[normal][part]
        across = centred[normal][part]
        fluxes = [momenta[normal][part]]
        for second in range(3):
            term = momenta[second][part] * speed - across * centred[second][part]
            if second == normal:
                term = term + pressure[part]
            fluxes.append(term)
        fluxes.append((energy[part] + pressure[part]) * speed - across * vel_dot[part])
        for member in range(5):
            flux = fluxes[member]
            held = conserved[member][part]
            if normal == 0:
                upwind = 0.5 * (flux[:-1] + flux[1:]) - 0.5 * MAX_SPEED * (held[1:] - held[:-1])
                delta = upwind[1:] - upwind[:-1]
            elif normal == 1:
                upwind = 0.5 * (behind(flux, 1) + flux) - 0.5 * MAX_SPEED * (held - behind(held, 1))
                delta = ahead(upwind, 1) - upwind
            else:
                upwind = 0.5 * (other_plane(flux) + flux) - 0.5 * MAX_SPEED * (held - other_plane(held))
                delta = other_plane(upwind) - upwind
            change[member] = -delta if change[member] is None else change[member] - delta
    change[1] = change[1] + 2.0 * ROTATION * mom_y[mid]
    change[2] = change[2] - (2.0 - SHEAR_RATE) * ROTATION * mom_x[mid]
    change[4] = change[4] + SHEAR_RATE * ROTATION * (mom_x[mid] * vel_y[mid] - cen_x[mid] * cen_y[mid])
    elec_x = -(vel_y * cen_z - vel_z * cen_y)
    elec_y = -(vel_z * cen_x - vel_x * cen_z)
    elec_z = -(vel_x * cen_y - vel_y * cen_x)
    pair_x = elec_x[mid] + behind(elec_x[mid], 1)
    edge_x = 0.25 * (pair_x + other_plane(pair_x))
    pair_y = elec_y[1:] + elec_y[:-1]
    edge_y = 0.25 * (pair_y + other_plane(pair_y))
    pair_z = elec_z[1:] + elec_z[:-1]
    edge_z = 0.25 * (pair_z + behind(pair_z, 1))
    delta_x = -(ahead(edge_z, 1) - edge_z - (other_plane(edge_y) - edge_y))
    delta_y = -(other_plane(edge_x) - edge_x - (edge_z[1:] - edge_z[:-1]))
    delta_z = -(edge_y[1:] - edge_y[:-1] - (ahead(edge_x, 1) - edge_x))
    done = [conserved[member][mid] + TIME_STEP * change[member] for member in range(5)]
    done.append(face_x[1:rows] + TIME_STEP * delta_x)
    done.append(face_y[mid] + TIME_STEP * delta_y)
    done.append(face_z[mid] + TIME_STEP * delta_z)
    return done


def window(ref, slot, blocks, cells, amount, kinds):
    hops = lax.div(amount, cells)
    rest = lax.rem(amount, cells)
    if kinds == 3:
        low = rest < 2
        hops = jnp.where(low, hops - 1, hops)
        rest = jnp.where(low, rest + cells, rest)
    total = blocks * 8
    lane = lax.broadcasted_iota(jnp.int32, (blocks, 8, 128), 2)
    chunk = lax.broadcasted_iota(jnp.int32, (blocks, 8, 128), 1) % 4
    place = chunk * 128 + lane - 2 - rest
    result = None
    for kind in reversed(range(kinds)):
        distance = rest - kind * cells + 1024
        lanes = lax.rem(distance, 128)
        sublanes = lax.div(distance, 128) - 8
        back = lax.rem(8 * (hops + kind) + sublanes + total, total)
        near = ref[slot, pl.ds(total - back, total), :].reshape(blocks, 8, 128)
        far = ref[slot, pl.ds(total - back - 1, total), :].reshape(blocks, 8, 128)
        near = pltpu.roll(near, lanes, 2)
        far = pltpu.roll(far, lanes, 2)
        moved = jnp.where(lane >= lanes, near, far)
        if result is None:
            result = moved
        else:
            result = jnp.where(place >= -kind * cells, moved, result)
    return result


def kernel(
    n_gx,
    n_gy,
    cells,
    shear_hbm,
    remap_hbm,
    frac_hbm,
    state_hbm,
    out_ref,
    shear_ref,
    remap_ref,
    frac_ref,
    remap_own,
    frac_own,
    state_ref,
    raw,
    held,
    ext,
    last_face,
    to_left,
    to_right,
    from_left,
    from_right,
    edges,
    next_edges,
    line_ghost,
    line_own,
    line_far,
    line_face,
    near_face,
    pages,
    framed,
    framed_next,
    ghost_next,
    framed_face,
    fresh,
    fresh_edges,
    to_next,
    from_previous,
    line_in,
    line_out,
    lines,
    send_sems,
    recv_sems,
    load_sems,
    known,
):
    gx = lax.axis_index("gx")
    gy = lax.axis_index("gy")
    half = n_gy // 2
    per = LINES // n_gy
    left_y = lax.rem(gy + n_gy - 1, n_gy)
    right_y = lax.rem(gy + 1, n_gy)
    inside = lax.rem(gy, half)
    side = gy - inside
    core = gy + 1 - 2 * lax.rem(gy, 2)
    up, down, up_2, down_2 = (side + lax.rem(inside + half + step, half) for step in (2, -2, 4, -4))
    partner = lax.rem(gx + n_gx // 2, n_gx)
    middle = n_gx // 2
    last = n_gx - 1
    first_x = gx == 0
    last_x = gx == last
    barrier = pltpu.get_barrier_semaphore()
    load = pltpu.make_async_copy(state_hbm, state_ref, load_sems.at[0])
    load.start()
    small_loads = [
        pltpu.make_async_copy(source, target, load_sems.at[1 + k])
        for k, (source, target) in enumerate(
            ((shear_hbm, shear_ref), (remap_hbm, remap_own), (frac_hbm, frac_own))
        )
    ]
    for copy in small_loads:
        copy.start()

    def tell(sem, x, y):
        pl.semaphore_signal(sem, inc=1, device_id=(x, y), device_id_type=MESH)

    def everyone(body):
        def step(k, carry):
            body(lax.rem(k + gy, n_gy))
            return carry

        lax.fori_loop(0, n_gy, step, 0)

    def send(source, target, sent, arrived, x, y):
        return pltpu.make_async_remote_copy(
            src_ref=source,
            dst_ref=target,
            send_sem=send_sems.at[sent],
            recv_sem=recv_sems.at[arrived],
            device_id=(x, y),
            device_id_type=MESH,
        )

    def wait_bytes(ref, sem):
        pltpu.make_async_copy(ref, ref, sem).wait()

    @pl.when(first_x)
    def _():
        def step(k, carry):
            tell(barrier, 0, lax.rem(gy + k, n_gy))
            return carry

        lax.fori_loop(1, n_gy, step, 0)

    @pl.when(gx == middle)
    def _():
        everyone(lambda y: tell(barrier, 0, y))

    @pl.when(jnp.logical_not(first_x))
    def _():
        for y in (left_y, right_y, up, down):
            tell(barrier, gx, y)

    @pl.when(gx != middle)
    def _():
        for y in (gy, lax.rem(gy + half, n_gy)):
            tell(barrier, partner, y)

    @pl.when(jnp.logical_not(first_x))
    def _():
        tell(barrier, gx - 1, gy)

    @pl.when(jnp.logical_not(last_x))
    def _():
        tell(barrier, gx + 1, gy)

    @pl.when(first_x)
    def _():
        everyone(lambda y: tell(barrier, last, y))

    load.wait()
    whole = cells // 128
    for field in range(8):
        for plane in range(2):
            for chunk in range(4):
                if chunk < whole:
                    part = state_ref[field, plane, :, pl.ds(128 * chunk, 128)]
                else:
                    part = state_ref[field, plane, :, pl.ds(128 * whole, cells - 128 * whole)]
                    part = jnp.concatenate([part, jnp.zeros((ROWS, 128 * (whole + 1) - cells), jnp.float32)], axis=1)
                raw[pl.ds(field * 32 + plane * 4 + chunk, ROWS, stride=8), :] = part
    to_left[...] = raw[pl.ds(0, 64, stride=4), :]
    to_right[...] = raw[pl.ds(3, 64, stride=4), :]
    held[...] = behind(raw[...].reshape(LINES, 8, 128), 2)
    pl.semaphore_wait(barrier, jnp.where(last_x, 7 + n_gy, jnp.where(first_x, 2 * n_gy, 8)))

    @pl.when(jnp.logical_not(first_x))
    def _():
        for y in (core, up, down):
            tell(known.at[0], gx, y)


    def line_place(buffer, t):
        return buffer.at[lax.rem(t, per), pl.ds(pl.multiple_of(8 * gy, 8), 8), :]

    @pl.when(last_x)
    def _():
        def step(k, carry):
            u = lax.rem(k + lax.div(gy, 2), STRIPS)
            t = lax.div(u, 2) * ROWS + 2 + lax.rem(u, 2)
            send(held.at[t], line_place(line_far, t), 2, 16 + lax.rem(t, per), 0, lax.div(t, per)).start()
            return carry

        lax.fori_loop(0, STRIPS, step, 0)
        everyone(lambda y: tell(known.at[3], 0, y))

    near_copy = send(held.at[FACE_X * ROWS], near_face, 12, 8, 0, gy)
    strip_left = send(to_left, from_right, 0, 0, gx, left_y)
    strip_right = send(to_right, from_left, 1, 1, gx, right_y)
    strip_left.start()
    strip_right.start()

    @pl.when(gx == 1)
    def _():
        near_copy.start()

    amounts = send(remap_hbm, remap_ref, 10, 9, partner, gy)
    levels = send(frac_hbm, frac_ref, 11, 10, partner, gy)
    amounts.start()
    levels.start()
    @pl.when(jnp.logical_not(first_x))
    def _():
        pl.semaphore_wait(known.at[0], 3)
        if half > 4:
            for y in (up_2, down_2):
                tell(known.at[1], gx, y)
            pl.semaphore_wait(known.at[1], 2)

    for y in (gy, core):
        tell(known.at[2], partner, y)
        tell(known.at[2], partner, lax.rem(y + half, n_gy))

    @pl.when(first_x)
    def _():
        def ghosts(k, carry):
            u = lax.rem(k + lax.div(gy, 2), STRIPS + 1)
            rank = lax.rem(u, n_gy)
            slot = lax.div(u, n_gy)
            owner = jnp.where(rank < half, 2 * rank, 2 * (rank - half) + 1)
            tile = jnp.where(u == STRIPS, FACE_X * ROWS + 2, lax.div(u, 2) * ROWS + lax.rem(u, 2))
            target = line_ghost.at[slot, pl.ds(pl.multiple_of(8 * gy, 8), 8), :]
            arrived = 16 + per + slot

            @pl.when(owner != gy)
            def _():
                send(held.at[tile], target, 14, arrived, 0, owner).start()

            @pl.when(owner == gy)
            def _():
                pltpu.make_async_copy(held.at[tile], target, recv_sems.at[arrived]).start()

            return carry

        def whole(k, carry):
            t = lax.rem(k + (gy + half) * per, LINES)
            send(held.at[t], line_place(line_own, t), 2, 2, middle, lax.div(t, per)).start()
            return carry

        lax.fori_loop(0, LINES, whole, 0)
        lax.fori_loop(0, STRIPS + 1, ghosts, 0)
        near_copy.wait_recv()
        send(near_face, line_place(line_face, 0), 13, 16 + 2 * per, middle, n_gy - 1).start()

    strip_left.wait_recv()
    strip_right.wait_recv()
    lane = lax.broadcasted_iota(jnp.int32, (LINES, 8, 128), 2)
    chunk = lax.broadcasted_iota(jnp.int32, (LINES, 8, 128), 1) % 4
    beyond = cells % 128
    after = from_right[...]
    edges[pl.ds(0, 64, stride=4), :] = pltpu.roll(from_left[...], 130 - beyond, 1)
    edges[pl.ds(3, 64, stride=4), :] = pltpu.roll(after, beyond + 2, 1)
    outside = jnp.logical_or(
        jnp.logical_and(chunk == 0, lane < 2), jnp.logical_and(chunk == 3, lane >= beyond + 2)
    )
    full = jnp.where(outside, edges[...].reshape(LINES, 8, 128), held[...])
    for field in range(8):
        ext[field, 2:6] = full[ROWS * field : ROWS * field + ROWS]
    next_edges[pl.ds(3, 2 * ROWS, stride=4), :] = pltpu.roll(after[2 * ROWS * FACE_Y : 2 * ROWS * (FACE_Y + 1)], beyond + 1, 1)
    final = jnp.logical_and(chunk == 3, lane == 127)[:ROWS]
    ext[NEXT_Y, 2:6] = jnp.where(
        final, next_edges[...].reshape(ROWS, 8, 128), ahead(full[ROWS * FACE_Y : ROWS * (FACE_Y + 1)], 1)
    )

    to_up = send(ext.at[:, pl.ds(4, 2)], ext.at[:, pl.ds(0, 2)], 3, 3, gx + 1, gy)
    to_down = send(ext.at[:, pl.ds(2, 2)], ext.at[:, pl.ds(6, 2)], 4, 4, gx - 1, gy)
    to_down_face = send(ext.at[FACE_X, 4], last_face, 5, 5, gx - 1, gy)

    @pl.when(jnp.logical_not(last_x))
    def _():
        to_up.start()

    @pl.when(jnp.logical_not(first_x))
    def _():
        to_down.start()
        to_down_face.start()

    for copy in small_loads:
        copy.wait()

    total_cells = cells * n_gy
    spare = n_gy - 1

    def fill(page, buffer, slot, amount):
        pages[page] = window(buffer, slot, n_gy, cells, amount, 3)

    def deliver(source, target, sem, arrived, x, y):
        if x == "self":

            @pl.when(y != gy)
            def _():
                send(source, target, sem, arrived, 0, y).start()

            @pl.when(y == gy)
            def _():
                pltpu.make_async_copy(source, target, recv_sems.at[arrived]).start()

        else:
            send(source, target, sem, arrived, x, y).start()

    def hand(page, target, sem, arrived, x):
        everyone(lambda y: deliver(pages.at[page, y], target, sem, arrived, x, y))

    def hand_next(page, target, sem, arrived, x):
        def one(y):
            following = lax.rem(y + 1, n_gy)
            for plane in range(2):
                source = pages.at[page, following, pl.ds(4 * plane, 1)]
                deliver(source, target(plane), sem, arrived, x, y)

        everyone(one)

    def next_faces(faces, rows):
        shape = faces.shape
        lanes = lax.broadcasted_iota(jnp.int32, shape, 2)
        places = lax.broadcasted_iota(jnp.int32, shape, 1)
        follow = pltpu.roll(jnp.broadcast_to(rows[:, 0:1, :], (2 * shape[0], 8, 128)), 123, 2)
        follow = follow.reshape(shape[0], 2, 8, 128)
        chosen = jnp.where(places < 4, follow[:, 0], follow[:, 1])
        return jnp.where((places % 4 == 3) & (lanes == 127), chosen, ahead(faces, 1))

    def wait_left():
        wait_bytes(ext.at[:, pl.ds(0, 2)], recv_sems.at[3])

    def wait_right():
        wait_bytes(ext.at[:, pl.ds(6, 2)], recv_sems.at[4])
        wait_bytes(last_face, recv_sems.at[5])

    places = []
    for slot in range(per):
        t = gy * per + slot
        places.append((slot, lax.div(t, ROWS), lax.rem(t, ROWS)))

    def own_conditions(r, field, row):
        inner = row < 3 + r
        return inner, jnp.logical_and(inner, field == FACE_Y), (row == 3) & (field == FACE_X) & (r == 0)

    def far_conditions(r, field, row):
        inner = row >= 2 + r
        return inner, jnp.logical_and(inner, field == FACE_Y)

    mine = jnp.where(lax.rem(gy, 2) == 0, lax.div(gy, 2), half + lax.div(gy, 2))
    ghost_places = []
    for slot in range(-(-(STRIPS + 1) // n_gy)):
        u = slot * n_gy + mine
        ghost_places.append((slot, u, lax.div(u, 2) == FACE_Y))

    @pl.when(first_x)
    def _():
        wait_right()
        ext[:, 0:2] = ext[:, 2:4]

    @pl.when(jnp.logical_not(first_x))
    def _():
        wait_left()

    @pl.when(jnp.logical_not(jnp.logical_or(first_x, last_x)))
    def _():
        wait_right()

    @pl.when(last_x)
    def _():
        wait_bytes(ext.at[pl.ds(0, 8), pl.ds(6, 2)], recv_sems.at[4])
        wait_bytes(last_face, recv_sems.at[5])
        wait_bytes(ghost_next.at[:, pl.ds(0, 1)], recv_sems.at[17 + 2 * per])
        ext[NEXT_Y, 6:8] = next_faces(ext[FACE_Y, 6:8], ghost_next[...])

    fields = [ext[field] for field in range(8)]
    fields[FACE_X] = jnp.concatenate([fields[FACE_X], last_face[...][None]], axis=0)
    once = euler(fields, ext[NEXT_Y])
    twice = euler(once, ahead(once[FACE_Y], 1))
    for field in range(8):
        lines[ROWS * field : ROWS * field + ROWS] = 0.5 * (ext[field, 2:6] + twice[field][:ROWS])

    def spread(k, carry):
        t = lax.rem(k + (gy + half) * per, LINES)
        slot = lax.rem(t, per)
        target = line_in.at[slot, pl.ds(pl.multiple_of(8 * gy, 8), 8), :]

        @pl.when(jnp.logical_not(first_x) | (lax.rem(t, ROWS) >= 2))
        def _():
            send(lines.at[t], target, 6, 6, partner, lax.div(t, per)).start()

        return carry

    @pl.when(jnp.logical_not(first_x))
    def _():
        pl.semaphore_wait(known.at[2], 4)

    lax.fori_loop(0, LINES, spread, 0)

    @pl.when(first_x)
    def _():
        pl.semaphore_wait(known.at[2], 4)

    @pl.when(first_x)
    def _():
        ghost_amount = lax.rem(total_cells - shear_ref[0], total_cells)
        for slot, u, faces in ghost_places:

            @pl.when(u <= STRIPS)
            def _(slot=slot):
                wait_bytes(line_ghost.at[slot, pl.ds(0, 8 * n_gy), :], recv_sems.at[16 + per + slot])
                line_ghost[slot, pl.ds(8 * n_gy, 8 * n_gy), :] = line_ghost[slot, pl.ds(0, 8 * n_gy), :]
                fill(4 * per + slot, line_ghost, slot, ghost_amount)

        pl.semaphore_wait(known.at[3], n_gy)
        for slot, u, faces in ghost_places:

            @pl.when(u < STRIPS)
            def _(slot=slot, u=u):
                hand(4 * per + slot, ext.at[lax.div(u, 2), 6 + lax.rem(u, 2)], 8, 4, last)

            @pl.when(faces)
            def _(slot=slot, u=u):
                row = lax.rem(u, 2)
                hand_next(4 * per + slot, lambda plane: ghost_next.at[2 * row + plane, pl.ds(0, 1)], 15, 17 + 2 * per, last)

            @pl.when(u == STRIPS)
            def _(slot=slot):
                hand(4 * per + slot, last_face, 8, 5, last)

        for slot, field, row in places:

            @pl.when(row >= 2)
            def _(slot=slot, field=field, row=row):
                wait_bytes(line_far.at[slot, pl.ds(0, 8 * n_gy), :], recv_sems.at[16 + slot])
                line_far[slot, pl.ds(8 * n_gy, 8 * n_gy), :] = line_far[slot, pl.ds(0, 8 * n_gy), :]

                def frame(r, carry):
                    inner, faces = far_conditions(r, field, row)
                    page = (2 + r) * per + slot
                    amount = lax.rem(remap_own[r] + shear_ref[0], total_cells)

                    @pl.when(inner)
                    def _():
                        fill(page, line_far, slot, amount)
                        hand(page, framed.at[r, field, row - 2 - r], 9, 11 + r, "self")

                    @pl.when(faces)
                    def _():
                        start = 2 * (row - 2 - r)
                        hand_next(page, lambda plane: framed_next.at[r, start + plane, pl.ds(0, 1)], 15, 18 + 2 * per + r, "self")

                    return carry

                lax.fori_loop(0, 2, frame, 0)

    amounts.wait_recv()
    levels.wait_recv()

    @pl.when(gx == middle)
    def _():
        wait_bytes(line_own.at[:, pl.ds(0, 8 * n_gy), :], recv_sems.at[2])
        line_own[:, pl.ds(8 * n_gy, 8 * n_gy), :] = line_own[:, pl.ds(0, 8 * n_gy), :]
        for slot, field, row in places:

            def frame(r, carry, slot=slot, field=field, row=row):
                inner, faces, edge = own_conditions(r, field, row)
                page = r * per + slot

                @pl.when(jnp.logical_or(inner, edge))
                def _():
                    fill(page, line_own, slot, remap_ref[r])

                @pl.when(inner)
                def _():
                    hand(page, framed.at[r, field, row + 2 - r], 9, 11 + r, 0)

                @pl.when(edge)
                def _():
                    hand(page, framed_face.at[0], 9, 13, 0)

                @pl.when(faces)
                def _():
                    start = 2 * (row + 2 - r)
                    hand_next(page, lambda plane: framed_next.at[r, start + plane, pl.ds(0, 1)], 15, 18 + 2 * per + r, 0)

                return carry

            lax.fori_loop(0, 2, frame, 0)

        @pl.when(gy == spare)
        def _():
            wait_bytes(line_face.at[0, pl.ds(0, 8 * n_gy), :], recv_sems.at[16 + 2 * per])
            line_face[0, pl.ds(8 * n_gy, 8 * n_gy), :] = line_face[0, pl.ds(0, 8 * n_gy), :]
            fill(5 * per, line_face, 0, remap_ref[1])
            hand(5 * per, framed_face.at[1], 9, 14, 0)

    expected = [jnp.logical_or(gx != middle, row >= 2) for _, _, row in places]
    for slot in range(per):

        @pl.when(expected[slot])
        def _(slot=slot):
            wait_bytes(line_in.at[slot, pl.ds(0, 8 * n_gy), :], recv_sems.at[6])

    for slot in range(per):

        @pl.when(expected[slot])
        def _(slot=slot):
            row = lax.rem(gy * per + slot, ROWS)
            line_in[slot, pl.ds(8 * n_gy, 8 * n_gy), :] = line_in[slot, pl.ds(0, 8 * n_gy), :]
            tiles = window(line_in, slot, n_gy, cells, remap_ref[row], 2)
            weight = (frac_ref[row].astype(jnp.float32) + 0.5) / FRAC
            line_out[slot] = (1.0 - weight) * ahead(tiles, 2) + weight * ahead(tiles, 1)
            target = raw.at[pl.ds(pl.multiple_of(8 * (gy * per + slot), 8), 8), :]
            everyone(lambda y: send(line_out.at[slot, y], target, 7, 7, partner, y).start())

    next_copy = send(to_next, from_previous, 12, 15, 0, right_y)

    @pl.when(first_x)
    def _():
        for r in range(2):
            wait_bytes(framed.at[r], recv_sems.at[11 + r])
            wait_bytes(framed_face.at[r], recv_sems.at[13 + r])
            fields = [framed[r, field] for field in range(8)]
            fields[FACE_X] = jnp.concatenate([fields[FACE_X], framed_face[r][None]], axis=0)
            wait_bytes(framed_next.at[r, :, pl.ds(0, 1)], recv_sems.at[18 + 2 * per + r])
            once = euler(fields, next_faces(fields[FACE_Y], framed_next[r]))
            twice = euler(once, ahead(once[FACE_Y], 1))
            for field in range(8):
                fresh[pl.ds(64 * r + 8 * field, 8), :] = 0.5 * (framed[r, field, 2] + twice[field][0])
        to_next[...] = fresh[pl.ds(3, 32, stride=4), :]
        next_copy.start()
        next_copy.wait_recv()
        reach = cells % 128 + 1
        fresh_edges[pl.ds(0, 32, stride=4), :] = pltpu.roll(from_previous[...], 129 - reach, 1)

    @pl.when(jnp.logical_not(first_x))
    def _():
        wait_bytes(raw, recv_sems.at[7])

    @pl.when(first_x)
    def _():
        wait_bytes(raw.at[pl.ds(0, 4 * LINES)], recv_sems.at[7])
        tiles = fresh[...].reshape(16, 8, 128)
        lanes = lax.broadcasted_iota(jnp.int32, tiles.shape, 2)
        chunks = lax.broadcasted_iota(jnp.int32, tiles.shape, 1) % 4
        tiles = jnp.where((chunks == 0) & (lanes == 1), fresh_edges[...].reshape(16, 8, 128), tiles)
        here, there = ahead(tiles, 2), ahead(tiles, 1)
        for r in range(2):
            weight = (frac_own[r].astype(jnp.float32) + 0.5) / FRAC
            mixed = (1.0 - weight) * here[8 * r : 8 * r + 8] + weight * there[8 * r : 8 * r + 8]
            for field in range(8):
                raw[pl.ds(32 * field + 8 * r, 8), :] = mixed[field]

    out_ref[...] = raw[...]

    for copy in (strip_left, strip_right, amounts, levels):
        copy.wait_send()

    @pl.when(gx == 1)
    def _():
        near_copy.wait_send()

    @pl.when(jnp.logical_not(last_x))
    def _():
        to_up.wait_send()

    @pl.when(jnp.logical_not(first_x))
    def _():
        to_down.wait_send()
        to_down_face.wait_send()

    @pl.when(last_x)
    def _():
        wait_bytes(held.at[pl.ds(0, STRIPS)], send_sems.at[2])

    def left(condition, page, sem):
        @pl.when(condition)
        def _():
            wait_bytes(pages.at[page], send_sems.at[sem])

    def left_next(condition, one_less=0):
        @pl.when(condition)
        def _():
            wait_bytes(pages.at[pl.ds(0, 2), pl.ds(0, n_gy - one_less), pl.ds(0, 1)], send_sems.at[15])

    @pl.when(first_x)
    def _():
        wait_bytes(held, send_sems.at[2])
        wait_bytes(near_face, send_sems.at[13])
        next_copy.wait_send()
        count_own = sum((u <= STRIPS).astype(jnp.int32) for _, u, _ in ghost_places)
        for count in range(len(ghost_places) + 1):

            @pl.when(count_own == count)
            def _(count=count):
                wait_bytes(held.at[pl.ds(0, STRIPS + 1 - count)], send_sems.at[14])

        for slot, u, faces in ghost_places:
            left(u <= STRIPS, 4 * per + slot, 8)
            left_next(faces)

        for slot, field, row in places:
            for r in range(2):
                inner, faces = far_conditions(r, field, row)
                left_next(faces, 1)

                @pl.when(inner)
                def _(slot=slot, r=r):
                    wait_bytes(pages.at[(2 + r) * per + slot, pl.ds(0, n_gy - 1)], send_sems.at[9])


    @pl.when(gx == middle)
    def _():
        @pl.when(gy == spare)
        def _():
            wait_bytes(pages.at[5 * per], send_sems.at[9])

        for slot, field, row in places:
            for r in range(2):
                inner, faces, edge = own_conditions(r, field, row)
                left(jnp.logical_or(inner, edge), r * per + slot, 9)
                left_next(faces)

    @pl.when(first_x)
    def _():
        wait_bytes(lines.at[pl.ds(0, LINES // 2)], send_sems.at[6])

    @pl.when(jnp.logical_not(first_x))
    def _():
        wait_bytes(lines, send_sems.at[6])

    for slot in range(per):

        @pl.when(expected[slot])
        def _(slot=slot):
            wait_bytes(line_out.at[slot], send_sems.at[7])


def unpack(tiles_ref, out_ref):
    cells = out_ref.shape[3]
    for field in range(8):
        for plane in range(2):
            for chunk in range(4):
                part = tiles_ref[pl.ds(field * 32 + plane * 4 + chunk, ROWS, stride=8), :]
                width = min(128, cells - 128 * chunk)
                out_ref[field, plane, :, pl.ds(128 * chunk, width)] = part[:, :width]


def solution(mesh):
    n_gx = mesh.shape["gx"]
    n_gy = mesh.shape["gy"]

    def shards(state, shear_offset, remap_shift, frac_index):
        cells = state.shape[3]
        per = LINES // n_gy
        vmem = lambda *shape: pltpu.VMEM(shape, jnp.float32)
        large = pl.BlockSpec(memory_space=pltpu.VMEM)
        whole = pl.BlockSpec(memory_space=pltpu.HBM)
        tiles = pl.pallas_call(
            functools.partial(kernel, n_gx, n_gy, cells),
            out_shape=pltpu.VMEM((8 * LINES, 128), jnp.float32),
            in_specs=[whole] * 4,
            out_specs=large,
            scratch_shapes=[
                pltpu.SMEM((1,), jnp.int32),
                pltpu.SMEM((ROWS,), jnp.int32),
                pltpu.SMEM((ROWS,), jnp.int32),
                pltpu.SMEM((ROWS,), jnp.int32),
                pltpu.SMEM((ROWS,), jnp.int32),
                vmem(*state.shape),
                vmem(8 * LINES, 128),
                vmem(LINES, 8, 128),
                vmem(9, 8, 8, 128),
                vmem(8, 128),
                vmem(64, 128),
                vmem(64, 128),
                vmem(64, 128),
                vmem(64, 128),
                vmem(8 * LINES, 128),
                vmem(8 * ROWS, 128),
                vmem(per, 16 * n_gy, 128),
                vmem(per, 16 * n_gy, 128),
                vmem(per, 16 * n_gy, 128),
                vmem(1, 16 * n_gy, 128),
                vmem(8, 128),
                vmem(PAGES * per, n_gy, 8, 128),
                vmem(2, 8, 5, 8, 128),
                vmem(2, 10, 8, 128),
                vmem(4, 8, 128),
                vmem(2, 8, 128),
                vmem(128, 128),
                vmem(128, 128),
                vmem(32, 128),
                vmem(32, 128),
                vmem(per, 16 * n_gy, 128),
                vmem(per, n_gy, 8, 128),
                vmem(LINES, 8, 128),
                pltpu.SemaphoreType.DMA((16,)),
                pltpu.SemaphoreType.DMA((20 + 2 * per,)),
                pltpu.SemaphoreType.DMA((4,)),
                pltpu.SemaphoreType.REGULAR((4,)),
            ],
            compiler_params=pltpu.CompilerParams(
                collective_id=0, has_side_effects=True
            ),
        )(shear_offset, remap_shift, frac_index, state)
        return pl.pallas_call(
            unpack,
            out_shape=jax.ShapeDtypeStruct(state.shape, jnp.float32),
            in_specs=[large],
            out_specs=large,
            compiler_params=pltpu.CompilerParams(vmem_limit_bytes=8 * 2**20),
        )(tiles)

    placed = (P(None, None, "gx", "gy"), P(), P("gx"), P("gx"))
    return jax.shard_map(shards, mesh=mesh, in_specs=placed, out_specs=P(None, None, "gx", "gy"), check_vma=False)
```

```python
import functools

import jax
import jax.numpy as jnp
from jax import lax
from jax.experimental import pallas as pl
from jax.experimental.pallas import tpu as pltpu
from jax.sharding import PartitionSpec as P

FRAC = 16
GAMMA_LESS = 5.0 / 3.0 - 1.0
ROTATION = 1.0
SHEAR_RATE = 1.5
MAX_SPEED = 5.0
TIME_STEP = 0.05

FACE_X, FACE_Y, FACE_Z, NEXT_Y = 5, 6, 7, 8
ROWS = 4
LINES = 8 * ROWS
STRIPS = 16
PAGES = 6
MESH = pl.DeviceIdType.MESH


def ahead(value, count):
    lane = lax.broadcasted_iota(jnp.int32, value.shape, 2)
    moved = pltpu.roll(value, 128 - count, 2)
    return jnp.where(lane >= 128 - count, pltpu.roll(moved, 7, 1), moved)


def behind(value, count):
    lane = lax.broadcasted_iota(jnp.int32, value.shape, 2)
    moved = pltpu.roll(value, count, 2)
    return jnp.where(lane < count, pltpu.roll(moved, 1, 1), moved)


def other_plane(value):
    return pltpu.roll(value, 4, 1)


def euler(fields, next_y):
    density, mom_x, mom_y, mom_z, energy, face_x, face_y, face_z = fields
    rows = density.shape[0]
    mid = slice(1, rows - 1)
    cen_x = 0.5 * (face_x[:-1] + face_x[1:])
    cen_y = 0.5 * (face_y + next_y)
    cen_z = 0.5 * (face_z + other_plane(face_z))
    inverse = 1.0 / density
    vel_x = mom_x * inverse
    vel_y = mom_y * inverse
    vel_z = mom_z * inverse
    magnetic = 0.5 * (cen_x * cen_x + cen_y * cen_y + cen_z * cen_z)
    pressure = (
        GAMMA_LESS * (energy - 0.5 * (mom_x * vel_x + mom_y * vel_y + mom_z * vel_z) - magnetic) + magnetic
    )
    vel_dot = vel_x * cen_x + vel_y * cen_y + vel_z * cen_z
    conserved = (density, mom_x, mom_y, mom_z, energy)
    momenta = (mom_x, mom_y, mom_z)
    centred = (cen_x, cen_y, cen_z)
    velocity = (vel_x, vel_y, vel_z)
    change = [None] * 5
    for normal in range(3):
        part = slice(None) if normal == 0 else mid
        speed = velocity[normal][part]
        across = centred[normal][part]
        fluxes = [momenta[normal][part]]
        for second in range(3):
            term = momenta[second][part] * speed - across * centred[second][part]
            if second == normal:
                term = term + pressure[part]
            fluxes.append(term)
        fluxes.append((energy[part] + pressure[part]) * speed - across * vel_dot[part])
        for member in range(5):
            flux = fluxes[member]
            held = conserved[member][part]
            if normal == 0:
                upwind = 0.5 * (flux[:-1] + flux[1:]) - 0.5 * MAX_SPEED * (held[1:] - held[:-1])
                delta = upwind[1:] - upwind[:-1]
            elif normal == 1:
                upwind = 0.5 * (behind(flux, 1) + flux) - 0.5 * MAX_SPEED * (held - behind(held, 1))
                delta = ahead(upwind, 1) - upwind
            else:
                upwind = 0.5 * (other_plane(flux) + flux) - 0.5 * MAX_SPEED * (held - other_plane(held))
                delta = other_plane(upwind) - upwind
            change[member] = -delta if change[member] is None else change[member] - delta
    change[1] = change[1] + 2.0 * ROTATION * mom_y[mid]
    change[2] = change[2] - (2.0 - SHEAR_RATE) * ROTATION * mom_x[mid]
    change[4] = change[4] + SHEAR_RATE * ROTATION * (mom_x[mid] * vel_y[mid] - cen_x[mid] * cen_y[mid])
    elec_x = -(vel_y * cen_z - vel_z * cen_y)
    elec_y = -(vel_z * cen_x - vel_x * cen_z)
    elec_z = -(vel_x * cen_y - vel_y * cen_x)
    pair_x = elec_x[mid] + behind(elec_x[mid], 1)
    edge_x = 0.25 * (pair_x + other_plane(pair_x))
    pair_y = elec_y[1:] + elec_y[:-1]
    edge_y = 0.25 * (pair_y + other_plane(pair_y))
    pair_z = elec_z[1:] + elec_z[:-1]
    edge_z = 0.25 * (pair_z + behind(pair_z, 1))
    delta_x = -(ahead(edge_z, 1) - edge_z - (other_plane(edge_y) - edge_y))
    delta_y = -(other_plane(edge_x) - edge_x - (edge_z[1:] - edge_z[:-1]))
    delta_z = -(edge_y[1:] - edge_y[:-1] - (ahead(edge_x, 1) - edge_x))
    done = [conserved[member][mid] + TIME_STEP * change[member] for member in range(5)]
    done.append(face_x[1:rows] + TIME_STEP * delta_x)
    done.append(face_y[mid] + TIME_STEP * delta_y)
    done.append(face_z[mid] + TIME_STEP * delta_z)
    return done


def window(ref, slot, blocks, cells, amount, kinds):
    hops = lax.div(amount, cells)
    rest = lax.rem(amount, cells)
    if kinds == 3:
        low = rest < 2
        hops = jnp.where(low, hops - 1, hops)
        rest = jnp.where(low, rest + cells, rest)
    total = blocks * 8
    lane = lax.broadcasted_iota(jnp.int32, (blocks, 8, 128), 2)
    chunk = lax.broadcasted_iota(jnp.int32, (blocks, 8, 128), 1) % 4
    place = chunk * 128 + lane - 2 - rest
    result = None
    for kind in reversed(range(kinds)):
        distance = rest - kind * cells + 1024
        lanes = lax.rem(distance, 128)
        sublanes = lax.div(distance, 128) - 8
        back = lax.rem(8 * (hops + kind) + sublanes + total, total)
        near = ref[slot, pl.ds(total - back, total), :].reshape(blocks, 8, 128)
        far = ref[slot, pl.ds(total - back - 1, total), :].reshape(blocks, 8, 128)
        near = pltpu.roll(near, lanes, 2)
        far = pltpu.roll(far, lanes, 2)
        moved = jnp.where(lane >= lanes, near, far)
        if result is None:
            result = moved
        else:
            result = jnp.where(place >= -kind * cells, moved, result)
    return result


def kernel(
    n_gx,
    n_gy,
    cells,
    shear_hbm,
    remap_hbm,
    frac_hbm,
    state_hbm,
    out_ref,
    shear_ref,
    remap_ref,
    frac_ref,
    remap_own,
    frac_own,
    state_ref,
    raw,
    held,
    ext,
    last_face,
    to_left,
    to_right,
    from_left,
    from_right,
    edges,
    next_edges,
    line_ghost,
    line_own,
    line_far,
    line_face,
    near_face,
    pages,
    framed,
    framed_next,
    ghost_next,
    framed_face,
    prior,
    prior_face,
    fresh,
    fresh_edges,
    to_next,
    from_previous,
    line_in,
    line_out,
    lines,
    send_sems,
    recv_sems,
    load_sems,
    known,
):
    gx = lax.axis_index("gx")
    gy = lax.axis_index("gy")
    half = n_gy // 2
    per = LINES // n_gy
    left_y = lax.rem(gy + n_gy - 1, n_gy)
    right_y = lax.rem(gy + 1, n_gy)
    inside = lax.rem(gy, half)
    side = gy - inside
    core = gy + 1 - 2 * lax.rem(gy, 2)
    up, down, up_2, down_2 = (side + lax.rem(inside + half + step, half) for step in (2, -2, 4, -4))
    partner = lax.rem(gx + n_gx // 2, n_gx)
    middle = n_gx // 2
    last = n_gx - 1
    first_x = gx == 0
    last_x = gx == last
    barrier = pltpu.get_barrier_semaphore()
    load = pltpu.make_async_copy(state_hbm, state_ref, load_sems.at[0])
    load.start()
    small_loads = [
        pltpu.make_async_copy(source, target, load_sems.at[1 + k])
        for k, (source, target) in enumerate(
            ((shear_hbm, shear_ref), (remap_hbm, remap_own), (frac_hbm, frac_own))
        )
    ]
    for copy in small_loads:
        copy.start()

    def tell(sem, x, y):
        pl.semaphore_signal(sem, inc=1, device_id=(x, y), device_id_type=MESH)

    def everyone(body):
        def step(k, carry):
            body(lax.rem(k + gy, n_gy))
            return carry

        lax.fori_loop(0, n_gy, step, 0)

    def send(source, target, sent, arrived, x, y):
        return pltpu.make_async_remote_copy(
            src_ref=source,
            dst_ref=target,
            send_sem=send_sems.at[sent],
            recv_sem=recv_sems.at[arrived],
            device_id=(x, y),
            device_id_type=MESH,
        )

    def wait_bytes(ref, sem):
        pltpu.make_async_copy(ref, ref, sem).wait()

    @pl.when(first_x)
    def _():
        def step(k, carry):
            tell(barrier, 0, lax.rem(gy + k, n_gy))
            return carry

        lax.fori_loop(1, n_gy, step, 0)

    @pl.when(gx == middle)
    def _():
        everyone(lambda y: tell(barrier, 0, y))

    @pl.when(jnp.logical_not(first_x))
    def _():
        for y in (left_y, right_y, up, down):
            tell(barrier, gx, y)

    @pl.when(gx != middle)
    def _():
        for y in (gy, lax.rem(gy + half, n_gy)):
            tell(barrier, partner, y)

    @pl.when(jnp.logical_not(first_x))
    def _():
        tell(barrier, gx - 1, gy)

    @pl.when(jnp.logical_not(last_x))
    def _():
        tell(barrier, gx + 1, gy)

    @pl.when(first_x)
    def _():
        everyone(lambda y: tell(barrier, last, y))

    load.wait()
    whole = cells // 128
    for field in range(8):
        for plane in range(2):
            for chunk in range(4):
                if chunk < whole:
                    part = state_ref[field, plane, :, pl.ds(128 * chunk, 128)]
                else:
                    part = state_ref[field, plane, :, pl.ds(128 * whole, cells - 128 * whole)]
                    part = jnp.concatenate([part, jnp.zeros((ROWS, 128 * (whole + 1) - cells), jnp.float32)], axis=1)
                raw[pl.ds(field * 32 + plane * 4 + chunk, ROWS, stride=8), :] = part
    to_left[...] = raw[pl.ds(0, 64, stride=4), :]
    to_right[...] = raw[pl.ds(3, 64, stride=4), :]
    held[...] = behind(raw[...].reshape(LINES, 8, 128), 2)
    pl.semaphore_wait(barrier, jnp.where(last_x, 7 + n_gy, jnp.where(first_x, 2 * n_gy, 8)))

    @pl.when(jnp.logical_not(first_x))
    def _():
        for y in (core, up, down):
            tell(known.at[0], gx, y)


    def line_place(buffer, t):
        return buffer.at[lax.rem(t, per), pl.ds(pl.multiple_of(8 * gy, 8), 8), :]

    @pl.when(last_x)
    def _():
        def step(k, carry):
            u = lax.rem(k + lax.div(gy, 2), STRIPS)
            t = lax.div(u, 2) * ROWS + 2 + lax.rem(u, 2)
            send(held.at[t], line_place(line_far, t), 2, 16 + lax.rem(t, per), 0, lax.div(t, per)).start()
            return carry

        lax.fori_loop(0, STRIPS, step, 0)
        everyone(lambda y: tell(known.at[3], 0, y))

    near_copy = send(held.at[FACE_X * ROWS], near_face, 12, 8, 0, gy)
    strip_left = send(to_left, from_right, 0, 0, gx, left_y)
    strip_right = send(to_right, from_left, 1, 1, gx, right_y)
    strip_left.start()
    strip_right.start()

    @pl.when(gx == 1)
    def _():
        near_copy.start()

    amounts = send(remap_hbm, remap_ref, 10, 9, partner, gy)
    levels = send(frac_hbm, frac_ref, 11, 10, partner, gy)
    amounts.start()
    levels.start()
    @pl.when(jnp.logical_not(first_x))
    def _():
        pl.semaphore_wait(known.at[0], 3)
        if half > 4:
            for y in (up_2, down_2):
                tell(known.at[1], gx, y)
            pl.semaphore_wait(known.at[1], 2)

    for y in (gy, core):
        tell(known.at[2], partner, y)
        tell(known.at[2], partner, lax.rem(y + half, n_gy))

    @pl.when(first_x)
    def _():
        def ghosts(k, carry):
            u = lax.rem(k + lax.div(gy, 2), STRIPS + 1)
            rank = lax.rem(u, n_gy)
            slot = lax.div(u, n_gy)
            owner = jnp.where(rank < half, 2 * rank, 2 * (rank - half) + 1)
            tile = jnp.where(u == STRIPS, FACE_X * ROWS + 2, lax.div(u, 2) * ROWS + lax.rem(u, 2))
            target = line_ghost.at[slot, pl.ds(pl.multiple_of(8 * gy, 8), 8), :]
            arrived = 16 + per + slot

            @pl.when(owner != gy)
            def _():
                send(held.at[tile], target, 14, arrived, 0, owner).start()

            @pl.when(owner == gy)
            def _():
                pltpu.make_async_copy(held.at[tile], target, recv_sems.at[arrived]).start()

            return carry

        def whole(k, carry):
            t = lax.rem(k + (gy + half) * per, LINES)
            owner = lax.div(t, per)
            stays = lax.rem(t, ROWS) < 2

            @pl.when(jnp.logical_not(stays & (owner == gy)))
            def _():
                send(held.at[t], line_place(line_own, t), 2, 2, jnp.where(stays, 0, middle), owner).start()

            @pl.when(stays & (owner == gy))
            def _():
                pltpu.make_async_copy(held.at[t], line_place(line_own, t), recv_sems.at[2]).start()

            return carry

        lax.fori_loop(0, STRIPS + 1, ghosts, 0)
        lax.fori_loop(0, LINES, whole, 0)
        near_copy.wait_recv()
        send(near_face, line_place(line_face, 0), 13, 16 + 2 * per, middle, n_gy - 1).start()

    strip_left.wait_recv()
    strip_right.wait_recv()
    lane = lax.broadcasted_iota(jnp.int32, (LINES, 8, 128), 2)
    chunk = lax.broadcasted_iota(jnp.int32, (LINES, 8, 128), 1) % 4
    beyond = cells % 128
    after = from_right[...]
    edges[pl.ds(0, 64, stride=4), :] = pltpu.roll(from_left[...], 130 - beyond, 1)
    edges[pl.ds(3, 64, stride=4), :] = pltpu.roll(after, beyond + 2, 1)
    outside = jnp.logical_or(
        jnp.logical_and(chunk == 0, lane < 2), jnp.logical_and(chunk == 3, lane >= beyond + 2)
    )
    full = jnp.where(outside, edges[...].reshape(LINES, 8, 128), held[...])
    for field in range(8):
        ext[field, 2:6] = full[ROWS * field : ROWS * field + ROWS]
    next_edges[pl.ds(3, 2 * ROWS, stride=4), :] = pltpu.roll(after[2 * ROWS * FACE_Y : 2 * ROWS * (FACE_Y + 1)], beyond + 1, 1)
    final = jnp.logical_and(chunk == 3, lane == 127)[:ROWS]
    ext[NEXT_Y, 2:6] = jnp.where(
        final, next_edges[...].reshape(ROWS, 8, 128), ahead(full[ROWS * FACE_Y : ROWS * (FACE_Y + 1)], 1)
    )

    to_up = send(ext.at[:, pl.ds(4, 2)], ext.at[:, pl.ds(0, 2)], 3, 3, gx + 1, gy)
    to_down = send(ext.at[:, pl.ds(2, 2)], ext.at[:, pl.ds(6, 2)], 4, 4, gx - 1, gy)
    to_down_face = send(ext.at[FACE_X, 4], last_face, 5, 5, gx - 1, gy)

    @pl.when(jnp.logical_not(last_x))
    def _():
        to_up.start()

    @pl.when(jnp.logical_not(first_x))
    def _():
        to_down.start()
        to_down_face.start()

    for copy in small_loads:
        copy.wait()

    total_cells = cells * n_gy
    spare = n_gy - 1

    def fill(page, buffer, slot, amount):
        pages[page] = window(buffer, slot, n_gy, cells, amount, 3)

    def deliver(source, target, sem, arrived, x, y):
        if x == 0:
            here = first_x & (y == gy)

            @pl.when(jnp.logical_not(here))
            def _():
                send(source, target, sem, arrived, 0, y).start()

            @pl.when(here)
            def _():
                pltpu.make_async_copy(source, target, recv_sems.at[arrived]).start()

        else:
            send(source, target, sem, arrived, x, y).start()

    def hand(page, target, sem, arrived, x):
        everyone(lambda y: deliver(pages.at[page, y], target, sem, arrived, x, y))

    def hand_prior(page, target, r):
        for y in (0, half):
            for plane in range(2):
                part = pl.ds(4 * plane + 3, 1)
                source = pages.at[page, (y - 1) % n_gy, part]
                deliver(source, target.at[part], 9, 20 + 2 * per + r, 0, y)

    def hand_next(page, target, sem, arrived, x):
        def one(y):
            following = lax.rem(y + 1, n_gy)
            for plane in range(2):
                source = pages.at[page, following, pl.ds(4 * plane, 1)]
                deliver(source, target(plane), sem, arrived, x, y)

        everyone(one)

    def next_faces(faces, rows):
        shape = faces.shape
        lanes = lax.broadcasted_iota(jnp.int32, shape, 2)
        places = lax.broadcasted_iota(jnp.int32, shape, 1)
        follow = pltpu.roll(jnp.broadcast_to(rows[:, 0:1, :], (2 * shape[0], 8, 128)), 123, 2)
        follow = follow.reshape(shape[0], 2, 8, 128)
        chosen = jnp.where(places < 4, follow[:, 0], follow[:, 1])
        return jnp.where((places % 4 == 3) & (lanes == 127), chosen, ahead(faces, 1))

    def wait_left():
        wait_bytes(ext.at[:, pl.ds(0, 2)], recv_sems.at[3])

    def wait_right():
        wait_bytes(ext.at[:, pl.ds(6, 2)], recv_sems.at[4])
        wait_bytes(last_face, recv_sems.at[5])

    places = []
    for slot in range(per):
        t = gy * per + slot
        places.append((slot, lax.div(t, ROWS), lax.rem(t, ROWS)))

    def own_conditions(r, field, row):
        inner = (row < 3 + r) & ((row < 2) == first_x)
        edge = (row == 3) & (field == FACE_X) & (r == 0) & (gx == middle)
        return inner, jnp.logical_and(inner, field == FACE_Y), edge

    def far_conditions(r, field, row):
        inner = row >= 2 + r
        return inner, jnp.logical_and(inner, field == FACE_Y)

    def own_lines():
        for slot, field, row in places:

            @pl.when((row < 2) == first_x)
            def _(slot=slot):
                wait_bytes(line_own.at[slot, pl.ds(0, 8 * n_gy), :], recv_sems.at[2])

        line_own[:, pl.ds(8 * n_gy, 8 * n_gy), :] = line_own[:, pl.ds(0, 8 * n_gy), :]
        for slot, field, row in places:

            def frame(r, carry, slot=slot, field=field, row=row):
                inner, faces, edge = own_conditions(r, field, row)
                amount = jnp.where(first_x, remap_own[r], remap_ref[r])
                page = r * per + slot

                @pl.when(jnp.logical_or(inner, edge))
                def _():
                    fill(page, line_own, slot, amount)

                @pl.when(inner)
                def _():
                    hand(page, framed.at[r, field, row + 2 - r], 9, 11 + r, 0)
                    hand_prior(page, prior.at[r, field, row + 2 - r], r)

                @pl.when(edge)
                def _():
                    hand(page, framed_face.at[0], 9, 13, 0)
                    hand_prior(page, prior_face.at[0], 0)

                @pl.when(faces)
                def _():
                    start = 2 * (row + 2 - r)
                    hand_next(page, lambda plane: framed_next.at[r, start + plane, pl.ds(0, 1)], 15, 18 + 2 * per + r, 0)

                return carry

            lax.fori_loop(0, 2, frame, 0)

    mine = jnp.where(lax.rem(gy, 2) == 0, lax.div(gy, 2), half + lax.div(gy, 2))
    ghost_places = []
    for slot in range(-(-(STRIPS + 1) // n_gy)):
        u = slot * n_gy + mine
        ghost_places.append((slot, u, lax.div(u, 2) == FACE_Y))

    @pl.when(first_x)
    def _():
        wait_right()
        ext[:, 0:2] = ext[:, 2:4]

    @pl.when(jnp.logical_not(first_x))
    def _():
        wait_left()

    @pl.when(jnp.logical_not(jnp.logical_or(first_x, last_x)))
    def _():
        wait_right()

    @pl.when(last_x)
    def _():
        wait_bytes(ext.at[pl.ds(0, 8), pl.ds(6, 2)], recv_sems.at[4])
        wait_bytes(last_face, recv_sems.at[5])
        wait_bytes(ghost_next.at[:, pl.ds(0, 1)], recv_sems.at[17 + 2 * per])
        ext[NEXT_Y, 6:8] = next_faces(ext[FACE_Y, 6:8], ghost_next[...])

    fields = [ext[field] for field in range(8)]
    fields[FACE_X] = jnp.concatenate([fields[FACE_X], last_face[...][None]], axis=0)
    once = euler(fields, ext[NEXT_Y])
    twice = euler(once, ahead(once[FACE_Y], 1))
    for field in range(8):
        lines[ROWS * field : ROWS * field + ROWS] = 0.5 * (ext[field, 2:6] + twice[field][:ROWS])

    def spread(k, carry):
        t = lax.rem(k + (gy + half) * per, LINES)
        slot = lax.rem(t, per)
        target = line_in.at[slot, pl.ds(pl.multiple_of(8 * gy, 8), 8), :]

        @pl.when(jnp.logical_not(first_x) | (lax.rem(t, ROWS) >= 2))
        def _():
            send(lines.at[t], target, 6, 6, partner, lax.div(t, per)).start()

        return carry

    @pl.when(jnp.logical_not(first_x))
    def _():
        pl.semaphore_wait(known.at[2], 4)

    lax.fori_loop(0, LINES, spread, 0)

    @pl.when(first_x)
    def _():
        pl.semaphore_wait(known.at[2], 4)

    @pl.when(first_x)
    def _():
        ghost_amount = lax.rem(total_cells - shear_ref[0], total_cells)
        for slot, u, faces in ghost_places:

            @pl.when(u <= STRIPS)
            def _(slot=slot):
                wait_bytes(line_ghost.at[slot, pl.ds(0, 8 * n_gy), :], recv_sems.at[16 + per + slot])
                line_ghost[slot, pl.ds(8 * n_gy, 8 * n_gy), :] = line_ghost[slot, pl.ds(0, 8 * n_gy), :]
                fill(4 * per + slot, line_ghost, slot, ghost_amount)

        pl.semaphore_wait(known.at[3], n_gy)
        for slot, u, faces in ghost_places:

            @pl.when(u < STRIPS)
            def _(slot=slot, u=u):
                hand(4 * per + slot, ext.at[lax.div(u, 2), 6 + lax.rem(u, 2)], 8, 4, last)

            @pl.when(faces)
            def _(slot=slot, u=u):
                row = lax.rem(u, 2)
                hand_next(4 * per + slot, lambda plane: ghost_next.at[2 * row + plane, pl.ds(0, 1)], 15, 17 + 2 * per, last)

            @pl.when(u == STRIPS)
            def _(slot=slot):
                hand(4 * per + slot, last_face, 8, 5, last)

        own_lines()

        for slot, field, row in places:

            @pl.when(row >= 2)
            def _(slot=slot, field=field, row=row):
                wait_bytes(line_far.at[slot, pl.ds(0, 8 * n_gy), :], recv_sems.at[16 + slot])
                line_far[slot, pl.ds(8 * n_gy, 8 * n_gy), :] = line_far[slot, pl.ds(0, 8 * n_gy), :]

                def frame(r, carry):
                    inner, faces = far_conditions(r, field, row)
                    page = (2 + r) * per + slot
                    amount = lax.rem(remap_own[r] + shear_ref[0], total_cells)

                    @pl.when(inner)
                    def _():
                        fill(page, line_far, slot, amount)
                        hand(page, framed.at[r, field, row - 2 - r], 9, 11 + r, 0)
                        hand_prior(page, prior.at[r, field, row - 2 - r], r)

                    @pl.when(faces)
                    def _():
                        start = 2 * (row - 2 - r)
                        hand_next(page, lambda plane: framed_next.at[r, start + plane, pl.ds(0, 1)], 15, 18 + 2 * per + r, 0)

                    return carry

                lax.fori_loop(0, 2, frame, 0)

    amounts.wait_recv()
    levels.wait_recv()

    @pl.when(gx == middle)
    def _():
        own_lines()

        @pl.when(gy == spare)
        def _():
            wait_bytes(line_face.at[0, pl.ds(0, 8 * n_gy), :], recv_sems.at[16 + 2 * per])
            line_face[0, pl.ds(8 * n_gy, 8 * n_gy), :] = line_face[0, pl.ds(0, 8 * n_gy), :]
            fill(5 * per, line_face, 0, remap_ref[1])
            hand(5 * per, framed_face.at[1], 9, 14, 0)
            hand_prior(5 * per, prior_face.at[1], 1)

    expected = [jnp.logical_or(gx != middle, row >= 2) for _, _, row in places]
    for slot in range(per):

        @pl.when(expected[slot])
        def _(slot=slot):
            wait_bytes(line_in.at[slot, pl.ds(0, 8 * n_gy), :], recv_sems.at[6])

    for slot in range(per):

        @pl.when(expected[slot])
        def _(slot=slot):
            row = lax.rem(gy * per + slot, ROWS)
            line_in[slot, pl.ds(8 * n_gy, 8 * n_gy), :] = line_in[slot, pl.ds(0, 8 * n_gy), :]
            tiles = window(line_in, slot, n_gy, cells, remap_ref[row], 2)
            weight = (frac_ref[row].astype(jnp.float32) + 0.5) / FRAC
            line_out[slot] = (1.0 - weight) * ahead(tiles, 2) + weight * ahead(tiles, 1)
            target = raw.at[pl.ds(pl.multiple_of(8 * (gy * per + slot), 8), 8), :]
            everyone(lambda y: send(line_out.at[slot, y], target, 7, 7, partner, y).start())

    next_copy = send(to_next, from_previous, 12, 15, 0, right_y)
    far_left = (gy == 0) | (gy == half)
    sends_next = (gy != half - 1) & (gy != n_gy - 1)
    prior_bytes = line_in.at[0, pl.ds(0, 82), :]

    @pl.when(first_x)
    def _():
        def advance(fields, last, following):
            fields = fields[:FACE_X] + [jnp.concatenate([fields[FACE_X], last[None]], axis=0)] + fields[FACE_Y:]
            once = euler(fields, following)
            twice = euler(once, ahead(once[FACE_Y], 1))
            return [0.5 * (fields[field][2] + twice[field][0]) for field in range(8)]

        for r in range(2):
            wait_bytes(framed.at[r], recv_sems.at[11 + r])
            wait_bytes(framed_face.at[r], recv_sems.at[13 + r])
            wait_bytes(framed_next.at[r, :, pl.ds(0, 1)], recv_sems.at[18 + 2 * per + r])
            fields = [framed[r, field] for field in range(8)]
            done = advance(fields, framed_face[r], next_faces(fields[FACE_Y], framed_next[r]))
            for field in range(8):
                fresh[pl.ds(64 * r + 8 * field, 8), :] = done[field]

        @pl.when(sends_next)
        def _():
            to_next[...] = fresh[pl.ds(3, 32, stride=4), :]
            next_copy.start()

        @pl.when(far_left)
        def _():
            for r in range(2):
                wait_bytes(prior_bytes, recv_sems.at[20 + 2 * per + r])
                fields = [prior[r, field] for field in range(8)]
                lanes = lax.broadcasted_iota(jnp.int32, fields[0].shape, 2)
                chunks = lax.broadcasted_iota(jnp.int32, fields[0].shape, 1) % 4
                follow = pltpu.roll(pltpu.roll(framed[r, FACE_Y], 123, 2), 3, 1)
                following = jnp.where((chunks == 3) & (lanes == 127), follow, ahead(fields[FACE_Y], 1))
                done = advance(fields, prior_face[r], following)
                for field in range(8):
                    fresh_edges[pl.ds(64 * r + 8 * field, 8), :] = done[field]
            from_previous[...] = fresh_edges[pl.ds(3, 32, stride=4), :]

        @pl.when(jnp.logical_not(far_left))
        def _():
            next_copy.wait_recv()

        reach = cells % 128 + 1
        fresh_edges[pl.ds(0, 32, stride=4), :] = pltpu.roll(from_previous[...], 129 - reach, 1)

    @pl.when(jnp.logical_not(first_x))
    def _():
        wait_bytes(raw, recv_sems.at[7])

    @pl.when(first_x)
    def _():
        wait_bytes(raw.at[pl.ds(0, 4 * LINES)], recv_sems.at[7])
        tiles = fresh[...].reshape(16, 8, 128)
        lanes = lax.broadcasted_iota(jnp.int32, tiles.shape, 2)
        chunks = lax.broadcasted_iota(jnp.int32, tiles.shape, 1) % 4
        tiles = jnp.where((chunks == 0) & (lanes == 1), fresh_edges[...].reshape(16, 8, 128), tiles)
        here, there = ahead(tiles, 2), ahead(tiles, 1)
        for r in range(2):
            weight = (frac_own[r].astype(jnp.float32) + 0.5) / FRAC
            mixed = (1.0 - weight) * here[8 * r : 8 * r + 8] + weight * there[8 * r : 8 * r + 8]
            for field in range(8):
                raw[pl.ds(32 * field + 8 * r, 8), :] = mixed[field]

    out_ref[...] = raw[...]

    for copy in (strip_left, strip_right, amounts, levels):
        copy.wait_send()

    @pl.when(gx == 1)
    def _():
        near_copy.wait_send()

    @pl.when(jnp.logical_not(last_x))
    def _():
        to_up.wait_send()

    @pl.when(jnp.logical_not(first_x))
    def _():
        to_down.wait_send()
        to_down_face.wait_send()

    @pl.when(last_x)
    def _():
        wait_bytes(held.at[pl.ds(0, STRIPS)], send_sems.at[2])

    def left(condition, page, sem):
        @pl.when(condition)
        def _():
            wait_bytes(pages.at[page], send_sems.at[sem])

    def left_prior(near):
        for condition, rows in ((near, 2), (jnp.logical_not(near), 4)):

            @pl.when(condition)
            def _(rows=rows):
                wait_bytes(line_in.at[0, pl.ds(0, rows), :], send_sems.at[9])

    def left_next(condition, one_less=0):
        @pl.when(condition)
        def _():
            wait_bytes(pages.at[pl.ds(0, 2), pl.ds(0, n_gy - one_less), pl.ds(0, 1)], send_sems.at[15])

    @pl.when(first_x)
    def _():
        stayed = sum((row < 2).astype(jnp.int32) for _, _, row in places)
        for count in range(per + 1):

            @pl.when(stayed == count)
            def _(count=count):
                wait_bytes(held.at[pl.ds(0, LINES - count)], send_sems.at[2])

        wait_bytes(near_face, send_sems.at[13])

        @pl.when(sends_next)
        def _():
            next_copy.wait_send()

        count_own = sum((u <= STRIPS).astype(jnp.int32) for _, u, _ in ghost_places)
        for count in range(len(ghost_places) + 1):

            @pl.when(count_own == count)
            def _(count=count):
                wait_bytes(held.at[pl.ds(0, STRIPS + 1 - count)], send_sems.at[14])

        for slot, u, faces in ghost_places:
            left(u <= STRIPS, 4 * per + slot, 8)
            left_next(faces)

        for slot, field, row in places:
            for r in range(2):
                inner, faces = far_conditions(r, field, row)
                left_next(faces, 1)

                @pl.when(inner)
                def _(slot=slot, r=r):
                    wait_bytes(pages.at[(2 + r) * per + slot, pl.ds(0, n_gy - 1)], send_sems.at[9])
                    left_prior(far_left)

                inner, faces, _ = own_conditions(r, field, row)
                left_next(faces, 1)

                @pl.when(inner)
                def _(slot=slot, r=r):
                    wait_bytes(pages.at[r * per + slot, pl.ds(0, n_gy - 1)], send_sems.at[9])
                    left_prior(far_left)


    @pl.when(gx == middle)
    def _():
        @pl.when(gy == spare)
        def _():
            wait_bytes(pages.at[5 * per], send_sems.at[9])
            left_prior(first_x)

        for slot, field, row in places:
            for r in range(2):
                inner, faces, edge = own_conditions(r, field, row)
                left(jnp.logical_or(inner, edge), r * per + slot, 9)
                left_next(faces)

                @pl.when(jnp.logical_or(inner, edge))
                def _():
                    left_prior(first_x)


    @pl.when(first_x)
    def _():
        wait_bytes(lines.at[pl.ds(0, LINES // 2)], send_sems.at[6])

    @pl.when(jnp.logical_not(first_x))
    def _():
        wait_bytes(lines, send_sems.at[6])

    for slot in range(per):

        @pl.when(expected[slot])
        def _(slot=slot):
            wait_bytes(line_out.at[slot], send_sems.at[7])


def unpack(tiles_ref, out_ref):
    cells = out_ref.shape[3]
    for field in range(8):
        for plane in range(2):
            for chunk in range(4):
                part = tiles_ref[pl.ds(field * 32 + plane * 4 + chunk, ROWS, stride=8), :]
                width = min(128, cells - 128 * chunk)
                out_ref[field, plane, :, pl.ds(128 * chunk, width)] = part[:, :width]


def solution(mesh):
    n_gx = mesh.shape["gx"]
    n_gy = mesh.shape["gy"]

    def shards(state, shear_offset, remap_shift, frac_index):
        cells = state.shape[3]
        per = LINES // n_gy
        vmem = lambda *shape: pltpu.VMEM(shape, jnp.float32)
        large = pl.BlockSpec(memory_space=pltpu.VMEM)
        whole = pl.BlockSpec(memory_space=pltpu.HBM)
        tiles = pl.pallas_call(
            functools.partial(kernel, n_gx, n_gy, cells),
            out_shape=pltpu.VMEM((8 * LINES, 128), jnp.float32),
            in_specs=[whole] * 4,
            out_specs=large,
            scratch_shapes=[
                pltpu.SMEM((1,), jnp.int32),
                pltpu.SMEM((ROWS,), jnp.int32),
                pltpu.SMEM((ROWS,), jnp.int32),
                pltpu.SMEM((ROWS,), jnp.int32),
                pltpu.SMEM((ROWS,), jnp.int32),
                vmem(*state.shape),
                vmem(8 * LINES, 128),
                vmem(LINES, 8, 128),
                vmem(9, 8, 8, 128),
                vmem(8, 128),
                vmem(64, 128),
                vmem(64, 128),
                vmem(64, 128),
                vmem(64, 128),
                vmem(8 * LINES, 128),
                vmem(8 * ROWS, 128),
                vmem(per, 16 * n_gy, 128),
                vmem(per, 16 * n_gy, 128),
                vmem(per, 16 * n_gy, 128),
                vmem(1, 16 * n_gy, 128),
                vmem(8, 128),
                vmem(PAGES * per, n_gy, 8, 128),
                vmem(2, 8, 5, 8, 128),
                vmem(2, 10, 8, 128),
                vmem(4, 8, 128),
                vmem(2, 8, 128),
                vmem(2, 8, 5, 8, 128),
                vmem(2, 8, 128),
                vmem(128, 128),
                vmem(128, 128),
                vmem(32, 128),
                vmem(32, 128),
                vmem(per, 16 * n_gy, 128),
                vmem(per, n_gy, 8, 128),
                vmem(LINES, 8, 128),
                pltpu.SemaphoreType.DMA((16,)),
                pltpu.SemaphoreType.DMA((22 + 2 * per,)),
                pltpu.SemaphoreType.DMA((4,)),
                pltpu.SemaphoreType.REGULAR((4,)),
            ],
            compiler_params=pltpu.CompilerParams(
                collective_id=0, has_side_effects=True
            ),
        )(shear_offset, remap_shift, frac_index, state)
        return pl.pallas_call(
            unpack,
            out_shape=jax.ShapeDtypeStruct(state.shape, jnp.float32),
            in_specs=[large],
            out_specs=large,
            compiler_params=pltpu.CompilerParams(vmem_limit_bytes=8 * 2**20),
        )(tiles)

    placed = (P(None, None, "gx", "gy"), P(), P("gx"), P("gx"))
    return jax.shard_map(shards, mesh=mesh, in_specs=placed, out_specs=P(None, None, "gx", "gy"), check_vma=False)
```

```python
import functools

import jax
import jax.numpy as jnp
from jax import lax
from jax.experimental import pallas as pl
from jax.experimental.pallas import tpu as pltpu
from jax.sharding import PartitionSpec as P

FRAC = 16
GAMMA_LESS = 5.0 / 3.0 - 1.0
ROTATION = 1.0
SHEAR_RATE = 1.5
MAX_SPEED = 5.0
TIME_STEP = 0.05

FACE_X, FACE_Y, FACE_Z, NEXT_Y = 5, 6, 7, 8
ROWS = 4
LINES = 8 * ROWS
STRIPS = 16
PAGES = 6
MESH = pl.DeviceIdType.MESH


def ahead(value, count):
    lane = lax.broadcasted_iota(jnp.int32, value.shape, 2)
    moved = pltpu.roll(value, 128 - count, 2)
    return jnp.where(lane >= 128 - count, pltpu.roll(moved, 7, 1), moved)


def behind(value, count):
    lane = lax.broadcasted_iota(jnp.int32, value.shape, 2)
    moved = pltpu.roll(value, count, 2)
    return jnp.where(lane < count, pltpu.roll(moved, 1, 1), moved)


def other_plane(value):
    return pltpu.roll(value, 4, 1)


def euler(fields, next_y):
    density, mom_x, mom_y, mom_z, energy, face_x, face_y, face_z = fields
    rows = density.shape[0]
    mid = slice(1, rows - 1)
    cen_x = 0.5 * (face_x[:-1] + face_x[1:])
    cen_y = 0.5 * (face_y + next_y)
    cen_z = 0.5 * (face_z + other_plane(face_z))
    inverse = 1.0 / density
    vel_x = mom_x * inverse
    vel_y = mom_y * inverse
    vel_z = mom_z * inverse
    magnetic = 0.5 * (cen_x * cen_x + cen_y * cen_y + cen_z * cen_z)
    pressure = (
        GAMMA_LESS * (energy - 0.5 * (mom_x * vel_x + mom_y * vel_y + mom_z * vel_z) - magnetic) + magnetic
    )
    vel_dot = vel_x * cen_x + vel_y * cen_y + vel_z * cen_z
    conserved = (density, mom_x, mom_y, mom_z, energy)
    momenta = (mom_x, mom_y, mom_z)
    centred = (cen_x, cen_y, cen_z)
    velocity = (vel_x, vel_y, vel_z)
    change = [None] * 5
    for normal in range(3):
        part = slice(None) if normal == 0 else mid
        speed = velocity[normal][part]
        across = centred[normal][part]
        fluxes = [momenta[normal][part]]
        for second in range(3):
            term = momenta[second][part] * speed - across * centred[second][part]
            if second == normal:
                term = term + pressure[part]
            fluxes.append(term)
        fluxes.append((energy[part] + pressure[part]) * speed - across * vel_dot[part])
        for member in range(5):
            flux = fluxes[member]
            held = conserved[member][part]
            if normal == 0:
                upwind = 0.5 * (flux[:-1] + flux[1:]) - 0.5 * MAX_SPEED * (held[1:] - held[:-1])
                delta = upwind[1:] - upwind[:-1]
            elif normal == 1:
                upwind = 0.5 * (behind(flux, 1) + flux) - 0.5 * MAX_SPEED * (held - behind(held, 1))
                delta = ahead(upwind, 1) - upwind
            else:
                upwind = 0.5 * (other_plane(flux) + flux) - 0.5 * MAX_SPEED * (held - other_plane(held))
                delta = other_plane(upwind) - upwind
            change[member] = -delta if change[member] is None else change[member] - delta
    change[1] = change[1] + 2.0 * ROTATION * mom_y[mid]
    change[2] = change[2] - (2.0 - SHEAR_RATE) * ROTATION * mom_x[mid]
    change[4] = change[4] + SHEAR_RATE * ROTATION * (mom_x[mid] * vel_y[mid] - cen_x[mid] * cen_y[mid])
    elec_x = -(vel_y * cen_z - vel_z * cen_y)
    elec_y = -(vel_z * cen_x - vel_x * cen_z)
    elec_z = -(vel_x * cen_y - vel_y * cen_x)
    pair_x = elec_x[mid] + behind(elec_x[mid], 1)
    edge_x = 0.25 * (pair_x + other_plane(pair_x))
    pair_y = elec_y[1:] + elec_y[:-1]
    edge_y = 0.25 * (pair_y + other_plane(pair_y))
    pair_z = elec_z[1:] + elec_z[:-1]
    edge_z = 0.25 * (pair_z + behind(pair_z, 1))
    delta_x = -(ahead(edge_z, 1) - edge_z - (other_plane(edge_y) - edge_y))
    delta_y = -(other_plane(edge_x) - edge_x - (edge_z[1:] - edge_z[:-1]))
    delta_z = -(edge_y[1:] - edge_y[:-1] - (ahead(edge_x, 1) - edge_x))
    done = [conserved[member][mid] + TIME_STEP * change[member] for member in range(5)]
    done.append(face_x[1:rows] + TIME_STEP * delta_x)
    done.append(face_y[mid] + TIME_STEP * delta_y)
    done.append(face_z[mid] + TIME_STEP * delta_z)
    return done


def window(ref, slot, blocks, cells, amount, kinds):
    hops = lax.div(amount, cells)
    rest = lax.rem(amount, cells)
    if kinds == 3:
        low = rest < 2
        hops = jnp.where(low, hops - 1, hops)
        rest = jnp.where(low, rest + cells, rest)
    total = blocks * 8
    lane = lax.broadcasted_iota(jnp.int32, (blocks, 8, 128), 2)
    chunk = lax.broadcasted_iota(jnp.int32, (blocks, 8, 128), 1) % 4
    place = chunk * 128 + lane - 2 - rest
    result = None
    for kind in reversed(range(kinds)):
        distance = rest - kind * cells + 1024
        lanes = lax.rem(distance, 128)
        sublanes = lax.div(distance, 128) - 8
        back = lax.rem(8 * (hops + kind) + sublanes + total, total)
        near = ref[slot, pl.ds(total - back, total), :].reshape(blocks, 8, 128)
        far = ref[slot, pl.ds(total - back - 1, total), :].reshape(blocks, 8, 128)
        near = pltpu.roll(near, lanes, 2)
        far = pltpu.roll(far, lanes, 2)
        moved = jnp.where(lane >= lanes, near, far)
        if result is None:
            result = moved
        else:
            result = jnp.where(place >= -kind * cells, moved, result)
    return result


def kernel(
    n_gx,
    n_gy,
    cells,
    shear_hbm,
    remap_hbm,
    frac_hbm,
    state_hbm,
    out_ref,
    shear_ref,
    remap_ref,
    frac_ref,
    remap_own,
    frac_own,
    state_ref,
    raw,
    held,
    ext,
    last_face,
    to_left,
    to_right,
    from_left,
    from_right,
    edges,
    next_edges,
    line_ghost,
    line_own,
    line_far,
    line_face,
    near_face,
    pages,
    framed,
    framed_next,
    ghost_next,
    framed_face,
    prior,
    prior_face,
    fresh,
    fresh_edges,
    to_next,
    from_previous,
    line_in,
    line_out,
    lines,
    send_sems,
    recv_sems,
    load_sems,
    known,
):
    gx = lax.axis_index("gx")
    gy = lax.axis_index("gy")
    half = n_gy // 2
    per = LINES // n_gy
    left_y = lax.rem(gy + n_gy - 1, n_gy)
    right_y = lax.rem(gy + 1, n_gy)
    inside = lax.rem(gy, half)
    side = gy - inside
    core = gy + 1 - 2 * lax.rem(gy, 2)
    up, down, up_2, down_2 = (side + lax.rem(inside + half + step, half) for step in (2, -2, 4, -4))
    partner = lax.rem(gx + n_gx // 2, n_gx)
    middle = n_gx // 2
    last = n_gx - 1
    first_x = gx == 0
    last_x = gx == last
    barrier = pltpu.get_barrier_semaphore()
    load = pltpu.make_async_copy(state_hbm, state_ref, load_sems.at[0])
    load.start()
    small_loads = [
        pltpu.make_async_copy(source, target, load_sems.at[1 + k])
        for k, (source, target) in enumerate(
            ((shear_hbm, shear_ref), (remap_hbm, remap_own), (frac_hbm, frac_own))
        )
    ]
    for copy in small_loads:
        copy.start()

    def tell(sem, x, y):
        pl.semaphore_signal(sem, inc=1, device_id=(x, y), device_id_type=MESH)

    def everyone(body):
        def step(k, carry):
            body(lax.rem(k + gy, n_gy))
            return carry

        lax.fori_loop(0, n_gy, step, 0)

    def send(source, target, sent, arrived, x, y):
        return pltpu.make_async_remote_copy(
            src_ref=source,
            dst_ref=target,
            send_sem=send_sems.at[sent],
            recv_sem=recv_sems.at[arrived],
            device_id=(x, y),
            device_id_type=MESH,
        )

    def wait_bytes(ref, sem):
        pltpu.make_async_copy(ref, ref, sem).wait()

    @pl.when(first_x)
    def _():
        def step(k, carry):
            tell(barrier, 0, lax.rem(gy + k, n_gy))
            return carry

        lax.fori_loop(1, n_gy, step, 0)

    @pl.when(gx == middle)
    def _():
        everyone(lambda y: tell(barrier, 0, y))

    @pl.when(jnp.logical_not(first_x))
    def _():
        for y in (left_y, right_y, up, down):
            tell(barrier, gx, y)

    @pl.when(gx != middle)
    def _():
        for y in (gy, lax.rem(gy + half, n_gy)):
            tell(barrier, partner, y)

    @pl.when(jnp.logical_not(first_x))
    def _():
        tell(barrier, gx - 1, gy)

    @pl.when(jnp.logical_not(last_x))
    def _():
        tell(barrier, gx + 1, gy)

    @pl.when(first_x)
    def _():
        everyone(lambda y: tell(barrier, last, y))

    load.wait()
    whole = cells // 128
    for field in range(8):
        for plane in range(2):
            for chunk in range(4):
                if chunk < whole:
                    part = state_ref[field, plane, :, pl.ds(128 * chunk, 128)]
                else:
                    part = state_ref[field, plane, :, pl.ds(128 * whole, cells - 128 * whole)]
                    part = jnp.concatenate([part, jnp.zeros((ROWS, 128 * (whole + 1) - cells), jnp.float32)], axis=1)
                raw[pl.ds(field * 32 + plane * 4 + chunk, ROWS, stride=8), :] = part
    to_left[...] = raw[pl.ds(0, 64, stride=4), :]
    to_right[...] = raw[pl.ds(3, 64, stride=4), :]
    held[...] = behind(raw[...].reshape(LINES, 8, 128), 2)
    pl.semaphore_wait(barrier, jnp.where(last_x, 7 + n_gy, jnp.where(first_x, 2 * n_gy, 8)))

    @pl.when(jnp.logical_not(first_x))
    def _():
        for y in (core, up, down):
            tell(known.at[0], gx, y)


    def line_place(buffer, t):
        return buffer.at[lax.rem(t, per), pl.ds(pl.multiple_of(8 * gy, 8), 8), :]

    @pl.when(last_x)
    def _():
        def step(k, carry):
            u = lax.rem(k + lax.div(gy, 2), STRIPS)
            t = lax.div(u, 2) * ROWS + 2 + lax.rem(u, 2)
            send(held.at[t], line_place(line_far, t), 2, 16 + lax.rem(t, per), 0, lax.div(t, per)).start()
            return carry

        lax.fori_loop(0, STRIPS, step, 0)
        everyone(lambda y: tell(known.at[3], 0, y))

    near_copy = send(held.at[FACE_X * ROWS], near_face, 12, 8, 0, gy)
    strip_left = send(to_left, from_right, 0, 0, gx, left_y)
    strip_right = send(to_right, from_left, 1, 1, gx, right_y)
    strip_left.start()
    strip_right.start()

    @pl.when(gx == 1)
    def _():
        near_copy.start()

    amounts = send(remap_hbm, remap_ref, 10, 9, partner, gy)
    levels = send(frac_hbm, frac_ref, 11, 10, partner, gy)
    amounts.start()
    levels.start()
    @pl.when(jnp.logical_not(first_x))
    def _():
        pl.semaphore_wait(known.at[0], 3)
        if half > 4:
            for y in (up_2, down_2):
                tell(known.at[1], gx, y)
            pl.semaphore_wait(known.at[1], 2)

    for y in (gy, core):
        tell(known.at[2], partner, y)
        tell(known.at[2], partner, lax.rem(y + half, n_gy))

    @pl.when(first_x)
    def _():
        def ghosts(k, carry):
            u = lax.rem(k + lax.div(gy, 2), STRIPS + 1)
            rank = lax.rem(u, n_gy)
            slot = lax.div(u, n_gy)
            owner = jnp.where(rank < half, 2 * rank, 2 * (rank - half) + 1)
            tile = jnp.where(u == STRIPS, FACE_X * ROWS + 2, lax.div(u, 2) * ROWS + lax.rem(u, 2))
            target = line_ghost.at[slot, pl.ds(pl.multiple_of(8 * gy, 8), 8), :]
            arrived = 16 + per + slot

            @pl.when(owner != gy)
            def _():
                send(held.at[tile], target, 14, arrived, 0, owner).start()

            @pl.when(owner == gy)
            def _():
                pltpu.make_async_copy(held.at[tile], target, recv_sems.at[arrived]).start()

            return carry

        def whole(k, carry):
            t = lax.rem(k + (gy + half) * per, LINES)
            owner = lax.div(t, per)
            stays = lax.rem(t, ROWS) < 2

            @pl.when(jnp.logical_not(stays & (owner == gy)))
            def _():
                send(held.at[t], line_place(line_own, t), 2, 2, jnp.where(stays, 0, middle), owner).start()

            @pl.when(stays & (owner == gy))
            def _():
                pltpu.make_async_copy(held.at[t], line_place(line_own, t), recv_sems.at[2]).start()

            return carry

        lax.fori_loop(0, STRIPS + 1, ghosts, 0)
        lax.fori_loop(0, LINES, whole, 0)
        near_copy.wait_recv()
        send(near_face, line_place(line_face, 0), 13, 16 + 2 * per, middle, n_gy - 1).start()

    strip_left.wait_recv()
    strip_right.wait_recv()
    lane = lax.broadcasted_iota(jnp.int32, (LINES, 8, 128), 2)
    chunk = lax.broadcasted_iota(jnp.int32, (LINES, 8, 128), 1) % 4
    beyond = cells % 128
    after = from_right[...]
    edges[pl.ds(0, 64, stride=4), :] = pltpu.roll(from_left[...], 130 - beyond, 1)
    edges[pl.ds(3, 64, stride=4), :] = pltpu.roll(after, beyond + 2, 1)
    outside = jnp.logical_or(
        jnp.logical_and(chunk == 0, lane < 2), jnp.logical_and(chunk == 3, lane >= beyond + 2)
    )
    full = jnp.where(outside, edges[...].reshape(LINES, 8, 128), held[...])
    for field in range(8):
        ext[field, 2:6] = full[ROWS * field : ROWS * field + ROWS]
    next_edges[pl.ds(3, 2 * ROWS, stride=4), :] = pltpu.roll(after[2 * ROWS * FACE_Y : 2 * ROWS * (FACE_Y + 1)], beyond + 1, 1)
    final = jnp.logical_and(chunk == 3, lane == 127)[:ROWS]
    ext[NEXT_Y, 2:6] = jnp.where(
        final, next_edges[...].reshape(ROWS, 8, 128), ahead(full[ROWS * FACE_Y : ROWS * (FACE_Y + 1)], 1)
    )

    to_up = send(ext.at[:, pl.ds(4, 2)], ext.at[:, pl.ds(0, 2)], 3, 3, gx + 1, gy)
    to_down = send(ext.at[:, pl.ds(2, 2)], ext.at[:, pl.ds(6, 2)], 4, 4, gx - 1, gy)
    to_down_face = send(ext.at[FACE_X, 4], last_face, 5, 5, gx - 1, gy)

    @pl.when(jnp.logical_not(last_x))
    def _():
        to_up.start()

    @pl.when(jnp.logical_not(first_x))
    def _():
        to_down.start()
        to_down_face.start()

    for copy in small_loads:
        copy.wait()

    total_cells = cells * n_gy
    spare = n_gy - 1

    def fill(page, buffer, slot, amount):
        pages[page] = window(buffer, slot, n_gy, cells, amount, 3)

    def deliver(source, target, sem, arrived, x, y):
        if x == 0:
            here = first_x & (y == gy)

            @pl.when(jnp.logical_not(here))
            def _():
                send(source, target, sem, arrived, 0, y).start()

            @pl.when(here)
            def _():
                pltpu.make_async_copy(source, target, recv_sems.at[arrived]).start()

        else:
            send(source, target, sem, arrived, x, y).start()

    def hand(page, target, sem, arrived, x):
        everyone(lambda y: deliver(pages.at[page, y], target, sem, arrived, x, y))

    def hand_prior(page, target, r):
        for y in (0, half):
            for plane in range(2):
                part = pl.ds(4 * plane + 3, 1)
                source = pages.at[page, (y - 1) % n_gy, part]
                deliver(source, target.at[part], 9, 20 + 2 * per + r, 0, y)

    def hand_next(page, target, sem, arrived, x):
        def one(y):
            following = lax.rem(y + 1, n_gy)
            for plane in range(2):
                source = pages.at[page, following, pl.ds(4 * plane, 1)]
                deliver(source, target(plane), sem, arrived, x, y)

        everyone(one)

    def next_faces(faces, rows):
        shape = faces.shape
        lanes = lax.broadcasted_iota(jnp.int32, shape, 2)
        places = lax.broadcasted_iota(jnp.int32, shape, 1)
        follow = pltpu.roll(jnp.broadcast_to(rows[:, 0:1, :], (2 * shape[0], 8, 128)), 123, 2)
        follow = follow.reshape(shape[0], 2, 8, 128)
        chosen = jnp.where(places < 4, follow[:, 0], follow[:, 1])
        return jnp.where((places % 4 == 3) & (lanes == 127), chosen, ahead(faces, 1))

    def wait_left():
        wait_bytes(ext.at[:, pl.ds(0, 2)], recv_sems.at[3])

    def wait_right():
        wait_bytes(ext.at[:, pl.ds(6, 2)], recv_sems.at[4])
        wait_bytes(last_face, recv_sems.at[5])

    places = []
    for slot in range(per):
        t = gy * per + slot
        places.append((slot, lax.div(t, ROWS), lax.rem(t, ROWS)))

    def own_conditions(r, field, row):
        inner = (row < 3 + r) & ((row < 2) == first_x)
        edge = (row == 3) & (field == FACE_X) & (r == 0) & (gx == middle)
        return inner, jnp.logical_and(inner, field == FACE_Y), edge

    def far_conditions(r, field, row):
        inner = row >= 2 + r
        return inner, jnp.logical_and(inner, field == FACE_Y)

    def own_lines(amounts_ref):
        for slot, field, row in places:

            @pl.when((row < 2) == first_x)
            def _(slot=slot):
                wait_bytes(line_own.at[slot, pl.ds(0, 8 * n_gy), :], recv_sems.at[2])

        line_own[:, pl.ds(8 * n_gy, 8 * n_gy), :] = line_own[:, pl.ds(0, 8 * n_gy), :]
        for slot, field, row in places:

            def frame(r, carry, slot=slot, field=field, row=row):
                inner, faces, edge = own_conditions(r, field, row)
                page = r * per + slot

                @pl.when(jnp.logical_or(inner, edge))
                def _():
                    fill(page, line_own, slot, amounts_ref[r])

                @pl.when(inner)
                def _():
                    hand(page, framed.at[r, field, row + 2 - r], 9, 11 + r, 0)
                    hand_prior(page, prior.at[r, field, row + 2 - r], r)

                @pl.when(edge)
                def _():
                    hand(page, framed_face.at[0], 9, 13, 0)
                    hand_prior(page, prior_face.at[0], 0)

                @pl.when(faces)
                def _():
                    start = 2 * (row + 2 - r)
                    hand_next(page, lambda plane: framed_next.at[r, start + plane, pl.ds(0, 1)], 15, 18 + 2 * per + r, 0)

                return carry

            lax.fori_loop(0, 2, frame, 0)

    mine = jnp.where(lax.rem(gy, 2) == 0, lax.div(gy, 2), half + lax.div(gy, 2))
    ghost_places = []
    for slot in range(-(-(STRIPS + 1) // n_gy)):
        u = slot * n_gy + mine
        ghost_places.append((slot, u, lax.div(u, 2) == FACE_Y))

    @pl.when(first_x)
    def _():
        wait_right()
        ext[:, 0:2] = ext[:, 2:4]

    @pl.when(jnp.logical_not(first_x))
    def _():
        wait_left()

    @pl.when(jnp.logical_not(jnp.logical_or(first_x, last_x)))
    def _():
        wait_right()

    @pl.when(last_x)
    def _():
        wait_bytes(ext.at[pl.ds(0, 8), pl.ds(6, 2)], recv_sems.at[4])
        wait_bytes(last_face, recv_sems.at[5])
        wait_bytes(ghost_next.at[:, pl.ds(0, 1)], recv_sems.at[17 + 2 * per])
        ext[NEXT_Y, 6:8] = next_faces(ext[FACE_Y, 6:8], ghost_next[...])

    fields = [ext[field] for field in range(8)]
    fields[FACE_X] = jnp.concatenate([fields[FACE_X], last_face[...][None]], axis=0)
    once = euler(fields, ext[NEXT_Y])
    twice = euler(once, ahead(once[FACE_Y], 1))
    for field in range(8):
        lines[ROWS * field : ROWS * field + ROWS] = 0.5 * (ext[field, 2:6] + twice[field][:ROWS])

    def spread(k, carry):
        t = lax.rem(k + (gy + half) * per, LINES)
        slot = lax.rem(t, per)
        target = line_in.at[slot, pl.ds(pl.multiple_of(8 * gy, 8), 8), :]

        @pl.when(jnp.logical_not(first_x) | (lax.rem(t, ROWS) >= 2))
        def _():
            send(lines.at[t], target, 6, 6, partner, lax.div(t, per)).start()

        return carry

    @pl.when(jnp.logical_not(first_x))
    def _():
        pl.semaphore_wait(known.at[2], 4)

    lax.fori_loop(0, LINES, spread, 0)

    @pl.when(first_x)
    def _():
        pl.semaphore_wait(known.at[2], 4)

    @pl.when(first_x)
    def _():
        ghost_amount = lax.rem(total_cells - shear_ref[0], total_cells)
        for slot, u, faces in ghost_places:

            @pl.when(u <= STRIPS)
            def _(slot=slot):
                wait_bytes(line_ghost.at[slot, pl.ds(0, 8 * n_gy), :], recv_sems.at[16 + per + slot])
                line_ghost[slot, pl.ds(8 * n_gy, 8 * n_gy), :] = line_ghost[slot, pl.ds(0, 8 * n_gy), :]
                fill(4 * per + slot, line_ghost, slot, ghost_amount)

        pl.semaphore_wait(known.at[3], n_gy)
        for slot, u, faces in ghost_places:

            @pl.when(u < STRIPS)
            def _(slot=slot, u=u):
                hand(4 * per + slot, ext.at[lax.div(u, 2), 6 + lax.rem(u, 2)], 8, 4, last)

            @pl.when(faces)
            def _(slot=slot, u=u):
                row = lax.rem(u, 2)
                hand_next(4 * per + slot, lambda plane: ghost_next.at[2 * row + plane, pl.ds(0, 1)], 15, 17 + 2 * per, last)

            @pl.when(u == STRIPS)
            def _(slot=slot):
                hand(4 * per + slot, last_face, 8, 5, last)

        own_lines(remap_own)

        for slot, field, row in places:

            @pl.when(row >= 2)
            def _(slot=slot, field=field, row=row):
                wait_bytes(line_far.at[slot, pl.ds(0, 8 * n_gy), :], recv_sems.at[16 + slot])
                line_far[slot, pl.ds(8 * n_gy, 8 * n_gy), :] = line_far[slot, pl.ds(0, 8 * n_gy), :]

                def frame(r, carry):
                    inner, faces = far_conditions(r, field, row)
                    page = (2 + r) * per + slot
                    amount = lax.rem(remap_own[r] + shear_ref[0], total_cells)

                    @pl.when(inner)
                    def _():
                        fill(page, line_far, slot, amount)
                        hand(page, framed.at[r, field, row - 2 - r], 9, 11 + r, 0)
                        hand_prior(page, prior.at[r, field, row - 2 - r], r)

                    @pl.when(faces)
                    def _():
                        start = 2 * (row - 2 - r)
                        hand_next(page, lambda plane: framed_next.at[r, start + plane, pl.ds(0, 1)], 15, 18 + 2 * per + r, 0)

                    return carry

                lax.fori_loop(0, 2, frame, 0)

    amounts.wait_recv()
    levels.wait_recv()

    @pl.when(gx == middle)
    def _():
        own_lines(remap_ref)

        @pl.when(gy == spare)
        def _():
            wait_bytes(line_face.at[0, pl.ds(0, 8 * n_gy), :], recv_sems.at[16 + 2 * per])
            line_face[0, pl.ds(8 * n_gy, 8 * n_gy), :] = line_face[0, pl.ds(0, 8 * n_gy), :]
            fill(5 * per, line_face, 0, remap_ref[1])
            hand(5 * per, framed_face.at[1], 9, 14, 0)
            hand_prior(5 * per, prior_face.at[1], 1)

    expected = [jnp.logical_or(gx != middle, row >= 2) for _, _, row in places]
    for slot in range(per):

        @pl.when(expected[slot])
        def _(slot=slot):
            wait_bytes(line_in.at[slot, pl.ds(0, 8 * n_gy), :], recv_sems.at[6])

    for slot in range(per):

        @pl.when(expected[slot])
        def _(slot=slot):
            row = lax.rem(gy * per + slot, ROWS)
            line_in[slot, pl.ds(8 * n_gy, 8 * n_gy), :] = line_in[slot, pl.ds(0, 8 * n_gy), :]
            tiles = window(line_in, slot, n_gy, cells, remap_ref[row], 2)
            weight = (frac_ref[row].astype(jnp.float32) + 0.5) / FRAC
            line_out[slot] = (1.0 - weight) * ahead(tiles, 2) + weight * ahead(tiles, 1)
            target = raw.at[pl.ds(pl.multiple_of(8 * (gy * per + slot), 8), 8), :]
            everyone(lambda y: send(line_out.at[slot, y], target, 7, 7, partner, y).start())

    next_copy = send(to_next, from_previous, 12, 15, 0, right_y)
    far_left = (gy == 0) | (gy == half)
    sends_next = (gy != half - 1) & (gy != n_gy - 1)
    prior_bytes = line_in.at[0, pl.ds(0, 82), :]

    @pl.when(first_x)
    def _():
        def advance(fields, last, following):
            fields = fields[:FACE_X] + [jnp.concatenate([fields[FACE_X], last[None]], axis=0)] + fields[FACE_Y:]
            once = euler(fields, following)
            twice = euler(once, ahead(once[FACE_Y], 1))
            return [0.5 * (fields[field][2] + twice[field][0]) for field in range(8)]

        for r in range(2):
            wait_bytes(framed.at[r], recv_sems.at[11 + r])
            wait_bytes(framed_face.at[r], recv_sems.at[13 + r])
            wait_bytes(framed_next.at[r, :, pl.ds(0, 1)], recv_sems.at[18 + 2 * per + r])
            fields = [framed[r, field] for field in range(8)]
            done = advance(fields, framed_face[r], next_faces(fields[FACE_Y], framed_next[r]))
            for field in range(8):
                fresh[pl.ds(64 * r + 8 * field, 8), :] = done[field]

        @pl.when(sends_next)
        def _():
            to_next[...] = fresh[pl.ds(3, 32, stride=4), :]
            next_copy.start()

        @pl.when(far_left)
        def _():
            for r in range(2):
                wait_bytes(prior_bytes, recv_sems.at[20 + 2 * per + r])
                fields = [prior[r, field] for field in range(8)]
                lanes = lax.broadcasted_iota(jnp.int32, fields[0].shape, 2)
                chunks = lax.broadcasted_iota(jnp.int32, fields[0].shape, 1) % 4
                follow = pltpu.roll(pltpu.roll(framed[r, FACE_Y], 123, 2), 3, 1)
                following = jnp.where((chunks == 3) & (lanes == 127), follow, ahead(fields[FACE_Y], 1))
                done = advance(fields, prior_face[r], following)
                for field in range(8):
                    fresh_edges[pl.ds(64 * r + 8 * field, 8), :] = done[field]
            from_previous[...] = fresh_edges[pl.ds(3, 32, stride=4), :]

        @pl.when(jnp.logical_not(far_left))
        def _():
            next_copy.wait_recv()

        reach = cells % 128 + 1
        fresh_edges[pl.ds(0, 32, stride=4), :] = pltpu.roll(from_previous[...], 129 - reach, 1)

    @pl.when(jnp.logical_not(first_x))
    def _():
        wait_bytes(raw, recv_sems.at[7])

    @pl.when(first_x)
    def _():
        wait_bytes(raw.at[pl.ds(0, 4 * LINES)], recv_sems.at[7])
        tiles = fresh[...].reshape(16, 8, 128)
        lanes = lax.broadcasted_iota(jnp.int32, tiles.shape, 2)
        chunks = lax.broadcasted_iota(jnp.int32, tiles.shape, 1) % 4
        tiles = jnp.where((chunks == 0) & (lanes == 1), fresh_edges[...].reshape(16, 8, 128), tiles)
        here, there = ahead(tiles, 2), ahead(tiles, 1)
        for r in range(2):
            weight = (frac_own[r].astype(jnp.float32) + 0.5) / FRAC
            mixed = (1.0 - weight) * here[8 * r : 8 * r + 8] + weight * there[8 * r : 8 * r + 8]
            for field in range(8):
                raw[pl.ds(32 * field + 8 * r, 8), :] = mixed[field]

    out_ref[...] = raw[...]

    for copy in (strip_left, strip_right, amounts, levels):
        copy.wait_send()

    @pl.when(gx == 1)
    def _():
        near_copy.wait_send()

    @pl.when(jnp.logical_not(last_x))
    def _():
        to_up.wait_send()

    @pl.when(jnp.logical_not(first_x))
    def _():
        to_down.wait_send()
        to_down_face.wait_send()

    @pl.when(last_x)
    def _():
        wait_bytes(held.at[pl.ds(0, STRIPS)], send_sems.at[2])

    def left(condition, page, sem):
        @pl.when(condition)
        def _():
            wait_bytes(pages.at[page], send_sems.at[sem])

    def left_prior(near):
        for condition, rows in ((near, 2), (jnp.logical_not(near), 4)):

            @pl.when(condition)
            def _(rows=rows):
                wait_bytes(line_in.at[0, pl.ds(0, rows), :], send_sems.at[9])

    def left_next(condition, one_less=0):
        @pl.when(condition)
        def _():
            wait_bytes(pages.at[pl.ds(0, 2), pl.ds(0, n_gy - one_less), pl.ds(0, 1)], send_sems.at[15])

    @pl.when(first_x)
    def _():
        stayed = sum((row < 2).astype(jnp.int32) for _, _, row in places)
        for count in range(per + 1):

            @pl.when(stayed == count)
            def _(count=count):
                wait_bytes(held.at[pl.ds(0, LINES - count)], send_sems.at[2])

        wait_bytes(near_face, send_sems.at[13])

        @pl.when(sends_next)
        def _():
            next_copy.wait_send()

        count_own = sum((u <= STRIPS).astype(jnp.int32) for _, u, _ in ghost_places)
        for count in range(len(ghost_places) + 1):

            @pl.when(count_own == count)
            def _(count=count):
                wait_bytes(held.at[pl.ds(0, STRIPS + 1 - count)], send_sems.at[14])

        for slot, u, faces in ghost_places:
            left(u <= STRIPS, 4 * per + slot, 8)
            left_next(faces)

        for slot, field, row in places:
            for r in range(2):
                inner, faces = far_conditions(r, field, row)
                left_next(faces, 1)

                @pl.when(inner)
                def _(slot=slot, r=r):
                    wait_bytes(pages.at[(2 + r) * per + slot, pl.ds(0, n_gy - 1)], send_sems.at[9])
                    left_prior(far_left)

                inner, faces, _ = own_conditions(r, field, row)
                left_next(faces, 1)

                @pl.when(inner)
                def _(slot=slot, r=r):
                    wait_bytes(pages.at[r * per + slot, pl.ds(0, n_gy - 1)], send_sems.at[9])
                    left_prior(far_left)


    @pl.when(gx == middle)
    def _():
        @pl.when(gy == spare)
        def _():
            wait_bytes(pages.at[5 * per], send_sems.at[9])
            left_prior(first_x)

        for slot, field, row in places:
            for r in range(2):
                inner, faces, edge = own_conditions(r, field, row)
                left(jnp.logical_or(inner, edge), r * per + slot, 9)
                left_next(faces)

                @pl.when(jnp.logical_or(inner, edge))
                def _():
                    left_prior(first_x)


    @pl.when(first_x)
    def _():
        wait_bytes(lines.at[pl.ds(0, LINES // 2)], send_sems.at[6])

    @pl.when(jnp.logical_not(first_x))
    def _():
        wait_bytes(lines, send_sems.at[6])

    for slot in range(per):

        @pl.when(expected[slot])
        def _(slot=slot):
            wait_bytes(line_out.at[slot], send_sems.at[7])


def unpack(tiles_ref, out_ref):
    cells = out_ref.shape[3]
    for field in range(8):
        for plane in range(2):
            for chunk in range(4):
                part = tiles_ref[pl.ds(field * 32 + plane * 4 + chunk, ROWS, stride=8), :]
                width = min(128, cells - 128 * chunk)
                out_ref[field, plane, :, pl.ds(128 * chunk, width)] = part[:, :width]


def solution(mesh):
    n_gx = mesh.shape["gx"]
    n_gy = mesh.shape["gy"]

    def shards(state, shear_offset, remap_shift, frac_index):
        cells = state.shape[3]
        per = LINES // n_gy
        vmem = lambda *shape: pltpu.VMEM(shape, jnp.float32)
        large = pl.BlockSpec(memory_space=pltpu.VMEM)
        whole = pl.BlockSpec(memory_space=pltpu.HBM)
        tiles = pl.pallas_call(
            functools.partial(kernel, n_gx, n_gy, cells),
            out_shape=pltpu.VMEM((8 * LINES, 128), jnp.float32),
            in_specs=[whole] * 4,
            out_specs=large,
            scratch_shapes=[
                pltpu.SMEM((1,), jnp.int32),
                pltpu.SMEM((ROWS,), jnp.int32),
                pltpu.SMEM((ROWS,), jnp.int32),
                pltpu.SMEM((ROWS,), jnp.int32),
                pltpu.SMEM((ROWS,), jnp.int32),
                vmem(*state.shape),
                vmem(8 * LINES, 128),
                vmem(LINES, 8, 128),
                vmem(9, 8, 8, 128),
                vmem(8, 128),
                vmem(64, 128),
                vmem(64, 128),
                vmem(64, 128),
                vmem(64, 128),
                vmem(8 * LINES, 128),
                vmem(8 * ROWS, 128),
                vmem(per, 16 * n_gy, 128),
                vmem(per, 16 * n_gy, 128),
                vmem(per, 16 * n_gy, 128),
                vmem(1, 16 * n_gy, 128),
                vmem(8, 128),
                vmem(PAGES * per, n_gy, 8, 128),
                vmem(2, 8, 5, 8, 128),
                vmem(2, 10, 8, 128),
                vmem(4, 8, 128),
                vmem(2, 8, 128),
                vmem(2, 8, 5, 8, 128),
                vmem(2, 8, 128),
                vmem(128, 128),
                vmem(128, 128),
                vmem(32, 128),
                vmem(32, 128),
                vmem(per, 16 * n_gy, 128),
                vmem(per, n_gy, 8, 128),
                vmem(LINES, 8, 128),
                pltpu.SemaphoreType.DMA((16,)),
                pltpu.SemaphoreType.DMA((22 + 2 * per,)),
                pltpu.SemaphoreType.DMA((4,)),
                pltpu.SemaphoreType.REGULAR((4,)),
            ],
            compiler_params=pltpu.CompilerParams(
                collective_id=0, has_side_effects=True
            ),
        )(shear_offset, remap_shift, frac_index, state)
        return pl.pallas_call(
            unpack,
            out_shape=jax.ShapeDtypeStruct(state.shape, jnp.float32),
            in_specs=[large],
            out_specs=large,
            compiler_params=pltpu.CompilerParams(vmem_limit_bytes=8 * 2**20),
        )(tiles)

    placed = (P(None, None, "gx", "gy"), P(), P("gx"), P("gx"))
    return jax.shard_map(shards, mesh=mesh, in_specs=placed, out_specs=P(None, None, "gx", "gy"), check_vma=False)
```

```python
import functools

import jax
import jax.numpy as jnp
from jax import lax
from jax.experimental import pallas as pl
from jax.experimental.pallas import tpu as pltpu
from jax.sharding import PartitionSpec as P

FRAC = 16
GAMMA_LESS = 5.0 / 3.0 - 1.0
ROTATION = 1.0
SHEAR_RATE = 1.5
MAX_SPEED = 5.0
TIME_STEP = 0.05

FACE_X, FACE_Y, FACE_Z, NEXT_Y = 5, 6, 7, 8
ROWS = 4
LINES = 8 * ROWS
STRIPS = 16
PAGES = 6
MESH = pl.DeviceIdType.MESH


def ahead(value, count):
    lane = lax.broadcasted_iota(jnp.int32, value.shape, 2)
    moved = pltpu.roll(value, 128 - count, 2)
    return jnp.where(lane >= 128 - count, pltpu.roll(moved, 7, 1), moved)


def behind(value, count):
    lane = lax.broadcasted_iota(jnp.int32, value.shape, 2)
    moved = pltpu.roll(value, count, 2)
    return jnp.where(lane < count, pltpu.roll(moved, 1, 1), moved)


def other_plane(value):
    return pltpu.roll(value, 4, 1)


def euler(fields, next_y):
    density, mom_x, mom_y, mom_z, energy, face_x, face_y, face_z = fields
    rows = density.shape[0]
    mid = slice(1, rows - 1)
    cen_x = 0.5 * (face_x[:-1] + face_x[1:])
    cen_y = 0.5 * (face_y + next_y)
    cen_z = 0.5 * (face_z + other_plane(face_z))
    inverse = 1.0 / density
    vel_x = mom_x * inverse
    vel_y = mom_y * inverse
    vel_z = mom_z * inverse
    magnetic = 0.5 * (cen_x * cen_x + cen_y * cen_y + cen_z * cen_z)
    pressure = (
        GAMMA_LESS * (energy - 0.5 * (mom_x * vel_x + mom_y * vel_y + mom_z * vel_z) - magnetic) + magnetic
    )
    vel_dot = vel_x * cen_x + vel_y * cen_y + vel_z * cen_z
    conserved = (density, mom_x, mom_y, mom_z, energy)
    momenta = (mom_x, mom_y, mom_z)
    centred = (cen_x, cen_y, cen_z)
    velocity = (vel_x, vel_y, vel_z)
    change = [None] * 5
    for normal in range(3):
        part = slice(None) if normal == 0 else mid
        speed = velocity[normal][part]
        across = centred[normal][part]
        fluxes = [momenta[normal][part]]
        for second in range(3):
            term = momenta[second][part] * speed - across * centred[second][part]
            if second == normal:
                term = term + pressure[part]
            fluxes.append(term)
        fluxes.append((energy[part] + pressure[part]) * speed - across * vel_dot[part])
        for member in range(5):
            flux = fluxes[member]
            held = conserved[member][part]
            if normal == 0:
                upwind = 0.5 * (flux[:-1] + flux[1:]) - 0.5 * MAX_SPEED * (held[1:] - held[:-1])
                delta = upwind[1:] - upwind[:-1]
            elif normal == 1:
                upwind = 0.5 * (behind(flux, 1) + flux) - 0.5 * MAX_SPEED * (held - behind(held, 1))
                delta = ahead(upwind, 1) - upwind
            else:
                upwind = 0.5 * (other_plane(flux) + flux) - 0.5 * MAX_SPEED * (held - other_plane(held))
                delta = other_plane(upwind) - upwind
            change[member] = -delta if change[member] is None else change[member] - delta
    change[1] = change[1] + 2.0 * ROTATION * mom_y[mid]
    change[2] = change[2] - (2.0 - SHEAR_RATE) * ROTATION * mom_x[mid]
    change[4] = change[4] + SHEAR_RATE * ROTATION * (mom_x[mid] * vel_y[mid] - cen_x[mid] * cen_y[mid])
    elec_x = -(vel_y * cen_z - vel_z * cen_y)
    elec_y = -(vel_z * cen_x - vel_x * cen_z)
    elec_z = -(vel_x * cen_y - vel_y * cen_x)
    pair_x = elec_x[mid] + behind(elec_x[mid], 1)
    edge_x = 0.25 * (pair_x + other_plane(pair_x))
    pair_y = elec_y[1:] + elec_y[:-1]
    edge_y = 0.25 * (pair_y + other_plane(pair_y))
    pair_z = elec_z[1:] + elec_z[:-1]
    edge_z = 0.25 * (pair_z + behind(pair_z, 1))
    delta_x = -(ahead(edge_z, 1) - edge_z - (other_plane(edge_y) - edge_y))
    delta_y = -(other_plane(edge_x) - edge_x - (edge_z[1:] - edge_z[:-1]))
    delta_z = -(edge_y[1:] - edge_y[:-1] - (ahead(edge_x, 1) - edge_x))
    done = [conserved[member][mid] + TIME_STEP * change[member] for member in range(5)]
    done.append(face_x[1:rows] + TIME_STEP * delta_x)
    done.append(face_y[mid] + TIME_STEP * delta_y)
    done.append(face_z[mid] + TIME_STEP * delta_z)
    return done


def window(ref, slot, blocks, cells, amount, kinds):
    hops = lax.div(amount, cells)
    rest = lax.rem(amount, cells)
    if kinds == 3:
        low = rest < 2
        hops = jnp.where(low, hops - 1, hops)
        rest = jnp.where(low, rest + cells, rest)
    total = blocks * 8
    lane = lax.broadcasted_iota(jnp.int32, (blocks, 8, 128), 2)
    chunk = lax.broadcasted_iota(jnp.int32, (blocks, 8, 128), 1) % 4
    place = chunk * 128 + lane - 2 - rest
    result = None
    for kind in reversed(range(kinds)):
        distance = rest - kind * cells + 1024
        lanes = lax.rem(distance, 128)
        sublanes = lax.div(distance, 128) - 8
        back = lax.rem(8 * (hops + kind) + sublanes + total, total)
        near = ref[slot, pl.ds(total - back, total), :].reshape(blocks, 8, 128)
        far = ref[slot, pl.ds(total - back - 1, total), :].reshape(blocks, 8, 128)
        near = pltpu.roll(near, lanes, 2)
        far = pltpu.roll(far, lanes, 2)
        moved = jnp.where(lane >= lanes, near, far)
        if result is None:
            result = moved
        else:
            result = jnp.where(place >= -kind * cells, moved, result)
    return result


def kernel(
    n_gx,
    n_gy,
    cells,
    shear_hbm,
    remap_hbm,
    frac_hbm,
    state_hbm,
    out_ref,
    shear_ref,
    remap_ref,
    frac_ref,
    remap_own,
    frac_own,
    state_ref,
    raw,
    held,
    ext,
    last_face,
    to_left,
    to_right,
    from_left,
    from_right,
    edges,
    next_edges,
    line_ghost,
    line_own,
    line_far,
    line_face,
    near_face,
    pages,
    framed,
    framed_next,
    ghost_next,
    framed_face,
    prior,
    prior_face,
    fresh,
    fresh_edges,
    to_next,
    from_previous,
    line_in,
    line_out,
    lines,
    send_sems,
    recv_sems,
    load_sems,
    known,
):
    gx = lax.axis_index("gx")
    gy = lax.axis_index("gy")
    half = n_gy // 2
    per = LINES // n_gy
    left_y = lax.rem(gy + n_gy - 1, n_gy)
    right_y = lax.rem(gy + 1, n_gy)
    inside = lax.rem(gy, half)
    side = gy - inside
    core = gy + 1 - 2 * lax.rem(gy, 2)
    up, down, up_2, down_2 = (side + lax.rem(inside + half + step, half) for step in (2, -2, 4, -4))
    partner = lax.rem(gx + n_gx // 2, n_gx)
    middle = n_gx // 2
    last = n_gx - 1
    first_x = gx == 0
    last_x = gx == last
    barrier = pltpu.get_barrier_semaphore()
    load = pltpu.make_async_copy(state_hbm, state_ref, load_sems.at[0])
    load.start()
    small_loads = [
        pltpu.make_async_copy(source, target, load_sems.at[1 + k])
        for k, (source, target) in enumerate(
            ((shear_hbm, shear_ref), (remap_hbm, remap_own), (frac_hbm, frac_own))
        )
    ]
    for copy in small_loads:
        copy.start()

    def tell(sem, x, y):
        pl.semaphore_signal(sem, inc=1, device_id=(x, y), device_id_type=MESH)

    def everyone(body):
        def step(k, carry):
            body(lax.rem(k + gy, n_gy))
            return carry

        lax.fori_loop(0, n_gy, step, 0)

    def send(source, target, sent, arrived, x, y):
        return pltpu.make_async_remote_copy(
            src_ref=source,
            dst_ref=target,
            send_sem=send_sems.at[sent],
            recv_sem=recv_sems.at[arrived],
            device_id=(x, y),
            device_id_type=MESH,
        )

    def wait_bytes(ref, sem):
        pltpu.make_async_copy(ref, ref, sem).wait()

    @pl.when(first_x)
    def _():
        def step(k, carry):
            tell(barrier, 0, lax.rem(gy + k, n_gy))
            return carry

        lax.fori_loop(1, n_gy, step, 0)

    @pl.when(gx == middle)
    def _():
        everyone(lambda y: tell(barrier, 0, y))

    @pl.when(jnp.logical_not(first_x))
    def _():
        for y in (left_y, right_y, up, down):
            tell(barrier, gx, y)

    @pl.when(gx != middle)
    def _():
        for y in (gy, lax.rem(gy + half, n_gy)):
            tell(barrier, partner, y)

    @pl.when(jnp.logical_not(first_x))
    def _():
        tell(barrier, gx - 1, gy)

    @pl.when(jnp.logical_not(last_x))
    def _():
        tell(barrier, gx + 1, gy)

    @pl.when(first_x)
    def _():
        everyone(lambda y: tell(barrier, last, y))

    load.wait()
    whole = cells // 128
    for field in range(8):
        for plane in range(2):
            for chunk in range(4):
                if chunk < whole:
                    part = state_ref[field, plane, :, pl.ds(128 * chunk, 128)]
                else:
                    part = state_ref[field, plane, :, pl.ds(128 * whole, cells - 128 * whole)]
                    part = jnp.concatenate([part, jnp.zeros((ROWS, 128 * (whole + 1) - cells), jnp.float32)], axis=1)
                raw[pl.ds(field * 32 + plane * 4 + chunk, ROWS, stride=8), :] = part
    to_left[...] = raw[pl.ds(0, 64, stride=4), :]
    to_right[...] = raw[pl.ds(3, 64, stride=4), :]
    held[...] = behind(raw[...].reshape(LINES, 8, 128), 2)
    pl.semaphore_wait(barrier, jnp.where(last_x, 7 + n_gy, jnp.where(first_x, 2 * n_gy, 8)))

    @pl.when(jnp.logical_not(first_x))
    def _():
        for y in (core, up, down):
            tell(known.at[0], gx, y)


    def line_place(buffer, t):
        return buffer.at[lax.rem(t, per), pl.ds(pl.multiple_of(8 * gy, 8), 8), :]

    @pl.when(last_x)
    def _():
        def step(k, carry):
            u = lax.rem(k + lax.div(gy, 2), STRIPS)
            t = lax.div(u, 2) * ROWS + 2 + lax.rem(u, 2)
            send(held.at[t], line_place(line_far, t), 2, 16 + lax.rem(t, per), 0, lax.div(t, per)).start()
            return carry

        lax.fori_loop(0, STRIPS, step, 0)
        everyone(lambda y: tell(known.at[3], 0, y))

    near_copy = send(held.at[FACE_X * ROWS], near_face, 12, 8, 0, gy)
    strip_left = send(to_left, from_right, 0, 0, gx, left_y)
    strip_right = send(to_right, from_left, 1, 1, gx, right_y)
    strip_left.start()
    strip_right.start()

    @pl.when(gx == 1)
    def _():
        near_copy.start()

    amounts = send(remap_hbm, remap_ref, 10, 9, partner, gy)
    levels = send(frac_hbm, frac_ref, 11, 10, partner, gy)
    amounts.start()
    levels.start()
    @pl.when(jnp.logical_not(first_x))
    def _():
        pl.semaphore_wait(known.at[0], 3)
        if half > 4:
            for y in (up_2, down_2):
                tell(known.at[1], gx, y)
            pl.semaphore_wait(known.at[1], 2)

    for y in (gy, core):
        tell(known.at[2], partner, y)
        tell(known.at[2], partner, lax.rem(y + half, n_gy))

    @pl.when(first_x)
    def _():
        def ghosts(k, carry):
            u = lax.rem(k + lax.div(gy, 2), STRIPS + 1)
            rank = lax.rem(u, n_gy)
            slot = lax.div(u, n_gy)
            owner = jnp.where(rank < half, 2 * rank, 2 * (rank - half) + 1)
            tile = jnp.where(u == STRIPS, FACE_X * ROWS + 2, lax.div(u, 2) * ROWS + lax.rem(u, 2))
            target = line_ghost.at[slot, pl.ds(pl.multiple_of(8 * gy, 8), 8), :]
            arrived = 16 + per + slot

            @pl.when(owner != gy)
            def _():
                send(held.at[tile], target, 14, arrived, 0, owner).start()

            @pl.when(owner == gy)
            def _():
                pltpu.make_async_copy(held.at[tile], target, recv_sems.at[arrived]).start()

            return carry

        def whole(k, carry):
            t = lax.rem(k + (gy + half) * per, LINES)
            owner = lax.div(t, per)
            stays = lax.rem(t, ROWS) < 2

            @pl.when(jnp.logical_not(stays & (owner == gy)))
            def _():
                send(held.at[t], line_place(line_own, t), 2, 2, jnp.where(stays, 0, middle), owner).start()

            @pl.when(stays & (owner == gy))
            def _():
                pltpu.make_async_copy(held.at[t], line_place(line_own, t), recv_sems.at[2]).start()

            return carry

        lax.fori_loop(0, STRIPS + 1, ghosts, 0)
        lax.fori_loop(0, LINES, whole, 0)
        near_copy.wait_recv()
        send(near_face, line_place(line_face, 0), 13, 16 + 2 * per, middle, n_gy - 1).start()

    strip_left.wait_recv()
    strip_right.wait_recv()
    lane = lax.broadcasted_iota(jnp.int32, (LINES, 8, 128), 2)
    chunk = lax.broadcasted_iota(jnp.int32, (LINES, 8, 128), 1) % 4
    beyond = cells % 128
    after = from_right[...]
    edges[pl.ds(0, 64, stride=4), :] = pltpu.roll(from_left[...], 130 - beyond, 1)
    edges[pl.ds(3, 64, stride=4), :] = pltpu.roll(after, beyond + 2, 1)
    outside = jnp.logical_or(
        jnp.logical_and(chunk == 0, lane < 2), jnp.logical_and(chunk == 3, lane >= beyond + 2)
    )
    full = jnp.where(outside, edges[...].reshape(LINES, 8, 128), held[...])
    for field in range(8):
        ext[field, 2:6] = full[ROWS * field : ROWS * field + ROWS]
    next_edges[pl.ds(3, 2 * ROWS, stride=4), :] = pltpu.roll(after[2 * ROWS * FACE_Y : 2 * ROWS * (FACE_Y + 1)], beyond + 1, 1)
    final = jnp.logical_and(chunk == 3, lane == 127)[:ROWS]
    ext[NEXT_Y, 2:6] = jnp.where(
        final, next_edges[...].reshape(ROWS, 8, 128), ahead(full[ROWS * FACE_Y : ROWS * (FACE_Y + 1)], 1)
    )

    to_up = send(ext.at[:, pl.ds(4, 2)], ext.at[:, pl.ds(0, 2)], 3, 3, gx + 1, gy)
    to_down = send(ext.at[:, pl.ds(2, 2)], ext.at[:, pl.ds(6, 2)], 4, 4, gx - 1, gy)
    to_down_face = send(ext.at[FACE_X, 4], last_face, 5, 5, gx - 1, gy)

    @pl.when(jnp.logical_not(last_x))
    def _():
        to_up.start()

    @pl.when(jnp.logical_not(first_x))
    def _():
        to_down.start()
        to_down_face.start()

    for copy in small_loads:
        copy.wait()

    total_cells = cells * n_gy
    spare = n_gy - 1

    def fill(page, buffer, slot, amount):
        pages[page] = window(buffer, slot, n_gy, cells, amount, 3)

    def deliver(source, target, sem, arrived, x, y):
        if x == 0:
            here = first_x & (y == gy)

            @pl.when(jnp.logical_not(here))
            def _():
                send(source, target, sem, arrived, 0, y).start()

            @pl.when(here)
            def _():
                pltpu.make_async_copy(source, target, recv_sems.at[arrived]).start()

        else:
            send(source, target, sem, arrived, x, y).start()

    def hand(page, target, sem, arrived, x):
        everyone(lambda y: deliver(pages.at[page, y], target, sem, arrived, x, y))

    def hand_prior(page, target, r):
        for y in (0, half):
            for plane in range(2):
                part = pl.ds(4 * plane + 3, 1)
                source = pages.at[page, (y - 1) % n_gy, part]
                deliver(source, target.at[part], 9, 20 + 2 * per + r, 0, y)

    def hand_next(page, target, sem, arrived, x):
        def one(y):
            following = lax.rem(y + 1, n_gy)
            for plane in range(2):
                source = pages.at[page, following, pl.ds(4 * plane, 1)]
                deliver(source, target(plane), sem, arrived, x, y)

        everyone(one)

    def next_faces(faces, rows):
        shape = faces.shape
        lanes = lax.broadcasted_iota(jnp.int32, shape, 2)
        places = lax.broadcasted_iota(jnp.int32, shape, 1)
        follow = pltpu.roll(jnp.broadcast_to(rows[:, 0:1, :], (2 * shape[0], 8, 128)), 123, 2)
        follow = follow.reshape(shape[0], 2, 8, 128)
        chosen = jnp.where(places < 4, follow[:, 0], follow[:, 1])
        return jnp.where((places % 4 == 3) & (lanes == 127), chosen, ahead(faces, 1))

    def wait_left():
        wait_bytes(ext.at[:, pl.ds(0, 2)], recv_sems.at[3])

    def wait_right():
        wait_bytes(ext.at[:, pl.ds(6, 2)], recv_sems.at[4])
        wait_bytes(last_face, recv_sems.at[5])

    places = []
    for slot in range(per):
        t = gy * per + slot
        places.append((slot, lax.div(t, ROWS), lax.rem(t, ROWS)))

    def own_conditions(r, field, row):
        inner = (row < 3 + r) & ((row < 2) == first_x)
        edge = (row == 3) & (field == FACE_X) & (r == 0) & (gx == middle)
        return inner, jnp.logical_and(inner, field == FACE_Y), edge

    def far_conditions(r, field, row):
        inner = row >= 2 + r
        return inner, jnp.logical_and(inner, field == FACE_Y)

    def own_lines(amounts_ref):
        for slot, field, row in places:

            @pl.when((row < 2) == first_x)
            def _(slot=slot):
                wait_bytes(line_own.at[slot, pl.ds(0, 8 * n_gy), :], recv_sems.at[2])

        line_own[:, pl.ds(8 * n_gy, 8 * n_gy), :] = line_own[:, pl.ds(0, 8 * n_gy), :]
        for slot, field, row in places:

            def frame(r, carry, slot=slot, field=field, row=row):
                inner, faces, edge = own_conditions(r, field, row)
                page = r * per + slot

                @pl.when(jnp.logical_or(inner, edge))
                def _():
                    fill(page, line_own, slot, amounts_ref[r])

                @pl.when(inner)
                def _():
                    hand(page, framed.at[r, field, row + 2 - r], 9, 11 + r, 0)
                    hand_prior(page, prior.at[r, field, row + 2 - r], r)

                @pl.when(edge)
                def _():
                    hand(page, framed_face.at[0], 9, 13, 0)
                    hand_prior(page, prior_face.at[0], 0)

                @pl.when(faces)
                def _():
                    start = 2 * (row + 2 - r)
                    hand_next(page, lambda plane: framed_next.at[r, start + plane, pl.ds(0, 1)], 15, 18 + 2 * per + r, 0)

                return carry

            lax.fori_loop(0, 2, frame, 0)

    mine = jnp.where(lax.rem(gy, 2) == 0, lax.div(gy, 2), half + lax.div(gy, 2))
    ghost_places = []
    for slot in range(-(-(STRIPS + 1) // n_gy)):
        u = slot * n_gy + mine
        ghost_places.append((slot, u, lax.div(u, 2) == FACE_Y))

    @pl.when(first_x)
    def _():
        wait_right()
        ext[:, 0:2] = ext[:, 2:4]

    @pl.when(jnp.logical_not(first_x))
    def _():
        wait_left()

    @pl.when(jnp.logical_not(jnp.logical_or(first_x, last_x)))
    def _():
        wait_right()

    @pl.when(last_x)
    def _():
        wait_bytes(ext.at[pl.ds(0, 8), pl.ds(6, 2)], recv_sems.at[4])
        wait_bytes(last_face, recv_sems.at[5])
        wait_bytes(ghost_next.at[:, pl.ds(0, 1)], recv_sems.at[17 + 2 * per])
        ext[NEXT_Y, 6:8] = next_faces(ext[FACE_Y, 6:8], ghost_next[...])

    fields = [ext[field] for field in range(8)]
    fields[FACE_X] = jnp.concatenate([fields[FACE_X], last_face[...][None]], axis=0)
    once = euler(fields, ext[NEXT_Y])
    twice = euler(once, ahead(once[FACE_Y], 1))
    for field in range(8):
        lines[ROWS * field : ROWS * field + ROWS] = 0.5 * (ext[field, 2:6] + twice[field][:ROWS])

    def spread(k, carry):
        t = lax.rem(k + (gy + half) * per, LINES)
        slot = lax.rem(t, per)
        target = line_in.at[slot, pl.ds(pl.multiple_of(8 * gy, 8), 8), :]

        @pl.when(jnp.logical_not(first_x) | (lax.rem(t, ROWS) >= 2))
        def _():
            send(lines.at[t], target, 6, 6, partner, lax.div(t, per)).start()

        return carry

    @pl.when(jnp.logical_not(first_x))
    def _():
        pl.semaphore_wait(known.at[2], 4)

    lax.fori_loop(0, LINES, spread, 0)

    @pl.when(first_x)
    def _():
        pl.semaphore_wait(known.at[2], 4)

    @pl.when(first_x)
    def _():
        ghost_amount = lax.rem(total_cells - shear_ref[0], total_cells)
        for slot, u, faces in ghost_places:

            @pl.when(u <= STRIPS)
            def _(slot=slot):
                wait_bytes(line_ghost.at[slot, pl.ds(0, 8 * n_gy), :], recv_sems.at[16 + per + slot])
                line_ghost[slot, pl.ds(8 * n_gy, 8 * n_gy), :] = line_ghost[slot, pl.ds(0, 8 * n_gy), :]
                fill(4 * per + slot, line_ghost, slot, ghost_amount)

        pl.semaphore_wait(known.at[3], n_gy)
        for slot, u, faces in ghost_places:

            @pl.when(u < STRIPS)
            def _(slot=slot, u=u):
                hand(4 * per + slot, ext.at[lax.div(u, 2), 6 + lax.rem(u, 2)], 8, 4, last)

            @pl.when(faces)
            def _(slot=slot, u=u):
                row = lax.rem(u, 2)
                hand_next(4 * per + slot, lambda plane: ghost_next.at[2 * row + plane, pl.ds(0, 1)], 15, 17 + 2 * per, last)

            @pl.when(u == STRIPS)
            def _(slot=slot):
                hand(4 * per + slot, last_face, 8, 5, last)


        for slot, field, row in places:

            @pl.when(row >= 2)
            def _(slot=slot, field=field, row=row):
                wait_bytes(line_far.at[slot, pl.ds(0, 8 * n_gy), :], recv_sems.at[16 + slot])
                line_far[slot, pl.ds(8 * n_gy, 8 * n_gy), :] = line_far[slot, pl.ds(0, 8 * n_gy), :]

                def frame(r, carry):
                    inner, faces = far_conditions(r, field, row)
                    page = (2 + r) * per + slot
                    amount = lax.rem(remap_own[r] + shear_ref[0], total_cells)

                    @pl.when(inner)
                    def _():
                        fill(page, line_far, slot, amount)
                        hand(page, framed.at[r, field, row - 2 - r], 9, 11 + r, 0)
                        hand_prior(page, prior.at[r, field, row - 2 - r], r)

                    @pl.when(faces)
                    def _():
                        start = 2 * (row - 2 - r)
                        hand_next(page, lambda plane: framed_next.at[r, start + plane, pl.ds(0, 1)], 15, 18 + 2 * per + r, 0)

                    return carry

                lax.fori_loop(0, 2, frame, 0)

        own_lines(remap_own)

    amounts.wait_recv()
    levels.wait_recv()

    @pl.when(gx == middle)
    def _():
        own_lines(remap_ref)

        @pl.when(gy == spare)
        def _():
            wait_bytes(line_face.at[0, pl.ds(0, 8 * n_gy), :], recv_sems.at[16 + 2 * per])
            line_face[0, pl.ds(8 * n_gy, 8 * n_gy), :] = line_face[0, pl.ds(0, 8 * n_gy), :]
            fill(5 * per, line_face, 0, remap_ref[1])
            hand(5 * per, framed_face.at[1], 9, 14, 0)
            hand_prior(5 * per, prior_face.at[1], 1)

    expected = [jnp.logical_or(gx != middle, row >= 2) for _, _, row in places]
    for slot in range(per):

        @pl.when(expected[slot])
        def _(slot=slot):
            wait_bytes(line_in.at[slot, pl.ds(0, 8 * n_gy), :], recv_sems.at[6])

    for slot in range(per):

        @pl.when(expected[slot])
        def _(slot=slot):
            row = lax.rem(gy * per + slot, ROWS)
            line_in[slot, pl.ds(8 * n_gy, 8 * n_gy), :] = line_in[slot, pl.ds(0, 8 * n_gy), :]
            tiles = window(line_in, slot, n_gy, cells, remap_ref[row], 2)
            weight = (frac_ref[row].astype(jnp.float32) + 0.5) / FRAC
            line_out[slot] = (1.0 - weight) * ahead(tiles, 2) + weight * ahead(tiles, 1)
            target = raw.at[pl.ds(pl.multiple_of(8 * (gy * per + slot), 8), 8), :]
            everyone(lambda y: send(line_out.at[slot, y], target, 7, 7, partner, y).start())

    next_copy = send(to_next, from_previous, 12, 15, 0, right_y)
    far_left = (gy == 0) | (gy == half)
    sends_next = (gy != half - 1) & (gy != n_gy - 1)
    prior_bytes = line_in.at[0, pl.ds(0, 82), :]

    @pl.when(first_x)
    def _():
        def advance(fields, last, following):
            fields = fields[:FACE_X] + [jnp.concatenate([fields[FACE_X], last[None]], axis=0)] + fields[FACE_Y:]
            once = euler(fields, following)
            twice = euler(once, ahead(once[FACE_Y], 1))
            return [0.5 * (fields[field][2] + twice[field][0]) for field in range(8)]

        for r in range(2):
            wait_bytes(framed.at[r], recv_sems.at[11 + r])
            wait_bytes(framed_face.at[r], recv_sems.at[13 + r])
            wait_bytes(framed_next.at[r, :, pl.ds(0, 1)], recv_sems.at[18 + 2 * per + r])
            fields = [framed[r, field] for field in range(8)]
            done = advance(fields, framed_face[r], next_faces(fields[FACE_Y], framed_next[r]))
            for field in range(8):
                fresh[pl.ds(64 * r + 8 * field, 8), :] = done[field]

        @pl.when(sends_next)
        def _():
            to_next[...] = fresh[pl.ds(3, 32, stride=4), :]
            next_copy.start()

        @pl.when(far_left)
        def _():
            for r in range(2):
                wait_bytes(prior_bytes, recv_sems.at[20 + 2 * per + r])
                fields = [prior[r, field] for field in range(8)]
                lanes = lax.broadcasted_iota(jnp.int32, fields[0].shape, 2)
                chunks = lax.broadcasted_iota(jnp.int32, fields[0].shape, 1) % 4
                follow = pltpu.roll(pltpu.roll(framed[r, FACE_Y], 123, 2), 3, 1)
                following = jnp.where((chunks == 3) & (lanes == 127), follow, ahead(fields[FACE_Y], 1))
                done = advance(fields, prior_face[r], following)
                for field in range(8):
                    fresh_edges[pl.ds(64 * r + 8 * field, 8), :] = done[field]
            from_previous[...] = fresh_edges[pl.ds(3, 32, stride=4), :]

        @pl.when(jnp.logical_not(far_left))
        def _():
            next_copy.wait_recv()

        reach = cells % 128 + 1
        fresh_edges[pl.ds(0, 32, stride=4), :] = pltpu.roll(from_previous[...], 129 - reach, 1)

    @pl.when(jnp.logical_not(first_x))
    def _():
        wait_bytes(raw, recv_sems.at[7])

    @pl.when(first_x)
    def _():
        wait_bytes(raw.at[pl.ds(0, 4 * LINES)], recv_sems.at[7])
        tiles = fresh[...].reshape(16, 8, 128)
        lanes = lax.broadcasted_iota(jnp.int32, tiles.shape, 2)
        chunks = lax.broadcasted_iota(jnp.int32, tiles.shape, 1) % 4
        tiles = jnp.where((chunks == 0) & (lanes == 1), fresh_edges[...].reshape(16, 8, 128), tiles)
        here, there = ahead(tiles, 2), ahead(tiles, 1)
        for r in range(2):
            weight = (frac_own[r].astype(jnp.float32) + 0.5) / FRAC
            mixed = (1.0 - weight) * here[8 * r : 8 * r + 8] + weight * there[8 * r : 8 * r + 8]
            for field in range(8):
                raw[pl.ds(32 * field + 8 * r, 8), :] = mixed[field]

    out_ref[...] = raw[...]

    for copy in (strip_left, strip_right, amounts, levels):
        copy.wait_send()

    @pl.when(gx == 1)
    def _():
        near_copy.wait_send()

    @pl.when(jnp.logical_not(last_x))
    def _():
        to_up.wait_send()

    @pl.when(jnp.logical_not(first_x))
    def _():
        to_down.wait_send()
        to_down_face.wait_send()

    @pl.when(last_x)
    def _():
        wait_bytes(held.at[pl.ds(0, STRIPS)], send_sems.at[2])

    def left(condition, page, sem):
        @pl.when(condition)
        def _():
            wait_bytes(pages.at[page], send_sems.at[sem])

    def left_prior(near):
        for condition, rows in ((near, 2), (jnp.logical_not(near), 4)):

            @pl.when(condition)
            def _(rows=rows):
                wait_bytes(line_in.at[0, pl.ds(0, rows), :], send_sems.at[9])

    def left_next(condition, one_less=0):
        @pl.when(condition)
        def _():
            wait_bytes(pages.at[pl.ds(0, 2), pl.ds(0, n_gy - one_less), pl.ds(0, 1)], send_sems.at[15])

    @pl.when(first_x)
    def _():
        stayed = sum((row < 2).astype(jnp.int32) for _, _, row in places)
        for count in range(per + 1):

            @pl.when(stayed == count)
            def _(count=count):
                wait_bytes(held.at[pl.ds(0, LINES - count)], send_sems.at[2])

        wait_bytes(near_face, send_sems.at[13])

        @pl.when(sends_next)
        def _():
            next_copy.wait_send()

        count_own = sum((u <= STRIPS).astype(jnp.int32) for _, u, _ in ghost_places)
        for count in range(len(ghost_places) + 1):

            @pl.when(count_own == count)
            def _(count=count):
                wait_bytes(held.at[pl.ds(0, STRIPS + 1 - count)], send_sems.at[14])

        for slot, u, faces in ghost_places:
            left(u <= STRIPS, 4 * per + slot, 8)
            left_next(faces)

        for slot, field, row in places:
            for r in range(2):
                inner, faces = far_conditions(r, field, row)
                left_next(faces, 1)

                @pl.when(inner)
                def _(slot=slot, r=r):
                    wait_bytes(pages.at[(2 + r) * per + slot, pl.ds(0, n_gy - 1)], send_sems.at[9])
                    left_prior(far_left)

                inner, faces, _ = own_conditions(r, field, row)
                left_next(faces, 1)

                @pl.when(inner)
                def _(slot=slot, r=r):
                    wait_bytes(pages.at[r * per + slot, pl.ds(0, n_gy - 1)], send_sems.at[9])
                    left_prior(far_left)


    @pl.when(gx == middle)
    def _():
        @pl.when(gy == spare)
        def _():
            wait_bytes(pages.at[5 * per], send_sems.at[9])
            left_prior(first_x)

        for slot, field, row in places:
            for r in range(2):
                inner, faces, edge = own_conditions(r, field, row)
                left(jnp.logical_or(inner, edge), r * per + slot, 9)
                left_next(faces)

                @pl.when(jnp.logical_or(inner, edge))
                def _():
                    left_prior(first_x)


    @pl.when(first_x)
    def _():
        wait_bytes(lines.at[pl.ds(0, LINES // 2)], send_sems.at[6])

    @pl.when(jnp.logical_not(first_x))
    def _():
        wait_bytes(lines, send_sems.at[6])

    for slot in range(per):

        @pl.when(expected[slot])
        def _(slot=slot):
            wait_bytes(line_out.at[slot], send_sems.at[7])


def unpack(tiles_ref, out_ref):
    cells = out_ref.shape[3]
    for field in range(8):
        for plane in range(2):
            for chunk in range(4):
                part = tiles_ref[pl.ds(field * 32 + plane * 4 + chunk, ROWS, stride=8), :]
                width = min(128, cells - 128 * chunk)
                out_ref[field, plane, :, pl.ds(128 * chunk, width)] = part[:, :width]


def solution(mesh):
    n_gx = mesh.shape["gx"]
    n_gy = mesh.shape["gy"]

    def shards(state, shear_offset, remap_shift, frac_index):
        cells = state.shape[3]
        per = LINES // n_gy
        vmem = lambda *shape: pltpu.VMEM(shape, jnp.float32)
        large = pl.BlockSpec(memory_space=pltpu.VMEM)
        whole = pl.BlockSpec(memory_space=pltpu.HBM)
        tiles = pl.pallas_call(
            functools.partial(kernel, n_gx, n_gy, cells),
            out_shape=pltpu.VMEM((8 * LINES, 128), jnp.float32),
            in_specs=[whole] * 4,
            out_specs=large,
            scratch_shapes=[
                pltpu.SMEM((1,), jnp.int32),
                pltpu.SMEM((ROWS,), jnp.int32),
                pltpu.SMEM((ROWS,), jnp.int32),
                pltpu.SMEM((ROWS,), jnp.int32),
                pltpu.SMEM((ROWS,), jnp.int32),
                vmem(*state.shape),
                vmem(8 * LINES, 128),
                vmem(LINES, 8, 128),
                vmem(9, 8, 8, 128),
                vmem(8, 128),
                vmem(64, 128),
                vmem(64, 128),
                vmem(64, 128),
                vmem(64, 128),
                vmem(8 * LINES, 128),
                vmem(8 * ROWS, 128),
                vmem(per, 16 * n_gy, 128),
                vmem(per, 16 * n_gy, 128),
                vmem(per, 16 * n_gy, 128),
                vmem(1, 16 * n_gy, 128),
                vmem(8, 128),
                vmem(PAGES * per, n_gy, 8, 128),
                vmem(2, 8, 5, 8, 128),
                vmem(2, 10, 8, 128),
                vmem(4, 8, 128),
                vmem(2, 8, 128),
                vmem(2, 8, 5, 8, 128),
                vmem(2, 8, 128),
                vmem(128, 128),
                vmem(128, 128),
                vmem(32, 128),
                vmem(32, 128),
                vmem(per, 16 * n_gy, 128),
                vmem(per, n_gy, 8, 128),
                vmem(LINES, 8, 128),
                pltpu.SemaphoreType.DMA((16,)),
                pltpu.SemaphoreType.DMA((22 + 2 * per,)),
                pltpu.SemaphoreType.DMA((4,)),
                pltpu.SemaphoreType.REGULAR((4,)),
            ],
            compiler_params=pltpu.CompilerParams(
                collective_id=0, has_side_effects=True
            ),
        )(shear_offset, remap_shift, frac_index, state)
        return pl.pallas_call(
            unpack,
            out_shape=jax.ShapeDtypeStruct(state.shape, jnp.float32),
            in_specs=[large],
            out_specs=large,
            compiler_params=pltpu.CompilerParams(vmem_limit_bytes=8 * 2**20),
        )(tiles)

    placed = (P(None, None, "gx", "gy"), P(), P("gx"), P("gx"))
    return jax.shard_map(shards, mesh=mesh, in_specs=placed, out_specs=P(None, None, "gx", "gy"), check_vma=False)
```
